128 devices in a mesh: dp: 32 (over y_lo, z, x), head: 4 (over y_hi, core).
Axes of the slice: x: 4, y: 4 (y_hi: 2, y_lo: 2; y = y_hi * 2 + y_lo), z: 4, core: 2. Of those that a mesh axis runs over, the one named last changes fastest.
Arguments:
- inputs: bfloat16 [128, 512, 768], P('dp'), may hold values from -6 to 6
- memory: bfloat16 [128, 512, 768], P('dp', 'head'), may hold values from -6 to 6
- doc_ids: int32 [128, 512], P('dp'), may hold values from 0 to 3, never falling along the last dimension, each value on 1 to 256 neighbouring positions
- key_valid: int32 [128, 512], P('dp'), may hold values 0 or 1
- sticky_bins: int32 [128, 256], P('dp'), may hold values from 0 to 255
- ln_gain: float32 [2, 768], replicated, may hold values from 0.25 to 1.75
- ln_shift: float32 [2, 768], replicated, may hold values from -2 to 2
- w_qkv: bfloat16 [3, 768, 768], P(None, None, 'head'), may hold values from -0.21875 to 0.21875
- b_qv: float32 [2, 768], P(None, 'head'), may hold values from -2 to 2
- w_gauss: float32 [2, 12, 256], P(None, 'head'), may hold values from -0.125 to 0.125
- w_out: bfloat16 [768, 768], P('head'), may hold values from -1.25 to 1.25
- b_out: float32 [768], replicated, may hold values from -2 to 2
- w_fc: bfloat16 [768, 3072], P(None, 'head'), may hold values from -0.21875 to 0.21875
- b_fc: float32 [3072], P('head'), may hold values from -2 to 2
- w_proj: bfloat16 [3072, 768], P('head'), may hold values from -0.109375 to 0.109375
- b_proj: float32 [768], replicated, may hold values from -2 to 2
- cotangent: bfloat16 [128, 512, 768], P('dp'), may hold values from -6 to 6
Outputs:
- mixed: bfloat16 [128, 512, 768], P('dp')
- grad_input: float32 [128, 512, 768], P('dp')
- grad_ln_gain: float32 [2, 768], replicated
- grad_ln_shift: float32 [2, 768], replicated
- grad_w_qkv: float32 [3, 768, 768], P(None, None, 'head')
- grad_b_qv: float32 [2, 768], P(None, 'head')
- grad_w_gauss: float32 [2, 12, 256], P(None, 'head')
- grad_w_out: float32 [768, 768], P('head')
- grad_b_out: float32 [768], replicated
- grad_w_fc: float32 [768, 3072], P(None, 'head')
- grad_b_fc: float32 [3072], P('head')
- grad_w_proj: float32 [3072, 768], P('head')
- grad_b_proj: float32 [768], replicated
The draws below stay inside these ranges and needn't reach their ends.
Inputs may be any that keep to these rules, and one draw needn't show every extreme that they name: `doc_ids`: within a segment the ids never fall; all 4 documents appear, each of 1 to 256 tokens, one exactly that long.
All inputs are finite; a program needn't handle non-finite values. No bound on the sum of `key_valid` on one device may be relied on, other than what follows from the above.
Results may differ from the reference program's by a relative error of at most 0.012.
The reference program's roundings to bfloat16 on the way count: a program that leaves them out, or rounds other values in their place, can miss the bound.
Values may be sent and summed in bfloat16 or wider, within the bound.
A program may use at most 192 MiB of HBM per device.

```python
import math
from functools import partial
import jax
import jax.numpy as jnp
import numpy as np
from jax import lax

D = 768
HEADS = 12
FF = 3072
N = 256
MEM = 512
HALF = 256
NBINS = 256
SEG = 512
DOCS = 4
SEGS = 128


def with_ends(values, own_key, least, high):
    spot = [jax.random.randint(jax.random.fold_in(own_key, axis), (), 0, length) for axis, length in enumerate(values.shape)]
    main_axis = values.shape.index(max(values.shape))
    next_to = spot[:main_axis] + [(spot[main_axis] + 1) % values.shape[main_axis]] + spot[main_axis + 1:]
    return values.at[tuple(spot)].set(least).at[tuple(next_to)].set(high)


def shard_levels(own_key, shape, cuts, low, top_value):
    gain, own = 1.0, jax.random.fold_in(own_key, 6)
    for dim, blocks in cuts:
        heights = jnp.exp(jax.random.uniform(jax.random.fold_in(own, dim), (blocks,), jnp.float32, low / len(cuts), top_value / len(cuts)))
        gain = gain * jnp.repeat(heights, shape[dim] // blocks).reshape([-1 if axis == dim else 1 for axis in range(len(shape))])
    return gain


def rank_bounds(count, skew):
    portions = [(1 << 20) // math.isqrt(grade ** skew) + 1 for grade in range(1, count + 1)]
    deviation = 1 + sum(portions) // (1 << 30)
    return np.cumsum(np.array([max(1, weight // deviation) for weight in portions]))


def skewed_ids(key, extent, count, slope):
    listing = rank_bounds(count, slope)
    lot = jax.random.randint(jax.random.fold_in(key, 1), extent, 0, int(listing[count - 1]))
    standing = jnp.searchsorted(jnp.asarray(listing, jnp.int32), lot, side="right")
    return jax.random.permutation(jax.random.fold_in(key, 2), count)[standing].astype(jnp.int32)


def split_up(number_of, total, reach, slope):
    loads = [(1 << 20) // math.isqrt(standing ** slope) + 1 for standing in range(2, number_of + 1)]
    surplus, given = total - reach - (number_of - 1), [1] * (number_of - 1)
    while surplus > 0:
        free = [i for i in range(number_of - 1) if given[i] < reach]
        mass, budget = sum([loads[i] for i in free]), surplus
        for i in free:
            extra = min(reach - given[i], max(1, budget * loads[i] // mass), surplus)
            given[i] = given[i] + extra
            surplus = surplus - extra
    return np.array([reach] + given)


def uneven_parts(key, count, total, most, lean):
    if count == 2:
        one = jax.random.randint(key, (), max(1, total - most), min(most, total - 1) + 1)
        return jnp.stack([one, total - one])
    lengths = jnp.asarray(split_up(count, total, most, lean), jnp.int32)
    pairs = (count - 1) // 2
    source_of, taker = lengths[1:1 + 2 * pairs:2], lengths[2:2 + 2 * pairs:2]
    margin = jnp.minimum(source_of - 1, most - taker)
    shifted = jax.random.randint(jax.random.fold_in(key, 1), (pairs,), 0, 1 << 20) % (margin + 1)
    lengths = lengths.at[1:1 + 2 * pairs:2].set(source_of - shifted).at[2:2 + 2 * pairs:2].set(taker + shifted)
    return lengths[jax.random.permutation(jax.random.fold_in(key, 2), count)]


def bell_draw(own_key, shape, width, limit, shards=(), kind=jnp.bfloat16):
    drawn = jax.random.normal(own_key, shape, jnp.float32) * width
    if len(shards) > 0:
        drawn = shard_levels(own_key, shape, shards, -0.22, 0.18) * drawn
    return jnp.clip(drawn, min=-limit, max=limit).astype(kind)


def setup_inputs(seed: int = 0) -> dict:
    seeds = jax.random.split(jax.random.key(seed), 18)
    return {
        "inputs": bell_draw(seeds[0], (SEGS, SEG, D), 1.0, 6.0, ((0, 32),)),
        "memory": bell_draw(seeds[1], (SEGS, MEM, D), 1.0, 6.0, ((0, 32), (1, 4))),
        "doc_ids": jax.vmap(lambda own: jnp.searchsorted(jnp.cumsum(uneven_parts(own, DOCS, SEG, SEG // 2, 0)), jnp.arange(SEG), side="right"))(jax.random.split(seeds[2], SEGS)).reshape((SEGS, SEG)).astype(jnp.int32),
        "key_valid": with_ends((jax.random.randint(seeds[3], (SEGS, SEG), 0, 8) < 7).astype(jnp.int32), jax.random.fold_in(seeds[3], 1), 0, 1),
        "sticky_bins": with_ends(skewed_ids(seeds[4], (SEGS, HALF), NBINS, 2), jax.random.fold_in(seeds[4], 3), 0, NBINS - 1).astype(jnp.int32),
        "ln_gain": jnp.clip(1.0 + 0.15 * jax.random.normal(seeds[5], (2, D), jnp.float32), 0.25, 1.75),
        "ln_shift": bell_draw(seeds[6], (2, D), 0.3, 2.0, (), jnp.float32),
        "w_qkv": bell_draw(seeds[7], (3, D, D), D ** -0.5, 0.21875, ((2, 4),)),
        "b_qv": bell_draw(seeds[8], (2, D), 0.3, 2.0, ((1, 4),), jnp.float32),
        "w_gauss": bell_draw(seeds[9], (2, HEADS, N), (8 * N) ** -0.5, 0.125, ((1, 4),), jnp.float32),
        "w_out": bell_draw(seeds[10], (D, D), (D // 32) ** -0.5, 1.25, ((0, 4),)),
        "b_out": bell_draw(seeds[11], (D,), 0.3, 2.0, (), jnp.float32),
        "w_fc": bell_draw(seeds[12], (D, FF), D ** -0.5, 0.21875, ((1, 4),)),
        "b_fc": bell_draw(seeds[13], (FF,), 0.3, 2.0, ((0, 4),), jnp.float32),
        "w_proj": bell_draw(seeds[14], (FF, D), FF ** -0.5, 0.109375, ((0, 4),)),
        "b_proj": bell_draw(seeds[15], (D,), 0.3, 2.0, (), jnp.float32),
        "cotangent": bell_draw(seeds[16], (SEGS, SEG, D), 1.0, 6.0, ((0, 32),)),
    }


EPSILON = 1e-05
RIDGE_WEIGHT = 0.5
SIGMA_SCALE = 0.01
SCORE_SCALE = 0.125
NEG_FILL = -1e+30
GELU_COEFF = 0.7978845608028654
PRECISE = lax.Precision.HIGHEST

@jax.custom_vjp
def low(v):
    return lax.optimization_barrier(v.astype(jnp.bfloat16)).astype(jnp.float32)

@jax.custom_vjp
def low_back(v):
    return v

def low_keep(v):
    return (low(v), None)

def low_pass(kept, grad):
    return (grad,)

def back_keep(v):
    return (v, None)

def back_low(kept, grad):
    return (low(grad),)
low.defvjp(low_keep, low_pass)
low_back.defvjp(back_keep, back_low)

def both_round(values):
    return low_back(low(values))

def dense(left_side, right_side):
    return jnp.dot(left_side, right_side, precision=PRECISE)

def layer_norm(values, ln_weight, ln_bias):
    row_mean = lax.optimization_barrier(jnp.mean(values, axis=-1, keepdims=True))
    centred = values - row_mean
    inverse = lax.rsqrt(lax.optimization_barrier(jnp.mean(centred * centred, axis=-1, keepdims=True)) + EPSILON)
    return centred * inverse * ln_weight + ln_bias

def gelu_tanh(values):
    return 0.5 * values * (1.0 + jnp.tanh(GELU_COEFF * (values + 0.044715 * values * values * values)))

def ridge_matrix(bin_row, basis_count, bin_count):
    half_len = bin_row.shape[0]
    first_half = (jnp.arange(half_len, dtype=jnp.float32) + 0.5) / half_len
    sticky_half = (bin_row.astype(jnp.float32) + 0.5) / bin_count
    places = jnp.concatenate([first_half, sticky_half])
    centres = (jnp.arange(basis_count, dtype=jnp.float32) + 0.5) / basis_count
    spread = 1.0 / basis_count
    offsets = places[:, None] - centres[None, :]
    basis_vals = jnp.exp(-offsets * offsets / (2.0 * spread * spread))
    gram_matrix = jnp.dot(basis_vals.T, basis_vals, precision=PRECISE) + RIDGE_WEIGHT * jnp.eye(basis_count, dtype=jnp.float32)
    factor = jnp.linalg.cholesky(gram_matrix)
    return jax.scipy.linalg.cho_solve((factor, True), basis_vals.T)

def memory_density(mem_scores, gauss_weights, basis_count):
    centres = (jnp.arange(basis_count, dtype=jnp.float32) + 0.5) / basis_count
    spread = 1.0 / basis_count
    centre_logit = jnp.einsum('...hsn,hn->...hs', mem_scores, gauss_weights[0], precision=PRECISE)
    width_logit = jnp.einsum('...hsn,hn->...hs', mem_scores, gauss_weights[1], precision=PRECISE)
    middle = jax.nn.sigmoid(centre_logit)
    variance = SIGMA_SCALE * jax.nn.softplus(width_logit) + spread * spread
    offsets = middle[..., None] - centres
    return spread * lax.rsqrt(variance)[..., None] * jnp.exp(-offsets * offsets / (2.0 * variance[..., None]))

def attention_mask(doc_ids, key_valid):
    seg_len = doc_ids.shape[-1]
    places = jnp.arange(seg_len)
    causal = places[None, :] <= places[:, None]
    itself = places[None, :] == places[:, None]
    same_doc = doc_ids[..., :, None] == doc_ids[..., None, :]
    live_key = (key_valid[..., None, :] == 1) | itself
    return causal & same_doc & live_key

def segment_forward(params, packed):
    ln_gain, ln_shift, w_qkv, b_qv, w_gauss, w_out, b_out, w_fc, b_fc, w_proj, b_proj = params
    seg_in, seg_coeffs, seg_docs, seg_valid = packed
    heads_all = w_gauss.shape[1]
    seg_len, model_width = seg_in.shape
    head_dim = model_width // heads_all
    split_shape = (seg_len, heads_all, head_dim)
    mem_shape = (seg_coeffs.shape[0], heads_all, head_dim)
    normed_one = low(layer_norm(seg_in, ln_gain[0], ln_shift[0]))
    queries = both_round(dense(normed_one, w_qkv[0]) + b_qv[0]).reshape(split_shape)
    keys_all = both_round(dense(normed_one, w_qkv[1])).reshape(split_shape)
    values_all = both_round(dense(normed_one, w_qkv[2]) + b_qv[1]).reshape(split_shape)
    mem_keys = both_round(dense(seg_coeffs, w_qkv[1])).reshape(mem_shape)
    mem_values = both_round(dense(seg_coeffs, w_qkv[2])).reshape(mem_shape)
    allowed = attention_mask(seg_docs, seg_valid)
    scores = low_back(jnp.einsum('shd,thd->hst', queries, keys_all, precision=PRECISE) * SCORE_SCALE)
    probs = low(jax.nn.softmax(jnp.where(allowed[None], scores, NEG_FILL), axis=-1))
    attended = jnp.einsum('hst,thd->shd', probs, values_all, precision=PRECISE)
    mem_scores = low_back(jnp.einsum('shd,nhd->hsn', queries, mem_keys, precision=PRECISE) * SCORE_SCALE)
    density = low(memory_density(mem_scores, w_gauss, N))
    mem_gate = (seg_docs == seg_docs[0]).astype(jnp.float32)[:, None, None]
    recalled = jnp.einsum('hsn,nhd->shd', density, mem_values, precision=PRECISE) * mem_gate
    context = both_round((attended + recalled).reshape(seg_len, model_width))
    hidden_one = seg_in + low_back(dense(context, w_out)) + b_out
    normed_two = low(layer_norm(hidden_one, ln_gain[1], ln_shift[1]))
    pre_act = low_back(dense(normed_two, w_fc) + b_fc)
    activation = low(gelu_tanh(pre_act))
    return hidden_one + low_back(dense(activation, w_proj)) + b_proj

def reference(inputs, memory, doc_ids, key_valid, sticky_bins, ln_gain, ln_shift, w_qkv, b_qv, w_gauss, w_out, b_out, w_fc, b_fc, w_proj, b_proj, cotangent):
    params = (ln_gain, ln_shift, w_qkv.astype(jnp.float32), b_qv, w_gauss, w_out.astype(jnp.float32), b_out, w_fc.astype(jnp.float32), b_fc, w_proj.astype(jnp.float32), b_proj)

    def forward(seg_inputs, weights):
        ridge_maps = lax.map(partial(ridge_matrix, basis_count=N, bin_count=NBINS), sticky_bins)
        coeffs = low(jnp.einsum('bnm,bmd->bnd', ridge_maps, memory.astype(jnp.float32), precision=PRECISE))
        step_fn = jax.checkpoint(partial(segment_forward, weights))
        return lax.map(step_fn, (seg_inputs, coeffs, doc_ids, key_valid))
    outputs, pullback = jax.vjp(forward, inputs.astype(jnp.float32), params)
    grad_input, grads = pullback(cotangent.astype(jnp.float32))
    grad_gain, grad_shift, grad_qkv, grad_bias_qv, grad_gauss, grad_wout, grad_bout, grad_wfc, grad_bfc, grad_wproj, grad_bproj = grads
    return (outputs.astype(jnp.bfloat16), grad_input, grad_gain, grad_shift, grad_qkv, grad_bias_qv, grad_gauss, grad_wout, grad_bout, grad_wfc, grad_bfc, grad_wproj, grad_bproj)
```

```python
from functools import partial

import jax
import jax.numpy as jnp
from jax import lax
from jax.experimental import pallas as pl
from jax.experimental.pallas import tpu as pltpu
from jax.sharding import PartitionSpec as P

MESH = pl.DeviceIdType.MESH
BF16, F32 = jnp.bfloat16, jnp.float32
D, N, HEADS, HD, FF, SEG = 768, 256, 12, 64, 3072, 512
SHARD_ROWS = 2304
PIECE = 72
EPSILON = 1e-05
RIDGE_WEIGHT = 0.5
SIGMA_SCALE = 0.01
SCORE_SCALE = 0.125
NEG_FILL = -1e30
GELU_COEFF = 0.7978845608028654
PRECISE = lax.Precision.HIGHEST
VMEM_LIMIT = 60 * 1024 * 1024


class Place:
    def __init__(self):
        dp, head = lax.axis_index("dp"), lax.axis_index("head")
        self.head = head
        self.yl = lax.div(dp, 16)
        self.z = lax.rem(lax.div(dp, 4), 4)
        self.x = lax.rem(dp, 4)
        self.yh = lax.div(head, 2)
        self.c = lax.rem(head, 2)
        self.y = self.yh * 2 + self.yl

    def at(self, x=None, z=None, y=None, c=None):
        x = self.x if x is None else x
        z = self.z if z is None else z
        c = self.c if c is None else c
        if y is None:
            yl, yh = self.yl, self.yh
        else:
            yl, yh = lax.rem(y, 2), lax.div(y, 2)
        return (yl * 16 + z * 4 + x, yh * 2 + c)


def step(place, by):
    return lax.rem(place + by, 4)


def barrier(devices):
    sem = pltpu.get_barrier_semaphore()
    for device in devices:
        pl.semaphore_signal(sem, inc=1, device_id=device, device_id_type=MESH)
    pl.semaphore_wait(sem, len(devices))


class Copies:
    def __init__(self, send, recv):
        self.send, self.recv, self.used = send, recv, 0
        self.open = []

    def start(self, src, dst, device, arrives):
        i = self.used
        self.used += 1
        copy = pltpu.make_async_remote_copy(
            src_ref=src, dst_ref=dst, send_sem=self.send.at[i], recv_sem=self.recv.at[i],
            device_id=device, device_id_type=MESH)
        copy.start()
        self.open.append(copy)
        here = pltpu.make_async_remote_copy(
            src_ref=src, dst_ref=arrives, send_sem=self.send.at[i], recv_sem=self.recv.at[i],
            device_id=device, device_id_type=MESH)
        return here.wait_recv

    def finish(self):
        for copy in self.open:
            copy.wait_send()


def plane_gather(a, me, copies, after_first=None, after_second=None):
    first_x, first_z = [], []
    for k in (1, 3, 2):
        first_x.append(copies.start(a.at[me.z, me.x, 0], a.at[me.z, me.x, 0],
                                    me.at(x=step(me.x, k)), a.at[me.z, step(me.x, 4 - k), 0]))
        first_z.append(copies.start(a.at[me.z, me.x, 1], a.at[me.z, me.x, 1],
                                    me.at(z=step(me.z, k)), a.at[step(me.z, 4 - k), me.x, 1]))
    for wait in first_x:
        wait()
    second = []
    for k in (1, 3, 2):
        second.append((copies.start(a.at[me.z, :, 0], a.at[me.z, :, 0],
                                    me.at(z=step(me.z, k)), a.at[step(me.z, 4 - k), :, 0]),
                       a.at[step(me.z, 4 - k), :, 0]))
    for wait in first_z:
        wait()
    for k in (1, 3, 2):
        second.append((copies.start(a.at[:, me.x, 1], a.at[:, me.x, 1],
                                    me.at(x=step(me.x, k)), a.at[:, step(me.x, 4 - k), 1]),
                       a.at[:, step(me.x, 4 - k), 1]))
    if after_first is not None:
        after_first(a.at[me.z, :, 0])
        after_first(a.at[:, me.x, 1])
    for wait, block in (second[0], second[3], second[1], second[4], second[2], second[5]):
        wait()
        if after_second is not None:
            after_second(block)


def gather_kernel(pack, memory, small, wall, mseg, sall, send, recv, local):
    me = Place()
    core = me.at(c=1 - me.c)
    across = me.at(y=3 - me.y)
    far = [me.at(y=step(me.y, 2)), me.at(y=step(me.y, 2), c=1 - me.c)]
    barrier([core, across] + far + [me.at(x=step(me.x, k)) for k in (1, 2, 3)]
            + [me.at(z=step(me.z, k)) for k in (1, 2, 3)])
    copies = Copies(send, recv)
    waits = []
    remote = wall.at[1 - me.yh, me.c]
    got_across = copies.start(pack.at[me.z, me.x], wall.at[me.yh, me.c, me.z, me.x], across,
                              remote.at[me.z, me.x])
    own = [pltpu.make_async_copy(pack, wall.at[me.yh, me.c], local.at[0]),
           pltpu.make_async_copy(memory.at[me.head], mseg.at[me.head], local.at[1]),
           pltpu.make_async_copy(small, sall.at[me.head], local.at[2])]
    for copy in own:
        copy.start()
    for k in (1, 2, 3):
        other = me.head + k - 4 * lax.div(me.head + k, 4)
        before = me.head + (4 - k) - 4 * lax.div(me.head + (4 - k), 4)
        device = (me.yl * 16 + me.z * 4 + me.x, other)
        waits.append(copies.start(memory.at[other], mseg.at[me.head], device, mseg.at[before]))
        waits.append(copies.start(small, sall.at[me.head], device, sall.at[before]))
    waits.append(copies.start(pack, wall.at[me.yh, me.c], core, wall.at[me.yh, 1 - me.c]))
    got_across()

    def to_core(block):
        index = copies.used
        del index
        waits.append(copies.start(block, block, core, block))

    def forward(select):
        waits.append(copies.start(select(remote), select(remote), core, select(wall.at[1 - me.yh, 1 - me.c])))

    plane_forward(remote, me, copies, forward)
    for wait in waits:
        wait()
    for copy in own:
        copy.wait()
    copies.finish()


def plane_forward(a, me, copies, forward):
    first_x, first_z = [], []
    for k in (1, 3, 2):
        first_x.append(copies.start(a.at[me.z, me.x, 0], a.at[me.z, me.x, 0],
                                    me.at(x=step(me.x, k)), a.at[me.z, step(me.x, 4 - k), 0]))
        first_z.append(copies.start(a.at[me.z, me.x, 1], a.at[me.z, me.x, 1],
                                    me.at(z=step(me.z, k)), a.at[step(me.z, 4 - k), me.x, 1]))
    for wait in first_x:
        wait()
    second = []
    for k in (1, 3, 2):
        back = step(me.z, 4 - k)
        second.append((copies.start(a.at[me.z, :, 0], a.at[me.z, :, 0], me.at(z=step(me.z, k)), a.at[back, :, 0]),
                       lambda ref, back=back: ref.at[back, :, 0]))
    for wait in first_z:
        wait()
    for k in (1, 3, 2):
        back = step(me.x, 4 - k)
        second.append((copies.start(a.at[:, me.x, 1], a.at[:, me.x, 1], me.at(x=step(me.x, k)), a.at[:, back, 1]),
                       lambda ref, back=back: ref.at[:, back, 1]))
    if forward is not None:
        forward(lambda ref: ref.at[me.z, :, 0])
        forward(lambda ref: ref.at[:, me.x, 1])
    for i in (0, 3, 1, 4, 2, 5):
        wait, select = second[i]
        wait()
        if forward is not None:
            forward(select)


def gather_weights(pack, memory, small):
    any_spec = pl.BlockSpec(memory_space=pl.ANY)
    count = 1 + 6 + 1 + 12 + 8
    return pl.pallas_call(
        gather_kernel,
        out_shape=(
            jax.ShapeDtypeStruct((2, 2, 4, 4, 2, PIECE, D), BF16),
            jax.ShapeDtypeStruct((4, 128, D), BF16),
            jax.ShapeDtypeStruct((4, 8, D), F32),
        ),
        in_specs=[any_spec] * 3,
        out_specs=[any_spec] * 3,
        scratch_shapes=[pltpu.SemaphoreType.DMA((count,)), pltpu.SemaphoreType.DMA((count,)),
                        pltpu.SemaphoreType.DMA((3,))],
        compiler_params=pltpu.CompilerParams(collective_id=1, has_side_effects=True),
        name="gather_weights",
    )(pack, memory, small)


def ridge_steps():
    low, high = RIDGE_WEIGHT, 650.0
    gap = (high - low) / (high + low)
    scales = []
    while gap > 1e-9:
        square = gap * gap
        scale = 2.0 / (2.0 - square) if square > 1e-3 else 1.0
        gap = square / (2.0 - square) if square > 1e-3 else square
        scales.append(scale)
    return 2.0 / (low + high), scales


def ridge_kernel(bins, memory, coeffs):
    dot = partial(jnp.dot, preferred_element_type=F32, precision=PRECISE)
    rows = lax.broadcasted_iota(jnp.int32, (N, N), 0)
    cols = lax.broadcasted_iota(jnp.int32, (N, N), 1)
    gap = (rows - cols).astype(F32)
    curve = jnp.exp(-0.5 * gap * gap)
    eye = (rows == cols).astype(F32)
    picked = (bins[...] == rows).astype(F32)
    counts = 1.0 + jnp.sum(picked, axis=1, keepdims=True)
    gram = dot(curve, counts * curve) + RIDGE_WEIGHT * eye
    start, scales = ridge_steps()
    inverse = scales[0] * (2.0 * start * eye - (start * start) * gram)
    for scale in scales[1:]:
        inverse = scale * (2.0 * inverse - dot(inverse, dot(gram, inverse)))
    held = memory[:HALF].astype(F32) + jnp.dot(
        picked.astype(BF16), memory[HALF:], preferred_element_type=F32)
    coeffs[...] = dot(inverse, dot(curve, held)).astype(BF16)


HALF = 256


def ridge(bins, memory):
    return pl.pallas_call(
        ridge_kernel,
        out_shape=jax.ShapeDtypeStruct((N, D), BF16),
        compiler_params=pltpu.CompilerParams(vmem_limit_bytes=VMEM_LIMIT),
        name="ridge",
    )(bins, memory)


def reduce_kernel(grads, small, mixed, gin, total, small_total, mixed_all, gin_all,
                  own, other, sbuf, rbuf, sbuf2, rbuf2, ylocal, ybuf, slots, final,
                  send, recv, local):
    me = Place()
    core = me.at(c=1 - me.c)
    far = me.at(y=step(me.y, 2))
    xs = [me.at(x=step(me.x, k)) for k in (1, 2, 3)]
    zs = [me.at(z=step(me.z, k)) for k in (1, 2, 3)]
    ys = [me.at(y=step(me.y, k)) for k in (1, 2, 3)]
    barrier([core] + xs + zs + ys)
    copies = Copies(send, recv)
    sent_local = []

    def local_copy(src, dst):
        copy = pltpu.make_async_copy(src, dst, local.at[len(sent_local)])
        copy.start()
        sent_local.append(copy)
        return copy

    def chunk(ref, half, k, c):
        if half == 0:
            return ref.at[:, c, :, step(me.x, k), 0]
        return ref.at[:, c, step(me.z, k), :, 1]

    order = [(half, k) for k in (2, 1, 3, 0) for half in (0, 1)]
    arrived, loaded = {}, {}
    for half, k in order:
        slot = half * 4 + k
        arrived[half, k] = copies.start(chunk(grads, half, k, 1 - me.c), other.at[slot], core, other.at[slot])
        loaded[half, k] = local_copy(chunk(grads, half, k, me.c), own.at[slot])
    tail = []
    local_copy(mixed, mixed_all.at[me.head])
    local_copy(gin, gin_all.at[me.head])
    far_head = (1 - me.yh) * 2 + me.c
    got_mixed = copies.start(mixed, mixed_all.at[me.head], far, mixed_all.at[far_head])
    got_gin = copies.start(gin, gin_all.at[me.head], far, gin_all.at[far_head])
    mate = me.yh * 2 + 1 - me.c
    far_mate = (1 - me.yh) * 2 + 1 - me.c
    tail.append(copies.start(mixed, mixed_all.at[me.head], core, mixed_all.at[mate]))
    tail.append(copies.start(gin, gin_all.at[me.head], core, gin_all.at[mate]))

    def small_stage(stage, place, peers_at, count):
        waits = []
        for k in range(1, count):
            back = lax.rem(place + count - k, count)
            waits.append(copies.start(slots.at[stage, place], slots.at[stage, place],
                                      peers_at(lax.rem(place + k, count)), slots.at[stage, back]))
        return waits

    def small_sum(stage, count):
        value = slots[stage, 0]
        for k in range(1, count):
            value = value + slots[stage, k]
        return value

    slots[0, me.c] = small[...]
    small_waits = small_stage(0, me.c, lambda p: me.at(c=p), 2)

    def add_cores(half, k):
        slot = half * 4 + k
        arrived[half, k]()
        loaded[half, k].wait()

        def body(i, carry):
            p, q = lax.div(i, 4), lax.rem(i, 4)
            value = own[slot, p, q] + other[slot, p, q]
            if k == 0:
                own[slot, p, q] = value
            else:
                sbuf[half * 3 + k - 1, p, q] = value.astype(BF16)
            return carry

        lax.fori_loop(0, 8, body, 0)

    got = {}
    for half, k in order:
        add_cores(half, k)
        if k:
            slot = half * 3 + k - 1
            device = xs[k - 1] if half == 0 else zs[k - 1]
            got[half, k] = copies.start(sbuf.at[slot], rbuf.at[slot], device, rbuf.at[slot])
    for wait in small_waits:
        wait()
    slots[1, me.x] = small_sum(0, 2)
    small_waits = small_stage(1, me.x, lambda p: me.at(x=p), 4)

    got2 = {}
    for half in (0, 1):
        for k in (1, 2, 3):
            got[half, k]()
        across = me.z if half == 0 else me.x

        def body(i, carry, half=half):
            p, q = lax.div(i, 4), lax.rem(i, 4)
            value = own[half * 4, p, q]
            for k in (1, 2, 3):
                value = value + rbuf[half * 3 + k - 1, p, q].astype(F32)
            own[half * 4, p, q] = value
            return carry

        lax.fori_loop(0, 8, body, 0)
        for k in (2, 1, 3):
            slot = half * 3 + k - 1
            target = step(across, k)
            for p in (0, 1):
                sbuf2[slot, p] = own[half * 4, p, target].astype(BF16)
            device = zs[k - 1] if half == 0 else xs[k - 1]
            got2[half, k] = copies.start(sbuf2.at[slot], rbuf2.at[slot], device, rbuf2.at[slot])
    for wait in small_waits:
        wait()
    slots[2, me.z] = small_sum(1, 4)
    small_waits = small_stage(2, me.z, lambda p: me.at(z=p), 4)
    for half in (0, 1):
        for k in (1, 2, 3):
            got2[half, k]()
        across = me.z if half == 0 else me.x
        for p in (0, 1):
            value = own[half * 4, p, across]
            for k in (1, 2, 3):
                value = value + rbuf2[half * 3 + k - 1, p].astype(F32)
            ylocal[p, half] = value
    got3 = []
    for k in (2, 1, 3):
        y = step(me.y, k)
        got3.append(copies.start(ylocal.at[lax.div(y, 2), lax.rem(y, 2)], ybuf.at[k - 1], me.at(y=y), ybuf.at[k - 1]))
    for wait in small_waits:
        wait()
    slots[3, me.y] = small_sum(2, 4)
    small_waits = small_stage(3, me.y, lambda p: me.at(y=p), 4)
    for wait in got3:
        wait()
    final[...] = (ylocal[me.yh, me.yl] + ybuf[0] + ybuf[1] + ybuf[2]).astype(BF16)
    pair = me.at(y=me.yh * 2 + 1 - me.yl)
    keep = local_copy(final, total.at[me.z, me.x, me.yl])
    got_pair = copies.start(final, total.at[me.z, me.x, me.yl], pair, total.at[me.z, me.x, 1 - me.yl])
    for wait in small_waits:
        wait()
    small_total[...] = small_sum(3, 4)
    got_mixed()
    tail.append(copies.start(mixed_all.at[far_head], mixed_all.at[far_head], core, mixed_all.at[far_mate]))
    keep.wait()
    got_pair()
    plane_forward(total, me, copies, None)
    got_gin()
    tail.append(copies.start(gin_all.at[far_head], gin_all.at[far_head], core, gin_all.at[far_mate]))
    for wait in tail:
        wait()
    for copy in sent_local[8:10]:
        copy.wait()
    copies.finish()


def reduce_all(grads, small, mixed, gin):
    any_spec = pl.BlockSpec(memory_space=pl.ANY)
    vmem_spec = pl.BlockSpec(memory_space=pltpu.VMEM)
    rows = small.shape[0]
    count = 8 + 6 + (1 + 3 + 3 + 3) + 6 + 6 + 3 + 1 + 12
    return pl.pallas_call(
        reduce_kernel,
        out_shape=(
            jax.ShapeDtypeStruct((4, 4, 2, PIECE, D), BF16),
            jax.ShapeDtypeStruct((rows, D), F32),
            jax.ShapeDtypeStruct((4, SEG, D), BF16),
            jax.ShapeDtypeStruct((4, SEG, D), F32),
        ),
        in_specs=[any_spec, vmem_spec, any_spec, any_spec],
        out_specs=[any_spec, vmem_spec, any_spec, any_spec],
        scratch_shapes=[
            pltpu.VMEM((8, 2, 4, PIECE, D), F32),
            pltpu.VMEM((8, 2, 4, PIECE, D), F32),
            pltpu.VMEM((6, 2, 4, PIECE, D), BF16),
            pltpu.VMEM((6, 2, 4, PIECE, D), BF16),
            pltpu.VMEM((6, 2, PIECE, D), BF16),
            pltpu.VMEM((6, 2, PIECE, D), BF16),
            pltpu.VMEM((2, 2, PIECE, D), F32),
            pltpu.VMEM((3, PIECE, D), F32),
            pltpu.VMEM((4, 4, rows, D), F32),
            pltpu.VMEM((PIECE, D), BF16),
            pltpu.SemaphoreType.DMA((count,)),
            pltpu.SemaphoreType.DMA((count,)),
            pltpu.SemaphoreType.DMA((12,)),
        ],
        compiler_params=pltpu.CompilerParams(
            collective_id=2, has_side_effects=True, vmem_limit_bytes=VMEM_LIMIT),
        name="reduce_all",
    )(grads, small, mixed, gin)


def layer_norm(values, ln_weight, ln_bias):
    row_mean = jnp.mean(values, axis=-1, keepdims=True)
    centred = values - row_mean
    inverse = lax.rsqrt(jnp.mean(centred * centred, axis=-1, keepdims=True) + EPSILON)
    return centred * inverse * ln_weight + ln_bias


def gelu_tanh(values):
    return (
        0.5 * values * (1.0 + jnp.tanh(GELU_COEFF * (values + 0.044715 * values * values * values)))
    )


def memory_density(mem_scores, gauss_weights, basis_count):
    centres = (jnp.arange(basis_count, dtype=F32) + 0.5) / basis_count
    spread = 1.0 / basis_count
    centre_logit = jnp.einsum("hsn,hn->hs", mem_scores, gauss_weights[0], precision=PRECISE)
    width_logit = jnp.einsum("hsn,hn->hs", mem_scores, gauss_weights[1], precision=PRECISE)
    middle = jax.nn.sigmoid(centre_logit)
    variance = SIGMA_SCALE * jax.nn.softplus(width_logit) + spread * spread
    offsets = middle[..., None] - centres
    return (
        spread
        * lax.rsqrt(variance)[..., None]
        * jnp.exp(-offsets * offsets / (2.0 * variance[..., None]))
    )


def attention_mask(doc_ids, key_valid):
    seg_len = doc_ids.shape[-1]
    places = jnp.arange(seg_len)
    causal = places[None, :] <= places[:, None]
    itself = places[None, :] == places[:, None]
    same_doc = doc_ids[:, None] == doc_ids[None, :]
    live_key = (key_valid[None, :] == 1) | itself
    return causal & same_doc & live_key


def ein(spec, *args):
    return jnp.einsum(spec, *args, preferred_element_type=F32)


def shards(inputs, memory, doc_ids, key_valid, sticky_bins, ln_gain, ln_shift, w_qkv, b_qv, w_gauss, w_out, b_out,
           w_fc, b_fc, w_proj, b_proj, cotangent):
    head = lax.axis_index("head")
    flat_in = inputs[head].astype(F32)
    grad_rows = cotangent[head]
    docs, valid, bins = doc_ids[head], key_valid[head], sticky_bins[head]
    pack = jnp.concatenate(
        [w_qkv.transpose(0, 2, 1).reshape(576, D), w_out, w_fc, w_proj], axis=0
    ).reshape(4, 4, 2, PIECE, D)
    small = jnp.concatenate(
        [b_qv.reshape(-1), jnp.zeros((384,), F32), w_gauss.reshape(-1), b_fc, jnp.zeros((4 * D,), F32)]
    ).reshape(8, D)
    wall, mseg, sall = gather_weights(pack, memory, small)
    wall = wall.reshape(4, SHARD_ROWS, D)
    wqkv = wall[:, :576].reshape(4, 3, 192, D)
    wout = wall[:, 576:768].reshape(D, D)
    wfc = wall[:, 768:1536]
    wproj = wall[:, 1536:].reshape(FF, D)
    sall = sall.reshape(4, 8 * D)
    bqv = sall[:, :384].reshape(4, 2, 192).transpose(1, 0, 2).reshape(2, D)
    gauss = sall[:, 768:2304].reshape(4, 2, 3, N).transpose(1, 0, 2, 3).reshape(2, HEADS, N)
    bfc = sall[:, 2304:3072].reshape(FF)
    coeffs = ridge(bins[None], mseg.reshape(512, D))

    normed_one = layer_norm(flat_in, ln_gain[0], ln_shift[0]).astype(BF16)
    projected = ein("rd,gkpd->krgp", normed_one, wqkv).reshape(3, SEG, D)
    split = (SEG, HEADS, HD)
    queries = (projected[0] + bqv[0]).astype(BF16).reshape(split)
    keys_low = projected[1].astype(BF16).reshape(split)
    values_low = (projected[2] + bqv[1]).astype(BF16).reshape(split)
    mem_proj = ein("nd,gkpd->kngp", coeffs, wqkv[:, 1:]).astype(BF16).reshape(2, N, HEADS, HD)
    mem_keys, mem_values = mem_proj[0], mem_proj[1]
    allowed = attention_mask(docs, valid)
    raw = ein("shd,thd->hst", queries, keys_low) * SCORE_SCALE
    scores = jnp.where(allowed[None], raw, NEG_FILL)
    row_max = jnp.max(scores, axis=-1, keepdims=True)
    log_total = row_max + jnp.log(jnp.sum(jnp.exp(scores - row_max), axis=-1, keepdims=True))
    probs = jnp.exp(scores - log_total)
    probs_low = probs.astype(BF16)
    attended = ein("hst,thd->shd", probs_low, values_low)
    mem_scores = ein("shd,nhd->hsn", queries, mem_keys) * SCORE_SCALE
    density, density_back = jax.vjp(partial(memory_density, basis_count=N), mem_scores, gauss)
    density_low = density.astype(BF16)
    mem_gate = (docs == docs[:1]).astype(F32)[:, None, None]
    recalled = ein("hsn,nhd->shd", density_low, mem_values) * mem_gate
    context = (attended + recalled).astype(BF16).reshape(SEG, D)
    branch = jnp.dot(context, wout, preferred_element_type=F32)
    hidden_one = flat_in + branch + b_out
    normed_two = layer_norm(hidden_one, ln_gain[1], ln_shift[1]).astype(BF16)
    pre_act = ein("rd,gdf->rgf", normed_two, wfc).reshape(SEG, FF) + bfc
    activation = gelu_tanh(pre_act).astype(BF16)
    mlp_out = jnp.dot(activation, wproj, preferred_element_type=F32)
    mixed = (hidden_one + mlp_out + b_proj).astype(BF16)
    grad_b_proj = jnp.sum(grad_rows.astype(F32), axis=0)
    grad_w_proj = ein("rf,rd->fd", activation, grad_rows)
    grad_act = ein("rd,fd->rf", grad_rows, wproj)
    grad_pre = jax.vjp(gelu_tanh, pre_act)[1](grad_act)[0].astype(BF16)
    grad_b_fc = jnp.sum(grad_pre.astype(F32), axis=0)
    grad_pre_g = grad_pre.reshape(SEG, 4, D)
    grad_w_fc = ein("rd,rgf->gdf", normed_two, grad_pre_g)
    grad_normed_two = ein("rgf,gdf->rd", grad_pre_g, wfc)
    part, grad_gain_two, grad_shift_two = jax.vjp(layer_norm, hidden_one, ln_gain[1], ln_shift[1])[1](grad_normed_two)
    grad_hidden = grad_rows.astype(F32) + part
    grad_b_out = jnp.sum(grad_hidden, axis=0)
    grad_branch = grad_hidden.astype(BF16)
    grad_w_out = ein("rp,rd->pd", context, grad_branch)
    grad_context = ein("rd,pd->rp", grad_branch, wout).astype(BF16).reshape(split)
    grad_probs = ein("shd,thd->hst", grad_context, values_low)
    grad_values = ein("hst,shd->thd", probs_low, grad_context).astype(BF16)
    row_inner = jnp.sum(probs * grad_probs, axis=-1, keepdims=True)
    grad_scores = (probs * (grad_probs - row_inner)).astype(BF16)
    query_part = ein("hst,thd->shd", grad_scores, keys_low) * SCORE_SCALE
    grad_keys = (ein("hst,shd->thd", grad_scores, queries) * SCORE_SCALE).astype(BF16)
    grad_recalled = grad_context * mem_gate.astype(BF16)
    grad_density = ein("shd,nhd->hsn", grad_recalled, mem_values)
    grad_mem_values = ein("hsn,shd->nhd", density_low, grad_recalled).astype(BF16)
    grad_mem_scores, grad_gauss = density_back(grad_density)
    grad_mem_low = grad_mem_scores.astype(BF16)
    memory_part = ein("hsn,nhd->shd", grad_mem_low, mem_keys) * SCORE_SCALE
    grad_mem_keys = (ein("hsn,shd->nhd", grad_mem_low, queries) * SCORE_SCALE).astype(BF16)
    grad_queries = (query_part + memory_part).astype(BF16)
    grad_proj = jnp.stack([grad_queries, grad_keys, grad_values]).reshape(3, SEG, 4, 192)
    token_part = ein("krgp,rd->gkpd", grad_proj, normed_one)
    mem_grads = jnp.stack([grad_mem_keys, grad_mem_values]).reshape(2, N, 4, 192)
    mem_part = ein("kngp,nd->gkpd", mem_grads, coeffs)
    grad_w_qkv = token_part + jnp.pad(mem_part, ((0, 0), (1, 0), (0, 0), (0, 0)))
    flat_proj = grad_proj.astype(F32)
    grad_b_qv = jnp.stack([flat_proj[0].sum(axis=0), flat_proj[2].sum(axis=0)], axis=1)
    grad_normed_one = ein("krgp,gkpd->rd", grad_proj, wqkv)
    part, grad_gain_one, grad_shift_one = jax.vjp(layer_norm, flat_in, ln_gain[0], ln_shift[0])[1](grad_normed_one)
    grad_input = grad_hidden + part

    grads = jnp.concatenate(
        [grad_w_qkv.reshape(4, 576, D), grad_w_out.reshape(4, 192, D), grad_w_fc, grad_w_proj.reshape(4, D, D)],
        axis=1).reshape(2, 2, 4, 4, 2, PIECE, D)
    small_grads = jnp.concatenate([
        grad_gain_one, grad_gain_two, grad_shift_one, grad_shift_two, grad_b_out, grad_b_proj,
        grad_b_qv.reshape(-1), grad_gauss.reshape(2, 4, 3, N).transpose(1, 0, 2, 3).reshape(-1), grad_b_fc,
        jnp.zeros((4 * D,), F32)]).reshape(24, D)
    total, small_total, mixed_all, gin_all = reduce_all(grads, small_grads, mixed, grad_input)
    total = total.reshape(SHARD_ROWS, D).astype(F32)
    g_bqv = lax.dynamic_slice_in_dim(small_total[6:8].reshape(4, 2, 192), head, 1, 0)[0]
    g_gauss = lax.dynamic_slice_in_dim(small_total[8:16].reshape(4, 2, 3, N), head, 1, 0)[0]
    g_bfc = lax.dynamic_slice_in_dim(small_total[16:20], head, 1, 0)[0]
    return (
        mixed_all,
        gin_all,
        small_total[0:2],
        small_total[2:4],
        total[:576].reshape(3, 192, D).transpose(0, 2, 1),
        g_bqv,
        g_gauss,
        total[576:768],
        small_total[4],
        total[768:1536],
        g_bfc,
        total[1536:],
        small_total[5],
    )


def solution(mesh):
    return jax.shard_map(
        shards,
        mesh=mesh,
        in_specs=(
            P("dp", None, None),
            P("dp", "head", None),
            P("dp", None),
            P("dp", None),
            P("dp", None),
            P(),
            P(),
            P(None, None, "head"),
            P(None, "head"),
            P(None, "head", None),
            P("head", None),
            P(),
            P(None, "head"),
            P("head"),
            P("head", None),
            P(),
            P("dp", None, None),
        ),
        out_specs=(
            P("dp", None, None),
            P("dp", None, None),
            P(),
            P(),
            P(None, None, "head"),
            P(None, "head"),
            P(None, "head", None),
            P("head", None),
            P(),
            P(None, "head"),
            P("head"),
            P("head", None),
            P(),
        ),
        check_vma=False,
    )
```

```python
from functools import partial

import jax
import jax.numpy as jnp
from jax import lax
from jax.experimental import pallas as pl
from jax.experimental.pallas import tpu as pltpu
from jax.sharding import PartitionSpec as P

MESH = pl.DeviceIdType.MESH
BF16, F32 = jnp.bfloat16, jnp.float32
D, N, HEADS, HD, FF, SEG = 768, 256, 12, 64, 3072, 512
ATT_ROWS, MLP_ROWS = 768, 1536
ATT, MLP = ATT_ROWS // 32, MLP_ROWS // 32
HALF = 256
EPSILON = 1e-05
RIDGE_WEIGHT = 0.5
SIGMA_SCALE = 0.01
SCORE_SCALE = 0.125
NEG_FILL = -1e30
GELU_COEFF = 0.7978845608028654
PRECISE = lax.Precision.HIGHEST
VMEM_LIMIT = 60 * 1024 * 1024


class Place:
    def __init__(self):
        dp, head = lax.axis_index("dp"), lax.axis_index("head")
        self.head = head
        self.yl = lax.div(dp, 16)
        self.z = lax.rem(lax.div(dp, 4), 4)
        self.x = lax.rem(dp, 4)
        self.yh = lax.div(head, 2)
        self.c = lax.rem(head, 2)
        self.y = self.yh * 2 + self.yl

    def at(self, x=None, z=None, y=None, c=None):
        x = self.x if x is None else x
        z = self.z if z is None else z
        c = self.c if c is None else c
        if y is None:
            yl, yh = self.yl, self.yh
        else:
            yl, yh = lax.rem(y, 2), lax.div(y, 2)
        return (yl * 16 + z * 4 + x, yh * 2 + c)


def step(place, by):
    return lax.rem(place + by, 4)


def barrier(devices):
    sem = pltpu.get_barrier_semaphore()
    for device in devices:
        pl.semaphore_signal(sem, inc=1, device_id=device, device_id_type=MESH)
    pl.semaphore_wait(sem, len(devices))


class Copies:
    def __init__(self, send, recv):
        self.send, self.recv, self.used = send, recv, 0
        self.open = []

    def start(self, src, dst, device, arrives):
        i = self.used
        self.used += 1
        copy = pltpu.make_async_remote_copy(
            src_ref=src, dst_ref=dst, send_sem=self.send.at[i], recv_sem=self.recv.at[i],
            device_id=device, device_id_type=MESH)
        copy.start()
        self.open.append(copy)
        here = pltpu.make_async_remote_copy(
            src_ref=src, dst_ref=arrives, send_sem=self.send.at[i], recv_sem=self.recv.at[i],
            device_id=device, device_id_type=MESH)
        return here.wait_recv

    def finish(self):
        for copy in self.open:
            copy.wait_send()


def plane_forward(a, me, copies, forward):
    first_x, first_z = [], []
    for k in (1, 3, 2):
        first_x.append(copies.start(a.at[me.z, me.x, 0], a.at[me.z, me.x, 0],
                                    me.at(x=step(me.x, k)), a.at[me.z, step(me.x, 4 - k), 0]))
        first_z.append(copies.start(a.at[me.z, me.x, 1], a.at[me.z, me.x, 1],
                                    me.at(z=step(me.z, k)), a.at[step(me.z, 4 - k), me.x, 1]))
    for wait in first_x:
        wait()
    second = []
    for k in (1, 3, 2):
        back = step(me.z, 4 - k)
        second.append((copies.start(a.at[me.z, :, 0], a.at[me.z, :, 0], me.at(z=step(me.z, k)), a.at[back, :, 0]),
                       lambda ref, back=back: ref.at[back, :, 0]))
    for wait in first_z:
        wait()
    for k in (1, 3, 2):
        back = step(me.x, 4 - k)
        second.append((copies.start(a.at[:, me.x, 1], a.at[:, me.x, 1], me.at(x=step(me.x, k)), a.at[:, back, 1]),
                       lambda ref, back=back: ref.at[:, back, 1]))
    if forward is not None:
        forward(lambda ref: ref.at[me.z, :, 0])
        forward(lambda ref: ref.at[:, me.x, 1])
    for i in (0, 3, 1, 4, 2, 5):
        wait, select = second[i]
        wait()
        if forward is not None:
            forward(select)


def gather_kernel(patt, pmlp, memory, small, watt, wmlp, mseg, sall, send, recv, local):
    me = Place()
    core = me.at(c=1 - me.c)
    across = me.at(y=3 - me.y)
    far = [me.at(y=step(me.y, 2)), me.at(y=step(me.y, 2), c=1 - me.c)]
    barrier([core, across] + far + [me.at(x=step(me.x, k)) for k in (1, 2, 3)]
            + [me.at(z=step(me.z, k)) for k in (1, 2, 3)])
    copies = Copies(send, recv)
    waits = []
    parts = ((patt, watt), (pmlp, wmlp))
    got_across = [copies.start(pack.at[me.z, me.x], wall.at[me.yh, me.c, me.z, me.x], across,
                               wall.at[1 - me.yh, me.c, me.z, me.x]) for pack, wall in parts]
    own = [pltpu.make_async_copy(patt, watt.at[me.yh, me.c], local.at[0]),
           pltpu.make_async_copy(pmlp, wmlp.at[me.yh, me.c], local.at[1]),
           pltpu.make_async_copy(memory.at[me.head], mseg.at[me.head], local.at[2]),
           pltpu.make_async_copy(small, sall.at[me.head], local.at[3])]
    for copy in own:
        copy.start()
    for k in (1, 2, 3):
        other, before = lax.rem(me.head + k, 4), lax.rem(me.head + (4 - k), 4)
        device = (me.yl * 16 + me.z * 4 + me.x, other)
        waits.append(copies.start(memory.at[other], mseg.at[me.head], device, mseg.at[before]))
        waits.append(copies.start(small, sall.at[me.head], device, sall.at[before]))
    for (pack, wall), got in zip(parts, got_across):
        waits.append(copies.start(pack, wall.at[me.yh, me.c], core, wall.at[me.yh, 1 - me.c]))
        remote, mate = wall.at[1 - me.yh, me.c], wall.at[1 - me.yh, 1 - me.c]

        def forward(select, remote=remote, mate=mate):
            waits.append(copies.start(select(remote), select(remote), core, select(mate)))

        got()
        plane_forward(remote, me, copies, forward)
    for wait in waits:
        wait()
    for copy in own:
        copy.wait()
    copies.finish()


def gather_weights(patt, pmlp, memory, small):
    any_spec, vmem = pl.BlockSpec(memory_space=pl.ANY), pl.BlockSpec(memory_space=pltpu.VMEM)
    count = 2 + 6 + 2 * (1 + 12 + 8)
    return pl.pallas_call(
        gather_kernel,
        out_shape=(
            jax.ShapeDtypeStruct((2, 2, 4, 4, 2, ATT, D), BF16),
            jax.ShapeDtypeStruct((2, 2, 4, 4, 2, MLP, D), BF16),
            jax.ShapeDtypeStruct((4, 128, D), BF16),
            jax.ShapeDtypeStruct((4, 8, D), F32),
        ),
        in_specs=[vmem] * 4,
        out_specs=[any_spec] * 4,
        scratch_shapes=[pltpu.SemaphoreType.DMA((count,)), pltpu.SemaphoreType.DMA((count,)),
                        pltpu.SemaphoreType.DMA((4,))],
        compiler_params=pltpu.CompilerParams(
            collective_id=1, has_side_effects=True, vmem_limit_bytes=VMEM_LIMIT),
        name="gather_weights",
    )(patt, pmlp, memory, small)


def ridge_steps():
    low, high = RIDGE_WEIGHT, 650.0
    gap = (high - low) / (high + low)
    scales = []
    while gap > 1e-9:
        square = gap * gap
        scale = 2.0 / (2.0 - square) if square > 1e-3 else 1.0
        gap = square / (2.0 - square) if square > 1e-3 else square
        scales.append(scale)
    return 2.0 / (low + high), scales


def ridge_kernel(bins, memory, coeffs):
    dot = partial(jnp.dot, preferred_element_type=F32, precision=PRECISE)
    rows = lax.broadcasted_iota(jnp.int32, (N, N), 0)
    cols = lax.broadcasted_iota(jnp.int32, (N, N), 1)
    gap = (rows - cols).astype(F32)
    curve = jnp.exp(-0.5 * gap * gap)
    eye = (rows == cols).astype(F32)
    picked = (bins[...] == rows).astype(F32)
    counts = 1.0 + jnp.sum(picked, axis=1, keepdims=True)
    gram = dot(curve, counts * curve) + RIDGE_WEIGHT * eye
    start, scales = ridge_steps()
    inverse = scales[0] * (2.0 * start * eye - (start * start) * gram)
    for scale in scales[1:]:
        inverse = scale * (2.0 * inverse - dot(inverse, dot(gram, inverse)))
    held = memory[:HALF].astype(F32) + jnp.dot(
        picked.astype(BF16), memory[HALF:], preferred_element_type=F32)
    coeffs[...] = dot(inverse, dot(curve, held)).astype(BF16)


def ridge(bins, memory):
    return pl.pallas_call(
        ridge_kernel,
        out_shape=jax.ShapeDtypeStruct((N, D), BF16),
        compiler_params=pltpu.CompilerParams(vmem_limit_bytes=VMEM_LIMIT),
        name="ridge",
    )(bins, memory)


class PartSum:
    ORDER = [(half, k) for k in (2, 1, 3, 0) for half in (0, 1)]

    def __init__(self, me, copies, grads, total, own, other, sbuf, rbuf, sbuf2, rbuf2, ylocal, ybuf, final, local):
        self.me, self.copies, self.grads, self.total = me, copies, grads, total
        self.own, self.other, self.sbuf, self.rbuf = own, other, sbuf, rbuf
        self.sbuf2, self.rbuf2, self.ylocal, self.ybuf, self.final = sbuf2, rbuf2, ylocal, ybuf, final
        self.local = local

    def chunk(self, half, k, c):
        me = self.me
        if half == 0:
            return self.grads.at[:, c, :, step(me.x, k), 0]
        return self.grads.at[:, c, step(me.z, k), :, 1]

    def start_cores(self):
        me = self.me
        core = me.at(c=1 - me.c)
        self.arrived, self.loaded = {}, {}
        for half, k in self.ORDER:
            slot = half * 4 + k
            self.arrived[half, k] = self.copies.start(
                self.chunk(half, k, 1 - me.c), self.other.at[slot], core, self.other.at[slot])
            copy = pltpu.make_async_copy(self.chunk(half, k, me.c), self.own.at[slot], self.local.at[slot])
            copy.start()
            self.loaded[half, k] = copy

    def peer(self, along_x, k):
        return self.me.at(x=step(self.me.x, k)) if along_x else self.me.at(z=step(self.me.z, k))

    def first(self):
        self.got = {}
        for half, k in self.ORDER:
            slot = half * 4 + k
            self.arrived[half, k]()
            self.loaded[half, k].wait()

            def body(i, carry, slot=slot, half=half, k=k):
                p, q = lax.div(i, 4), lax.rem(i, 4)
                value = self.own[slot, p, q] + self.other[slot, p, q]
                if k == 0:
                    self.own[slot, p, q] = value
                else:
                    self.sbuf[half * 3 + k - 1, p, q] = value.astype(BF16)
                return carry

            lax.fori_loop(0, 8, body, 0)
            if k:
                i = half * 3 + k - 1
                self.got[half, k] = self.copies.start(
                    self.sbuf.at[i], self.rbuf.at[i], self.peer(half == 0, k), self.rbuf.at[i])

    def second(self):
        me = self.me
        self.got2 = {}
        for half in (0, 1):
            for k in (1, 2, 3):
                self.got[half, k]()
            across = me.z if half == 0 else me.x

            def body(i, carry, half=half):
                p, q = lax.div(i, 4), lax.rem(i, 4)
                value = self.own[half * 4, p, q]
                for k in (1, 2, 3):
                    value = value + self.rbuf[half * 3 + k - 1, p, q].astype(F32)
                self.own[half * 4, p, q] = value
                return carry

            lax.fori_loop(0, 8, body, 0)
            for k in (2, 1, 3):
                i = half * 3 + k - 1
                for p in (0, 1):
                    self.sbuf2[i, p] = self.own[half * 4, p, step(across, k)]
                self.got2[half, k] = self.copies.start(
                    self.sbuf2.at[i], self.rbuf2.at[i], self.peer(half == 1, k), self.rbuf2.at[i])

    def third(self):
        me = self.me
        for half in (0, 1):
            for k in (1, 2, 3):
                self.got2[half, k]()
            across = me.z if half == 0 else me.x
            for p in (0, 1):
                value = self.own[half * 4, p, across]
                for k in (1, 2, 3):
                    value = value + self.rbuf2[half * 3 + k - 1, p]
                self.ylocal[p, half] = value
        self.got3 = []
        for k in (2, 1, 3):
            y = step(me.y, k)
            self.got3.append(self.copies.start(
                self.ylocal.at[lax.div(y, 2), lax.rem(y, 2)], self.ybuf.at[k - 1], me.at(y=y), self.ybuf.at[k - 1]))

    def pair(self):
        me = self.me
        for wait in self.got3:
            wait()
        self.final[...] = (self.ylocal[me.yh, me.yl] + self.ybuf[0] + self.ybuf[1] + self.ybuf[2]).astype(
            self.final.dtype)
        mate = me.at(y=me.yh * 2 + 1 - me.yl)
        block = self.total.at[me.z, me.x, me.yl]
        self.keep = pltpu.make_async_copy(self.final, block, self.local.at[8])
        self.keep.start()
        self.got_pair = self.copies.start(self.final, block, mate, self.total.at[me.z, me.x, 1 - me.yl])

    def gather(self):
        self.keep.wait()
        self.got_pair()
        return PlaneGather(self.total, self.me, self.copies)


class PlaneGather:
    def __init__(self, a, me, copies):
        self.a, self.me, self.copies = a, me, copies
        self.waits = [[], []]
        for k in (1, 3, 2):
            self.waits[0].append(copies.start(
                a.at[me.z, me.x, 0], a.at[me.z, me.x, 0], me.at(x=step(me.x, k)), a.at[me.z, step(me.x, 4 - k), 0]))
            self.waits[1].append(copies.start(
                a.at[me.z, me.x, 1], a.at[me.z, me.x, 1], me.at(z=step(me.z, k)), a.at[step(me.z, 4 - k), me.x, 1]))

    def second(self):
        a, me, copies = self.a, self.me, self.copies
        last = []
        for wait in self.waits[0]:
            wait()
        for k in (1, 3, 2):
            last.append(copies.start(
                a.at[me.z, :, 0], a.at[me.z, :, 0], me.at(z=step(me.z, k)), a.at[step(me.z, 4 - k), :, 0]))
        for wait in self.waits[1]:
            wait()
        for k in (1, 3, 2):
            last.append(copies.start(
                a.at[:, me.x, 1], a.at[:, me.x, 1], me.at(x=step(me.x, k)), a.at[:, step(me.x, 4 - k), 1]))
        self.last = last

    def finish(self):
        for wait in self.last:
            wait()


def reduce_kernel(gatt, gmlp, small, mixed, gin, tatt, tmlp, small_total, mixed_all, gin_all, *scratch):
    satt, smlp, (slots, send, recv, latt, lmlp, local) = scratch[:9], scratch[9:18], scratch[18:]
    me = Place()
    core = me.at(c=1 - me.c)
    far = me.at(y=step(me.y, 2))
    barrier([core] + [me.at(x=step(me.x, k)) for k in (1, 2, 3)] + [me.at(z=step(me.z, k)) for k in (1, 2, 3)]
            + [me.at(y=step(me.y, k)) for k in (1, 2, 3)])
    copies = Copies(send, recv)
    mlp = PartSum(me, copies, gmlp, tmlp, *smlp, lmlp)
    att = PartSum(me, copies, gatt, tatt, *satt, latt)
    mlp.start_cores()
    att.start_cores()
    keep = [pltpu.make_async_copy(mixed, mixed_all.at[me.head], local.at[0]),
            pltpu.make_async_copy(gin, gin_all.at[me.head], local.at[1])]
    for copy in keep:
        copy.start()
    far_head = (1 - me.yh) * 2 + me.c
    mate, far_mate = me.yh * 2 + 1 - me.c, (1 - me.yh) * 2 + 1 - me.c
    got_mixed = copies.start(mixed, mixed_all.at[me.head], far, mixed_all.at[far_head])
    got_gin = copies.start(gin, gin_all.at[me.head], far, gin_all.at[far_head])
    tail = [copies.start(mixed, mixed_all.at[me.head], core, mixed_all.at[mate]),
            copies.start(gin, gin_all.at[me.head], core, gin_all.at[mate])]

    def small_stage(stage, place, peers_at, count):
        waits = []
        for k in range(1, count):
            back = lax.rem(place + count - k, count)
            waits.append(copies.start(slots.at[stage, place], slots.at[stage, place],
                                      peers_at(lax.rem(place + k, count)), slots.at[stage, back]))
        return waits

    def small_sum(waits, stage, count):
        for wait in waits:
            wait()
        value = slots[stage, 0]
        for k in range(1, count):
            value = value + slots[stage, k]
        return value

    slots[0, me.c] = small[...]
    waits = small_stage(0, me.c, lambda p: me.at(c=p), 2)
    mlp.first()
    att.first()
    slots[1, me.x] = small_sum(waits, 0, 2)
    waits = small_stage(1, me.x, lambda p: me.at(x=p), 4)
    mlp.second()
    att.second()
    slots[2, me.z] = small_sum(waits, 1, 4)
    waits = small_stage(2, me.z, lambda p: me.at(z=p), 4)
    mlp.third()
    att.third()
    slots[3, me.y] = small_sum(waits, 2, 4)
    waits = small_stage(3, me.y, lambda p: me.at(y=p), 4)
    mlp.pair()
    att.pair()
    gather_mlp = mlp.gather()
    gather_att = att.gather()
    gather_mlp.second()
    gather_att.second()
    small_total[...] = small_sum(waits, 3, 4)
    got_mixed()
    tail.append(copies.start(mixed_all.at[far_head], mixed_all.at[far_head], core, mixed_all.at[far_mate]))
    got_gin()
    tail.append(copies.start(gin_all.at[far_head], gin_all.at[far_head], core, gin_all.at[far_mate]))
    gather_mlp.finish()
    gather_att.finish()
    for wait in tail:
        wait()
    for copy in keep:
        copy.wait()
    copies.finish()


def part_scratch(rows, dtype):
    return [
        pltpu.VMEM((8, 2, 4, rows, D), F32),
        pltpu.VMEM((8, 2, 4, rows, D), F32),
        pltpu.VMEM((6, 2, 4, rows, D), BF16),
        pltpu.VMEM((6, 2, 4, rows, D), BF16),
        pltpu.VMEM((6, 2, rows, D), F32),
        pltpu.VMEM((6, 2, rows, D), F32),
        pltpu.VMEM((2, 2, rows, D), F32),
        pltpu.VMEM((3, rows, D), F32),
        pltpu.VMEM((rows, D), dtype),
    ]


def reduce_all(gatt, gmlp, small, mixed, gin):
    any_spec = pl.BlockSpec(memory_space=pl.ANY)
    vmem = pl.BlockSpec(memory_space=pltpu.VMEM)
    rows = small.shape[0]
    count = 2 * (8 + 6 + 6 + 3 + 1 + 12) + (1 + 3 + 3 + 3) + 6
    return pl.pallas_call(
        reduce_kernel,
        out_shape=(
            jax.ShapeDtypeStruct((4, 4, 2, ATT, D), F32),
            jax.ShapeDtypeStruct((4, 4, 2, MLP, D), BF16),
            jax.ShapeDtypeStruct((rows, D), F32),
            jax.ShapeDtypeStruct((4, SEG, D), BF16),
            jax.ShapeDtypeStruct((4, SEG, D), F32),
        ),
        in_specs=[any_spec, any_spec, vmem, vmem, vmem],
        out_specs=[any_spec, any_spec, vmem, any_spec, any_spec],
        scratch_shapes=part_scratch(ATT, F32) + part_scratch(MLP, BF16) + [
            pltpu.VMEM((4, 4, rows, D), F32),
            pltpu.SemaphoreType.DMA((count,)),
            pltpu.SemaphoreType.DMA((count,)),
            pltpu.SemaphoreType.DMA((9,)),
            pltpu.SemaphoreType.DMA((9,)),
            pltpu.SemaphoreType.DMA((2,)),
        ],
        compiler_params=pltpu.CompilerParams(
            collective_id=2, has_side_effects=True, vmem_limit_bytes=VMEM_LIMIT),
        name="reduce_all",
    )(gatt, gmlp, small, mixed, gin)


def nt(a, b):
    return lax.dot_general(a, b, (((1,), (1,)), ((), ())), preferred_element_type=F32)


def nn(a, b):
    return lax.dot_general(a, b, (((1,), (0,)), ((), ())), preferred_element_type=F32)


def tn(a, b):
    return lax.dot_general(a, b, (((0,), (0,)), ((), ())), preferred_element_type=F32)


def normalize(values):
    centred = values - jnp.mean(values, axis=-1, keepdims=True)
    inverse = lax.rsqrt(jnp.mean(centred * centred, axis=-1, keepdims=True) + EPSILON)
    return centred * inverse, inverse


def norm_back(grad, normed, inverse, gain):
    scaled = grad * gain
    return inverse * (scaled - jnp.mean(scaled, axis=-1, keepdims=True)
                      - normed * jnp.mean(scaled * normed, axis=-1, keepdims=True))


def column_sum(values):
    return jnp.sum(values, axis=0, keepdims=True)


def mask_bias(doc_col, doc_row, valid_row):
    rows = lax.broadcasted_iota(jnp.int32, (SEG, SEG), 0)
    cols = lax.broadcasted_iota(jnp.int32, (SEG, SEG), 1)
    live = (valid_row == 1) | (rows == cols)
    return jnp.where((cols <= rows) & (doc_col == doc_row) & live, 0.0, NEG_FILL)


def gaussian(mem_scores, gauss):
    centre = jax.nn.sigmoid(jnp.sum(mem_scores * gauss[0:1], axis=-1, keepdims=True))
    width = jnp.sum(mem_scores * gauss[1:2], axis=-1, keepdims=True)
    softplus = jnp.maximum(width, 0.0) + jnp.log1p(jnp.exp(-jnp.abs(width)))
    variance = SIGMA_SCALE * softplus + (1.0 / N) ** 2
    places = (lax.broadcasted_iota(jnp.int32, (1, N), 1).astype(F32) + 0.5) / N
    offsets = centre - places
    inverse = 1.0 / variance
    density = (1.0 / N) * lax.rsqrt(variance) * jnp.exp(-0.5 * offsets * offsets * inverse)
    return centre, width, offsets, inverse, density


BLOCK = 256
BLOCKS = SEG // BLOCK


def forward_kernel(x, cot, watt, wmlp, coeffs, doc_col, doc_row, valid_row, ln_gain, ln_shift, bqv, gauss, b_out, b_fc,
                   b_proj, mixed, ghidden, qs, ks, vs, mks, mvs, lse, context, gmlp, sums, gfc_sum,
                   bias, n1, n2, hidden, acc, gn2, buf, sem):
    values, _ = normalize(x[...].astype(F32))
    n1[...] = (values * ln_gain[0:1] + ln_shift[0:1]).astype(BF16)
    bias[...] = mask_bias(doc_col[...], doc_row[...], valid_row[...])
    hidden[...] = x[...].astype(F32) + b_out[...]

    def heads(g, carry):
        q3 = (nt(n1[...], watt[g, 0:192]) + bqv[0, g]).astype(BF16)
        k3 = nt(n1[...], watt[g, 192:384]).astype(BF16)
        v3 = (nt(n1[...], watt[g, 384:576]) + bqv[1, g]).astype(BF16)
        mk3 = nt(coeffs[...], watt[g, 192:384]).astype(BF16)
        mv3 = nt(coeffs[...], watt[g, 384:576]).astype(BF16)
        for i in range(3):
            part = slice(i * HD, (i + 1) * HD)
            h = g * 3 + i
            qs[h], ks[h], vs[h] = q3[:, part], k3[:, part], v3[:, part]
            mks[h], mvs[h] = mk3[:, part], mv3[:, part]
        parts = []
        for i in range(3):
            h = g * 3 + i
            blocks = []
            for r in range(BLOCKS):
                rows, cols = slice(r * BLOCK, (r + 1) * BLOCK), slice(0, (r + 1) * BLOCK)
                q = qs[h, rows]
                scores = nt(q, ks[h, cols]) * SCORE_SCALE + bias[rows, cols]
                top = jnp.max(scores, axis=-1, keepdims=True)
                weights = jnp.exp(scores - top)
                total = jnp.sum(weights, axis=-1, keepdims=True)
                lse[h, rows] = top + jnp.log(total)
                probs = (weights * (1.0 / total)).astype(BF16)
                attended = nn(probs, vs[h, cols])
                mem_scores = nt(q, mks[h]) * SCORE_SCALE
                density = gaussian(mem_scores, gauss[h])[-1].astype(BF16)
                gate = (doc_col[rows] == doc_col[0:1]).astype(F32)
                blocks.append((attended + gate * nn(density, mvs[h])).astype(BF16))
            parts.append(jnp.concatenate(blocks, axis=0))
        context[g] = jnp.concatenate(parts, axis=1)
        hidden[...] += nn(context[g], watt[g, 576:768])
        return carry

    lax.fori_loop(0, 4, heads, 0)
    values, inverse = normalize(hidden[...])
    n2[...] = (values * ln_gain[1:2] + ln_shift[1:2]).astype(BF16)
    acc[...] = hidden[...] + b_proj[...]
    gn2[...] = jnp.zeros_like(gn2)

    def units(g, carry):
        slot = lax.rem(g, 2)
        pre = nn(n2[...], wmlp[g, 0:768]) + b_fc[g]
        inner = jnp.tanh(GELU_COEFF * (pre + 0.044715 * pre * pre * pre))
        activation = (0.5 * pre * (1.0 + inner)).astype(BF16)
        slope = 0.5 * (1.0 + inner) + (0.5 * GELU_COEFF) * pre * (1.0 - inner * inner) * (
            1.0 + 3.0 * 0.044715 * pre * pre)
        acc[...] += nn(activation, wmlp[g, 768:1536])
        gact = nt(cot[...], wmlp[g, 768:1536])
        gpre32 = gact * slope
        gpre = gpre32.astype(BF16)
        gfc_sum[g] = column_sum(gpre.astype(F32))
        gn2[...] += nt(gpre, wmlp[g, 0:768])

        @pl.when(g >= 2)
        def _():
            pltpu.make_async_copy(buf.at[slot], gmlp.at[g - 2], sem.at[slot]).wait()

        buf[slot, 0:768] = tn(n2[...], gpre)
        buf[slot, 768:1536] = tn(activation, cot[...])
        pltpu.make_async_copy(buf.at[slot], gmlp.at[g], sem.at[slot]).start()
        return carry

    lax.fori_loop(0, 4, units, 0)
    mixed[...] = acc[...].astype(BF16)
    values, inverse = normalize(hidden[...])
    grad = gn2[...]
    cotangent = cot[...].astype(F32)
    total = cotangent + norm_back(grad, values, inverse, ln_gain[1:2])
    ghidden[...] = total
    sums[0:1] = column_sum(grad * values)
    sums[1:2] = column_sum(grad)
    sums[2:3] = column_sum(total)
    sums[3:4] = column_sum(cotangent)
    pltpu.make_async_copy(buf.at[0], gmlp.at[2], sem.at[0]).wait()
    pltpu.make_async_copy(buf.at[1], gmlp.at[3], sem.at[1]).wait()


def backward_kernel(x, ghidden, watt, coeffs, doc_col, doc_row, valid_row, ln_gain, ln_shift, gauss, qs, ks, vs, mks, mvs, lse,
                    context, gin, gatt, sums, ggauss, gqv,
                    bias, n1, gbranch, gn1, gcs, dks, dvs, gmks, gmvs, buf, sem):
    values, inverse = normalize(x[...].astype(F32))
    n1[...] = (values * ln_gain[0:1] + ln_shift[0:1]).astype(BF16)
    bias[...] = mask_bias(doc_col[...], doc_row[...], valid_row[...])
    gbranch[...] = ghidden[...].astype(BF16)
    gn1[...] = jnp.zeros_like(gn1)

    def heads(g, carry):
        slot = lax.rem(g, 2)
        gc3 = nt(gbranch[...], watt[g, 576:768]).astype(BF16)
        for i in range(3):
            gcs[i] = gc3[:, i * HD:(i + 1) * HD]
        gqs, gks, gvs, gmk3, gmv3 = [], [], [], [], []
        for i in range(3):
            h = g * 3 + i
            blocks = []
            grad0 = jnp.zeros((1, N), F32)
            grad1 = jnp.zeros((1, N), F32)
            for r in range(BLOCKS):
                rows, cols = slice(r * BLOCK, (r + 1) * BLOCK), slice(0, (r + 1) * BLOCK)
                q, gc = qs[h, rows], gcs[i, rows]
                k, v = ks[h, cols], vs[h, cols]
                scores = nt(q, k) * SCORE_SCALE + bias[rows, cols]
                probs = jnp.exp(scores - lse[h, rows])
                gprobs = nt(gc, v)
                inner = jnp.sum(probs * gprobs, axis=-1, keepdims=True)
                gscores = (probs * (gprobs - inner)).astype(BF16)
                dv = tn(probs.astype(BF16), gc)
                dk = tn(gscores, q)
                if r == 0:
                    dvs[cols], dks[cols] = dv, dk
                else:
                    old = slice(0, r * BLOCK)
                    dvs[old] += dv[old]
                    dks[old] += dk[old]
                    dvs[rows], dks[rows] = dv[rows], dk[rows]
                dq = nn(gscores, k)
                gate = (doc_col[rows] == doc_col[0:1]).astype(F32)
                mem_scores = nt(q, mks[h]) * SCORE_SCALE
                centre, width, offsets, inv, density = gaussian(mem_scores, gauss[h])
                grec = (gc.astype(F32) * gate).astype(BF16)
                gdens = nt(grec, mvs[h]) * density
                ratio = offsets * inv
                gcentre = -jnp.sum(gdens * ratio, axis=-1, keepdims=True)
                gvar = 0.5 * jnp.sum(gdens * (ratio * ratio - inv), axis=-1, keepdims=True)
                gcl = gcentre * (centre * (1.0 - centre))
                gwl = gvar * (SIGMA_SCALE * jax.nn.sigmoid(width))
                grad0 = grad0 + column_sum(gcl * mem_scores)
                grad1 = grad1 + column_sum(gwl * mem_scores)
                gms = (gcl * gauss[h, 0:1] + gwl * gauss[h, 1:2]).astype(BF16)
                gmv = tn(density.astype(BF16), grec)
                gmk = tn(gms, q)
                if r == 0:
                    gmvs[...], gmks[...] = gmv, gmk
                else:
                    gmvs[...] += gmv
                    gmks[...] += gmk
                blocks.append(((dq + nn(gms, mks[h])) * SCORE_SCALE).astype(BF16))
            ggauss[h, 0:1] = grad0
            ggauss[h, 1:2] = grad1
            gqs.append(jnp.concatenate(blocks, axis=0))
            gks.append((dks[...] * SCORE_SCALE).astype(BF16))
            gvs.append(dvs[...].astype(BF16))
            gmk3.append((gmks[...] * SCORE_SCALE).astype(BF16))
            gmv3.append(gmvs[...].astype(BF16))

        @pl.when(g >= 2)
        def _():
            pltpu.make_async_copy(buf.at[slot], gatt.at[g - 2], sem.at[slot]).wait()

        gq3, gk3, gv3 = (jnp.concatenate(p, axis=1) for p in (gqs, gks, gvs))
        gmk_all, gmv_all = jnp.concatenate(gmk3, axis=1), jnp.concatenate(gmv3, axis=1)
        gqv[0, g] = column_sum(gq3.astype(F32))
        gqv[1, g] = column_sum(gv3.astype(F32))
        gn1[...] += nn(gq3, watt[g, 0:192]) + nn(gk3, watt[g, 192:384]) + nn(gv3, watt[g, 384:576])
        buf[slot, 0:192] = tn(gq3, n1[...])
        buf[slot, 192:384] = tn(gk3, n1[...]) + tn(gmk_all, coeffs[...])
        buf[slot, 384:576] = tn(gv3, n1[...]) + tn(gmv_all, coeffs[...])
        buf[slot, 576:768] = tn(context[g], gbranch[...])
        pltpu.make_async_copy(buf.at[slot], gatt.at[g], sem.at[slot]).start()
        return carry

    lax.fori_loop(0, 4, heads, 0)
    grad = gn1[...]
    values, inverse = normalize(x[...].astype(F32))
    gin[...] = ghidden[...] + norm_back(grad, values, inverse, ln_gain[0:1])
    sums[0:1] = column_sum(grad * values)
    sums[1:2] = column_sum(grad)
    pltpu.make_async_copy(buf.at[0], gatt.at[2], sem.at[0]).wait()
    pltpu.make_async_copy(buf.at[1], gatt.at[3], sem.at[1]).wait()


def layer(x, cot, watt, wmlp, coeffs, docs, valid, ln_gain, ln_shift, bqv, gauss, b_out, b_fc, b_proj):
    vmem, hbm = pl.BlockSpec(memory_space=pltpu.VMEM), pl.BlockSpec(memory_space=pl.ANY)
    doc_col, doc_row, valid_row = docs.reshape(SEG, 1), docs.reshape(1, SEG), valid.reshape(1, SEG)
    S = jax.ShapeDtypeStruct
    params = pltpu.CompilerParams(vmem_limit_bytes=VMEM_LIMIT)
    mixed, ghidden, qs, ks, vs, mks, mvs, lse, context, gmlp, sums2, gfc = pl.pallas_call(
        forward_kernel,
        out_shape=(S((SEG, D), BF16), S((SEG, D), F32), S((HEADS, SEG, HD), BF16), S((HEADS, SEG, HD), BF16),
                   S((HEADS, SEG, HD), BF16), S((HEADS, N, HD), BF16), S((HEADS, N, HD), BF16), S((HEADS, SEG, 1), F32),
                   S((4, SEG, 192), BF16), S((4, 1536, D), F32), S((4, D), F32), S((4, 1, D), F32)),
        in_specs=[vmem] * 15,
        out_specs=[vmem] * 9 + [hbm] + [vmem] * 2,
        scratch_shapes=[pltpu.VMEM((SEG, SEG), F32), pltpu.VMEM((SEG, D), BF16), pltpu.VMEM((SEG, D), BF16),
                        pltpu.VMEM((SEG, D), F32), pltpu.VMEM((SEG, D), F32), pltpu.VMEM((SEG, D), F32),
                        pltpu.VMEM((2, 1536, D), F32), pltpu.SemaphoreType.DMA((2,))],
        compiler_params=params,
        name="layer_forward",
    )(x, cot, watt, wmlp, coeffs, doc_col, doc_row, valid_row, ln_gain, ln_shift, bqv, gauss, b_out, b_fc, b_proj)
    gin, gatt, sums1, ggauss, gqv = pl.pallas_call(
        backward_kernel,
        out_shape=(S((SEG, D), F32), S((4, 768, D), F32), S((2, D), F32), S((HEADS, 2, N), F32), S((2, 4, 1, 192), F32)),
        in_specs=[vmem] * 17,
        out_specs=[vmem, hbm, vmem, vmem, vmem],
        scratch_shapes=[pltpu.VMEM((SEG, SEG), F32), pltpu.VMEM((SEG, D), BF16), pltpu.VMEM((SEG, D), BF16),
                        pltpu.VMEM((SEG, D), F32), pltpu.VMEM((3, SEG, HD), BF16), pltpu.VMEM((SEG, HD), F32),
                        pltpu.VMEM((SEG, HD), F32), pltpu.VMEM((N, HD), F32), pltpu.VMEM((N, HD), F32),
                        pltpu.VMEM((2, 768, D), F32), pltpu.SemaphoreType.DMA((2,))],
        compiler_params=params,
        name="layer_backward",
    )(x, ghidden, watt, coeffs, doc_col, doc_row, valid_row, ln_gain, ln_shift, gauss, qs, ks, vs, mks, mvs, lse, context)
    return mixed, gin, gmlp, gatt, sums1, sums2, ggauss, gqv, gfc

def shards(inputs, memory, doc_ids, key_valid, sticky_bins, ln_gain, ln_shift, w_qkv, b_qv, w_gauss, w_out, b_out,
           w_fc, b_fc, w_proj, b_proj, cotangent):
    head = lax.axis_index("head")
    patt = jnp.concatenate([w_qkv.transpose(0, 2, 1).reshape(576, D), w_out], axis=0).reshape(4, 4, 2, ATT, D)
    pmlp = jnp.concatenate([w_fc, w_proj], axis=0).reshape(4, 4, 2, MLP, D)
    small = jnp.concatenate(
        [b_qv.reshape(-1), jnp.zeros((384,), F32), w_gauss.reshape(-1), b_fc, jnp.zeros((4 * D,), F32)]
    ).reshape(8, D)
    watt, wmlp, mseg, sall = gather_weights(patt, pmlp, memory, small)
    sall = sall.reshape(4, 8 * D)
    bqv = sall[:, :384].reshape(4, 2, 1, 192).transpose(1, 0, 2, 3)
    gauss = sall[:, 768:2304].reshape(4, 2, 3, N).transpose(0, 2, 1, 3).reshape(HEADS, 2, N)
    bfc = sall[:, 2304:3072].reshape(4, 1, D)
    coeffs = ridge(sticky_bins[head][None], mseg.reshape(2 * HALF, D))
    mixed, gin, gmlp, gatt, sums1, sums2, ggauss, gqv, gfc = layer(
        inputs[head], cotangent[head], watt.reshape(4, ATT_ROWS, D), wmlp.reshape(4, MLP_ROWS, D), coeffs, doc_ids[head],
        key_valid[head], ln_gain, ln_shift, bqv, gauss, b_out[None], bfc, b_proj[None])
    small_grads = jnp.concatenate([
        sums1[0:1], sums2[0:1], sums1[1:2], sums2[1:4], gqv.transpose(1, 0, 2, 3).reshape(2, D),
        ggauss.reshape(4, 3, 2, N).transpose(0, 2, 1, 3).reshape(8, D), gfc.reshape(4, D), jnp.zeros((4, D), F32)])
    tatt, tmlp, small_total, mixed_all, gin_all = reduce_all(
        gatt.reshape(2, 2, 4, 4, 2, ATT, D), gmlp.reshape(2, 2, 4, 4, 2, MLP, D), small_grads, mixed, gin)
    tatt = tatt.reshape(ATT_ROWS, D)
    tmlp = tmlp.reshape(MLP_ROWS, D).astype(F32)
    g_bqv = lax.dynamic_slice_in_dim(small_total[6:8].reshape(4, 2, 192), head, 1, 0)[0]
    g_gauss = lax.dynamic_slice_in_dim(small_total[8:16].reshape(4, 2, 3, N), head, 1, 0)[0]
    g_bfc = lax.dynamic_slice_in_dim(small_total[16:20], head, 1, 0)[0]
    return (
        mixed_all,
        gin_all,
        small_total[0:2],
        small_total[2:4],
        tatt[:576].reshape(3, 192, D).transpose(0, 2, 1),
        g_bqv,
        g_gauss,
        tatt[576:],
        small_total[4],
        tmlp[:768],
        g_bfc,
        tmlp[768:],
        small_total[5],
    )


def solution(mesh):
    return jax.shard_map(
        shards,
        mesh=mesh,
        in_specs=(
            P("dp", None, None),
            P("dp", "head", None),
            P("dp", None),
            P("dp", None),
            P("dp", None),
            P(),
            P(),
            P(None, None, "head"),
            P(None, "head"),
            P(None, "head", None),
            P("head", None),
            P(),
            P(None, "head"),
            P("head"),
            P("head", None),
            P(),
            P("dp", None, None),
        ),
        out_specs=(
            P("dp", None, None),
            P("dp", None, None),
            P(),
            P(),
            P(None, None, "head"),
            P(None, "head"),
            P(None, "head", None),
            P("head", None),
            P(),
            P(None, "head"),
            P("head"),
            P("head", None),
            P(),
        ),
        check_vma=False,
    )
```

```python
from functools import partial

import jax
import jax.numpy as jnp
from jax import lax
from jax.experimental import pallas as pl
from jax.experimental.pallas import tpu as pltpu
from jax.sharding import PartitionSpec as P

MESH = pl.DeviceIdType.MESH
BF16, F32 = jnp.bfloat16, jnp.float32
D, N, HEADS, HD, FF, SEG, HALF = 768, 256, 12, 64, 3072, 512, 256
PARTS, ROWS, LANES = 3, 16, 384
EPSILON = 1e-05
RIDGE_WEIGHT = 0.5
SIGMA_SCALE = 0.01
SCORE_SCALE = 0.125
NEG_FILL = -1e30
GELU_COEFF = 0.7978845608028654
PRECISE = lax.Precision.HIGHEST
VMEM_LIMIT = 60 * 1024 * 1024
BLOCK = 256
CHUNK = 128
BLOCKS = SEG // BLOCK


class Place:
    def __init__(self):
        dp, head = lax.axis_index("dp"), lax.axis_index("head")
        self.head = head
        self.yl = lax.div(dp, 16)
        self.z = lax.rem(lax.div(dp, 4), 4)
        self.x = lax.rem(dp, 4)
        self.yh = lax.div(head, 2)
        self.c = lax.rem(head, 2)
        self.y = self.yh * 2 + self.yl

    def at(self, x=None, z=None, y=None, c=None):
        x = self.x if x is None else x
        z = self.z if z is None else z
        c = self.c if c is None else c
        if y is None:
            yl, yh = self.yl, self.yh
        else:
            yl, yh = lax.rem(y, 2), lax.div(y, 2)
        return (yl * 16 + z * 4 + x, yh * 2 + c)

    def core(self):
        return self.at(c=1 - self.c)

    def ring(self, along_x, k):
        return self.at(x=step(self.x, k)) if along_x else self.at(z=step(self.z, k))


def step(place, by):
    return lax.rem(place + by, 4)


def lanes(half):
    return pl.ds(half * LANES, LANES)


def greet(devices):
    sem = pltpu.get_barrier_semaphore()
    for device in devices:
        pl.semaphore_signal(sem, inc=1, device_id=device, device_id_type=MESH)


def met(devices):
    pl.semaphore_wait(pltpu.get_barrier_semaphore(), len(devices))


class Links:
    def __init__(self, send, recv):
        self.send, self.recv, self.used, self.all = send, recv, 0, []

    def add(self, src, dst, device, arrives):
        link = Link(self, self.used, src, dst, device, arrives)
        self.used += 1
        self.all.append(link)
        return link

    def finish(self):
        for link in self.all:
            if not link.done:
                link.sent()


class Link:
    def __init__(self, links, index, src, dst, device, arrives):
        self.links, self.index, self.done = links, index, False
        self.src, self.dst, self.device, self.arrives = src, dst, device, arrives

    def copy(self, dst):
        return pltpu.make_async_remote_copy(
            src_ref=self.src(), dst_ref=dst, send_sem=self.links.send.at[self.index],
            recv_sem=self.links.recv.at[self.index], device_id=self.device(), device_id_type=MESH)

    def start(self):
        self.copy(self.dst()).start()

    def wait(self):
        self.copy(self.arrives()).wait_recv()

    def sent(self):
        self.copy(self.dst()).wait_send()


class PlaneGather:
    def __init__(self, links, me, view, row, column):
        self.one, self.two = [[], []], [[], []]
        for k in (1, 3, 2):
            back = 4 - k
            self.one[0].append(links.add(
                lambda: view(me.z, me.x, 0), lambda: view(me.z, me.x, 0), lambda k=k: me.ring(True, k),
                lambda back=back: view(me.z, step(me.x, back), 0)))
            self.one[1].append(links.add(
                lambda: view(me.z, me.x, 1), lambda: view(me.z, me.x, 1), lambda k=k: me.ring(False, k),
                lambda back=back: view(step(me.z, back), me.x, 1)))
            self.two[0].append(links.add(
                lambda: row(me.z, 0), lambda: row(me.z, 0), lambda k=k: me.ring(False, k),
                lambda back=back: row(step(me.z, back), 0)))
            self.two[1].append(links.add(
                lambda: column(me.x, 1), lambda: column(me.x, 1), lambda k=k: me.ring(True, k),
                lambda back=back: column(step(me.x, back), 1)))

    def first(self):
        for a, b in zip(*self.one):
            a.start()
            b.start()

    def second(self):
        for half in (0, 1):
            for link in self.one[half]:
                link.wait()
            for link in self.two[half]:
                link.start()

    def finish(self):
        for a, b in zip(*self.two):
            a.wait()
            b.wait()


def nt(a, b):
    return lax.dot_general(a, b, (((1,), (1,)), ((), ())), preferred_element_type=F32)


def nn(a, b):
    return lax.dot_general(a, b, (((1,), (0,)), ((), ())), preferred_element_type=F32)


def tn(a, b):
    return lax.dot_general(a, b, (((0,), (0,)), ((), ())), preferred_element_type=F32)


def normalize(values):
    centred = values - jnp.mean(values, axis=-1, keepdims=True)
    inverse = lax.rsqrt(jnp.mean(centred * centred, axis=-1, keepdims=True) + EPSILON)
    return centred * inverse, inverse


def norm_back(grad, normed, inverse, gain):
    scaled = grad * gain
    return inverse * (scaled - jnp.mean(scaled, axis=-1, keepdims=True)
                      - normed * jnp.mean(scaled * normed, axis=-1, keepdims=True))


def column_sum(values):
    return jnp.sum(values, axis=0, keepdims=True)


def mask_bias(doc_col, doc_row, valid_row):
    rows = lax.broadcasted_iota(jnp.int32, (SEG, SEG), 0)
    cols = lax.broadcasted_iota(jnp.int32, (SEG, SEG), 1)
    live = (valid_row == 1) | (rows == cols)
    return jnp.where((cols <= rows) & (doc_col == doc_row) & live, 0.0, NEG_FILL)


def gaussian(mem_scores, gauss):
    centre = jax.nn.sigmoid(jnp.sum(mem_scores * gauss[0:1], axis=-1, keepdims=True))
    width = jnp.sum(mem_scores * gauss[1:2], axis=-1, keepdims=True)
    softplus = jnp.maximum(width, 0.0) + jnp.log1p(jnp.exp(-jnp.abs(width)))
    variance = SIGMA_SCALE * softplus + (1.0 / N) ** 2
    places = (lax.broadcasted_iota(jnp.int32, (1, N), 1).astype(F32) + 0.5) / N
    offsets = centre - places
    inverse = 1.0 / variance
    density = (1.0 / N) * lax.rsqrt(variance) * jnp.exp(-0.5 * offsets * offsets * inverse)
    return centre, width, offsets, inverse, density


def ridge_steps():
    low, high = RIDGE_WEIGHT, 650.0
    gap = (high - low) / (high + low)
    scales = []
    while gap > 1e-9:
        square = gap * gap
        scale = 2.0 / (2.0 - square) if square > 1e-3 else 1.0
        gap = square / (2.0 - square) if square > 1e-3 else square
        scales.append(scale)
    return 2.0 / (low + high), scales


def attend_kernel(patt, pmlp, memory, small, bins, x, doc_col, doc_row, valid_row, ln_gain, ln_shift, b_out,
                  watt_out, wmlp, sall_out, coeffs, hidden, qs, ks, vs, mks, mvs, lse, context,
                  watt, mseg, sall, bias, n1, hq, hk, hv, send, recv, local):
    me = Place()
    peers = ([me.core(), me.at(y=3 - me.y), me.at(y=step(me.y, 2)), me.at(y=step(me.y, 2), c=1 - me.c)]
             + [me.ring(True, k) for k in (1, 2, 3)] + [me.ring(False, k) for k in (1, 2, 3)])
    greet(peers)
    values, _ = normalize(x[...].astype(F32))
    n1[...] = (values * ln_gain[0:1] + ln_shift[0:1]).astype(BF16)
    hidden[...] = x[...].astype(F32) + b_out[...]
    met(peers)

    links = Links(send, recv)
    walls = (watt, wmlp)
    packs = (patt, pmlp)
    across, own, gathers, forwards = [], [], [], []
    for pack, wall in zip(packs, walls):
        across.append(links.add(
            lambda pack=pack: pack.at[..., me.z, me.x, :, :],
            lambda wall=wall: wall.at[me.yh, me.c].at[..., me.z, me.x, :, :],
            lambda: me.at(y=3 - me.y),
            lambda wall=wall: wall.at[1 - me.yh, me.c].at[..., me.z, me.x, :, :]))
        own.append(links.add(
            lambda pack=pack: pack, lambda wall=wall: wall.at[me.yh, me.c], me.core,
            lambda wall=wall: wall.at[me.yh, 1 - me.c]))

        def view(z, x, half, c=None, wall=wall):
            return wall.at[1 - me.yh, me.c if c is None else c].at[..., z, x, :, lanes(half)]

        def row(z, half, c=None, wall=wall):
            return wall.at[1 - me.yh, me.c if c is None else c].at[..., z, :, :, lanes(half)]

        def column(x, half, c=None, wall=wall):
            return wall.at[1 - me.yh, me.c if c is None else c].at[..., :, x, :, lanes(half)]

        gathers.append(PlaneGather(links, me, view, row, column))
        passed = []
        for k in (0, 1, 3, 2):
            passed.append(links.add(
                lambda k=k, row=row: row(step(me.z, k), 0), lambda k=k, row=row: row(step(me.z, k), 0), me.core,
                lambda k=k, row=row: row(step(me.z, k), 0, 1 - me.c)))
            passed.append(links.add(
                lambda k=k, column=column: column(step(me.x, k), 1),
                lambda k=k, column=column: column(step(me.x, k), 1), me.core,
                lambda k=k, column=column: column(step(me.x, k), 1, 1 - me.c)))
        forwards.append(passed)
    sent, sent_small = [], []
    for k in (1, 2, 3):
        def other(k=k):
            return lax.rem(me.head + k, 4)

        def device(k=k):
            return (me.yl * 16 + me.z * 4 + me.x, lax.rem(me.head + k, 4))

        def before(k=k):
            return lax.rem(me.head + (4 - k), 4)

        sent.append(links.add(lambda other=other: memory.at[other()], lambda: mseg.at[me.head], device,
                              lambda before=before: mseg.at[before()]))
        sent_small.append(links.add(lambda: small, lambda: sall.at[me.head], device,
                                    lambda before=before: sall.at[before()]))
    across[0].start()
    for link in sent:
        link.start()
    own[0].start()
    for link in sent_small:
        link.start()
    across[1].start()
    own[1].start()
    kept = [pltpu.make_async_copy(patt, watt.at[me.yh, me.c], local.at[0]),
            pltpu.make_async_copy(memory.at[me.head], mseg.at[me.head], local.at[1]),
            pltpu.make_async_copy(small, sall.at[me.head], local.at[2]),
            pltpu.make_async_copy(pmlp, wmlp.at[me.yh, me.c], local.at[3])]
    for copy in kept:
        copy.start()

    dot = partial(jnp.dot, preferred_element_type=F32, precision=PRECISE)
    rows = lax.broadcasted_iota(jnp.int32, (N, N), 0)
    cols = lax.broadcasted_iota(jnp.int32, (N, N), 1)
    gap = (rows - cols).astype(F32)
    curve = jnp.exp(-0.5 * gap * gap)
    eye = (rows == cols).astype(F32)
    picked = (bins[...] == rows).astype(F32)
    counts = 1.0 + jnp.sum(picked, axis=1, keepdims=True)
    gram = dot(curve, counts * curve) + RIDGE_WEIGHT * eye
    start, scales = ridge_steps()
    inverse = scales[0] * (2.0 * start * eye - (start * start) * gram)
    across[0].wait()
    gathers[0].first()
    for scale in scales[1:4]:
        inverse = scale * (2.0 * inverse - dot(inverse, dot(gram, inverse)))
    gathers[0].second()
    forwards[0][0].start()
    forwards[0][1].start()
    across[1].wait()
    gathers[1].first()
    for scale in scales[4:]:
        inverse = scale * (2.0 * inverse - dot(inverse, dot(gram, inverse)))
    gathers[0].finish()
    for link in forwards[0][2:]:
        link.start()
    bias[...] = mask_bias(doc_col[...], doc_row[...], valid_row[...])
    kept[1].wait()
    for link in sent:
        link.wait()
    first_half = mseg[0:2].reshape(HALF, D).astype(F32)
    held = first_half + jnp.dot(picked.astype(BF16), mseg[2:4].reshape(HALF, D), preferred_element_type=F32)
    coeffs[...] = dot(inverse, dot(curve, held)).astype(BF16)
    gathers[1].second()
    forwards[1][0].start()
    forwards[1][1].start()
    kept[0].wait()
    kept[2].wait()
    own[0].wait()
    for link in forwards[0]:
        link.wait()
    for link in sent_small:
        link.wait()
    out = [pltpu.make_async_copy(watt, watt_out, local.at[4]), pltpu.make_async_copy(sall, sall_out, local.at[5])]
    for copy in out:
        copy.start()

    def group(i, carry):
        def weight(kind):
            return watt[:, :, i, kind].reshape(4 * HD, D)

        def heads_row(r):
            return jnp.concatenate([sall[g, i, r:r + 1, 0:HD] for g in range(4)], axis=1)

        q4 = (nt(n1[...], weight(0)) + heads_row(0)).astype(BF16)
        k4 = nt(n1[...], weight(1)).astype(BF16)
        v4 = (nt(n1[...], weight(2)) + heads_row(1)).astype(BF16)
        mk4 = nt(coeffs[...], weight(1)).astype(BF16)
        mv4 = nt(coeffs[...], weight(2)).astype(BF16)
        qs[i], ks[i], vs[i], mks[i], mvs[i] = q4, k4, v4, mk4, mv4
        for g in range(4):
            part = slice(g * HD, (g + 1) * HD)
            hq[g], hk[g], hv[g] = q4[:, part], k4[:, part], v4[:, part]
        parts = []
        for g in range(4):
            part = slice(g * HD, (g + 1) * HD)
            mk, mv = mk4[:, part], mv4[:, part]
            blocks = []
            for r in range(BLOCKS):
                rows, cols = slice(r * BLOCK, (r + 1) * BLOCK), slice(0, (r + 1) * BLOCK)
                q = hq[g, rows]
                scores = nt(q, hk[g, cols]) * SCORE_SCALE + bias[rows, cols]
                top = jnp.max(scores, axis=-1, keepdims=True)
                weights = jnp.exp(scores - top)
                total = jnp.sum(weights, axis=-1, keepdims=True)
                lse[i, rows, g:g + 1] = top + jnp.log(total)
                probs = (weights * (1.0 / total)).astype(BF16)
                attended = nn(probs, hv[g, cols])
                mem_scores = nt(q, mk) * SCORE_SCALE
                density = gaussian(mem_scores, sall[g, i, 2:4])[-1].astype(BF16)
                gate = (doc_col[rows] == doc_col[0:1]).astype(F32)
                blocks.append((attended + gate * nn(density, mv)).astype(BF16))
            parts.append(jnp.concatenate(blocks, axis=0))
        mixed = jnp.concatenate(parts, axis=1)
        context[i] = mixed
        hidden[...] += nn(mixed, weight(3))

        @pl.when(i == 1)
        def _():
            gathers[1].finish()
            for link in forwards[1][2:]:
                link.start()

        return carry

    lax.fori_loop(0, PARTS, group, 0)
    own[1].wait()
    for link in forwards[1]:
        link.wait()
    kept[3].wait()
    for copy in out:
        copy.wait()
    links.finish()


class Sums:
    def __init__(self, links, me, kinds, other, sbuf, rbuf, kept, credit):
        self.links, self.me, self.kinds = links, me, kinds
        self.other, self.sbuf, self.rbuf, self.kept, self.credit = other, sbuf, rbuf, kept, credit
        self.base = links.used
        links.used += PARTS * 7

    def swap(self, part, src):
        return Link(self.links, self.base + part, src, lambda: self.other, self.me.core, lambda: self.other)

    def send(self, part, half, k):
        i = half * 3 + k - 1
        return Link(self.links, self.base + PARTS + part * 6 + i, lambda: self.sbuf.at[part, i],
                    lambda: self.rbuf.at[part, i], lambda: self.me.ring(half == 0, k), lambda: self.rbuf.at[part, i])

    def first(self, part, own):
        me = self.me
        self.swap(part, lambda: self.other).wait()
        for k in (2, 1, 3, 0):
            for half in (0, 1):
                def body(i, carry, half=half, k=k):
                    t, kind = lax.div(i, self.kinds), lax.rem(i, self.kinds)
                    for q in range(4):
                        z, x = (q, step(me.x, k)) if half == 0 else (step(me.z, k), q)
                        cut = slice(half * LANES, (half + 1) * LANES)
                        value = own(t, kind, z, x, cut) + self.other[t, kind, z, x, :, cut]
                        if k == 0:
                            self.kept[part, half, t, kind, q] = value
                        else:
                            self.sbuf[part, half * 3 + k - 1, t, kind, q] = value.astype(BF16)
                    return carry

                lax.fori_loop(0, 2 * self.kinds, body, 0)
                if k:
                    self.send(part, half, k).start()
        pl.semaphore_signal(self.credit, inc=1, device_id=me.core(), device_id_type=MESH)


class Tail:
    def __init__(self, links, me, sums, low, high, total, rbuf2, ylocal, ybuf, final, local):
        self.me, self.sums, self.low, self.high, self.total = me, sums, low, high, total
        self.rbuf2, self.ylocal, self.ybuf, self.final, self.local = rbuf2, ylocal, ybuf, final, local
        kept = sums.kept
        self.two = {}
        for half in (0, 1):
            across = (lambda: me.z) if half == 0 else (lambda: me.x)
            for k in (2, 1, 3):
                i = half * 3 + k - 1
                self.two[half, k] = links.add(
                    lambda half=half, k=k, across=across: kept.at[low:high, half, :, :, step(across(), k)],
                    lambda i=i: rbuf2.at[i], lambda half=half, k=k: me.ring(half == 1, k), lambda i=i: rbuf2.at[i])
        self.three = []
        for k in (2, 1, 3):
            def target(k=k):
                return step(me.y, k)

            self.three.append(links.add(
                lambda target=target: ylocal.at[lax.div(target(), 2), lax.rem(target(), 2)],
                lambda k=k: ybuf.at[k - 1], lambda target=target: me.at(y=target()), lambda k=k: ybuf.at[k - 1]))

        def view(z, x, half):
            return total.at[low:high, :, z, x, :, lanes(half)]

        def row(z, half):
            return total.at[low:high, :, z, :, :, lanes(half)]

        def column(x, half):
            return total.at[low:high, :, :, x, :, lanes(half)]

        self.view = view
        self.mate = links.add(lambda: final, lambda: view(me.z, me.x, me.yl),
                              lambda: me.at(y=me.yh * 2 + 1 - me.yl), lambda: view(me.z, me.x, 1 - me.yl))
        self.gather = PlaneGather(links, me, view, row, column)

    def second(self):
        sums, kept = self.sums, self.sums.kept
        for half in (0, 1):
            for part in range(self.low, self.high):
                for k in (1, 2, 3):
                    sums.send(part, half, k).wait()

                def body(i, carry, half=half, part=part):
                    t, kind = lax.div(i, sums.kinds), lax.rem(i, sums.kinds)
                    value = kept[part, half, t, kind]
                    for k in (1, 2, 3):
                        value = value + sums.rbuf[part, half * 3 + k - 1, t, kind].astype(F32)
                    kept[part, half, t, kind] = value
                    return carry

                lax.fori_loop(0, 2 * sums.kinds, body, 0)
            for k in (2, 1, 3):
                self.two[half, k].start()

    def third(self):
        me, kept = self.me, self.sums.kept
        for half in (0, 1):
            for k in (1, 2, 3):
                self.two[half, k].wait()
            across = me.z if half == 0 else me.x
            for p in range(self.low, self.high):
                for t in (0, 1):
                    value = kept[p, half, t, :, across]
                    for k in (1, 2, 3):
                        value = value + self.rbuf2[half * 3 + k - 1, p - self.low, t]
                    self.ylocal[t, half, p - self.low] = value
        for link in self.three:
            link.start()

    def keep(self):
        return pltpu.make_async_copy(self.final, self.view(self.me.z, self.me.x, self.me.yl), self.local)

    def fourth(self):
        me = self.me
        for link in self.three:
            link.wait()
        self.final[...] = (self.ylocal[me.yh, me.yl] + self.ybuf[0] + self.ybuf[1] + self.ybuf[2]).astype(
            self.final.dtype)
        self.keep().start()
        self.mate.start()

    def fifth(self):
        self.keep().wait()
        self.mate.wait()
        self.gather.first()

    def sixth(self):
        self.gather.second()

    def finish(self):
        self.gather.finish()


def backward_kernel(x, cot, hidden_in, watt, wmlp, coeffs, sall, doc_col, doc_row, valid_row, ln_gain, ln_shift, b_proj,
                    qs, ks, vs, mks, mvs, lse, context,
                    tatt, tmlp, small_total, mixed_all, gin_all,
                    wbuf, gbuf, hidden, acc, gnorm, n12, gbranch, mixed, bias, hq, hk, hv, gcs, dks, dvs, gmks, gmvs,
                    otherm, sbufm, rbufm, keptm, othera, sbufa, rbufa, kepta,
                    r2m, ylm, ybm, finm, r2a, yla, yba, fina, r2b, ylb, ybb, finb,
                    small, slots, send, recv, creditm, credita, local):
    me = Place()
    peers = ([me.core()] + [me.ring(True, k) for k in (1, 2, 3)] + [me.ring(False, k) for k in (1, 2, 3)]
             + [me.at(y=step(me.y, k)) for k in (1, 2, 3)])
    greet(peers)
    links = Links(send, recv)
    mlp = Sums(links, me, 2, otherm, sbufm, rbufm, keptm, creditm)
    att = Sums(links, me, 1, othera, sbufa, rbufa, kepta, credita)
    tail_m = Tail(links, me, mlp, 0, 3, tmlp, r2m, ylm, ybm, finm, local.at[4])
    tail_a = Tail(links, me, att, 0, 2, tatt, r2a, yla, yba, fina, local.at[5])
    tail_b = Tail(links, me, att, 2, 3, tatt, r2b, ylb, ybb, finb, local.at[6])

    def load(index, slot):
        part, mine = lax.div(index, 2), lax.rem(index, 2)
        owner = mine * me.c + (1 - mine) * (1 - me.c)
        return pltpu.make_async_copy(wmlp.at[:, owner, part], wbuf.at[slot], local.at[slot])

    def load_att(part, slot):
        return pltpu.make_async_copy(watt.at[:, :, part], wbuf.at[slot], local.at[slot])

    load_hidden = pltpu.make_async_copy(hidden_in, hidden, local.at[7])
    load_hidden.start()
    load(0, 0).start()
    load(1, 1).start()
    load_hidden.wait()

    def start_mlp(i, carry):
        rows = pl.ds(i * CHUNK, CHUNK)
        values, _ = normalize(hidden[rows])
        n12[rows] = (values * ln_gain[1:2] + ln_shift[1:2]).astype(BF16)
        acc[rows] = hidden[rows] + b_proj[...]
        return carry

    lax.fori_loop(0, SEG // CHUNK, start_mlp, 0)
    gnorm[...] = jnp.zeros_like(gnorm)
    small[...] = jnp.zeros_like(small)
    met(peers)

    def own_mlp(t, kind, z, xx, cut):
        return gbuf[1, t, kind, z, xx, :, cut]

    def swap_mlp(part):
        return mlp.swap(part, lambda: gbuf.at[0])

    def units(index, carry):
        part, mine = lax.div(index, 2), lax.rem(index, 2)
        owner = mine * me.c + (1 - mine) * (1 - me.c)
        load(index, mine).wait()

        @pl.when((mine == 0) & (part > 0))
        def _():
            mlp.first(part - 1, own_mlp)
            swap_mlp(part - 1).sent()

        wfc = wbuf[mine, :, 0].reshape(512, D)
        wproj = wbuf[mine, :, 1].reshape(512, D)
        bias_fc = jnp.concatenate([sall[owner, part, 4:5], sall[2 + owner, part, 4:5]], axis=1)
        pre = nt(n12[...], wfc) + bias_fc
        inner = jnp.tanh(GELU_COEFF * (pre + 0.044715 * pre * pre * pre))
        activation = (0.5 * pre * (1.0 + inner)).astype(BF16)
        slope = 0.5 * (1.0 + inner) + (0.5 * GELU_COEFF) * pre * (1.0 - inner * inner) * (
            1.0 + 3.0 * 0.044715 * pre * pre)
        acc[...] += nn(activation, wproj)
        gpre = (nt(cot[...], wproj) * slope).astype(BF16)
        units_sum = column_sum(gpre.astype(F32))
        small[part, pl.ds(16 + owner, 1)] = units_sum[:, 0:256]
        small[part, pl.ds(18 + owner, 1)] = units_sum[:, 256:512]
        gnorm[...] += nn(gpre, wfc)
        gbuf[mine, :, 0] = tn(gpre, n12[...]).reshape(2, 4, 4, ROWS, D)
        gbuf[mine, :, 1] = tn(activation, cot[...]).reshape(2, 4, 4, ROWS, D)

        @pl.when(mine == 0)
        def _():
            @pl.when(part > 0)
            def _():
                pl.semaphore_wait(creditm, 1)

            swap_mlp(part).start()

        @pl.when(index < 4)
        def _():
            load(index + 2, mine).start()

        return carry

    lax.fori_loop(0, 6, units, 0)
    load_att(0, 0).start()
    load_att(1, 1).start()
    mlp.first(2, own_mlp)
    swap_mlp(2).sent()
    mixed[...] = acc[...].astype(BF16)
    far_head = (1 - me.yh) * 2 + me.c
    mate, far_mate = me.yh * 2 + 1 - me.c, (1 - me.yh) * 2 + 1 - me.c

    def spread(block, everywhere, slot):
        keep = pltpu.make_async_copy(block, everywhere.at[me.head], local.at[slot])
        far = links.add(lambda: block, lambda: everywhere.at[me.head], lambda: me.at(y=step(me.y, 2)),
                        lambda: everywhere.at[far_head])
        near = links.add(lambda: block, lambda: everywhere.at[me.head], me.core, lambda: everywhere.at[mate])
        passed = links.add(lambda: everywhere.at[far_head], lambda: everywhere.at[far_head], me.core,
                           lambda: everywhere.at[far_mate])
        return keep, far, near, passed

    mixed_moves = spread(mixed, mixed_all, 2)
    for move in mixed_moves[:3]:
        move.start()

    def put(row, vector):
        for i in range(3):
            small[i, row:row + 1] += vector[:, i * 256:(i + 1) * 256]

    def norm_two(i, carry):
        rows = pl.ds(i * CHUNK, CHUNK)
        values, inverse = normalize(hidden[rows])
        grad = gnorm[rows]
        cotangent = cot[rows].astype(F32)
        total = cotangent + norm_back(grad, values, inverse, ln_gain[1:2])
        hidden[rows] = total
        gbranch[rows] = total.astype(BF16)
        put(1, column_sum(grad * values))
        put(3, column_sum(grad))
        put(4, column_sum(total))
        put(5, column_sum(cotangent))
        values, _ = normalize(x[rows].astype(F32))
        n12[rows] = (values * ln_gain[0:1] + ln_shift[0:1]).astype(BF16)
        return carry

    lax.fori_loop(0, SEG // CHUNK, norm_two, 0)
    bias[...] = mask_bias(doc_col[...], doc_row[...], valid_row[...])
    acc[...] = jnp.zeros_like(acc)

    def own_att(part):
        slot = lax.rem(part, 2)
        return lambda t, kind, z, xx, cut: gbuf[slot, t, me.c, z, xx, :, cut]

    def swap_att(part):
        slot = lax.rem(part, 2)
        return att.swap(part, lambda: gbuf.at[slot, :, pl.ds(1 - me.c, 1)])

    def group(i, carry):
        slot = lax.rem(i, 2)
        load_att(i, slot).wait()

        def weight(kind):
            return wbuf[slot, :, :, kind].reshape(4 * HD, D)

        q4, k4, v4, mk4, mv4 = qs[i], ks[i], vs[i], mks[i], mvs[i]
        gc4 = nt(gbranch[...], weight(3)).astype(BF16)
        for g in range(4):
            part = slice(g * HD, (g + 1) * HD)
            hq[g], hk[g], hv[g], gcs[g] = q4[:, part], k4[:, part], v4[:, part], gc4[:, part]

        @pl.when(i > 0)
        def _():
            att.first(i - 1, own_att(i - 1))

        gqs, gks, gvs, gmk_all, gmv_all = [], [], [], [], []
        for g in range(4):
            part = slice(g * HD, (g + 1) * HD)
            mk, mv = mk4[:, part], mv4[:, part]
            gauss = sall[g, i, 2:4]
            blocks = []
            grad0 = jnp.zeros((1, N), F32)
            grad1 = jnp.zeros((1, N), F32)
            for r in range(BLOCKS):
                rows, cols = slice(r * BLOCK, (r + 1) * BLOCK), slice(0, (r + 1) * BLOCK)
                q, gc = hq[g, rows], gcs[g, rows]
                k, v = hk[g, cols], hv[g, cols]
                scores = nt(q, k) * SCORE_SCALE + bias[rows, cols]
                probs = jnp.exp(scores - lse[i, rows, g:g + 1])
                gprobs = nt(gc, v)
                inner = jnp.sum(probs * gprobs, axis=-1, keepdims=True)
                gscores = (probs * (gprobs - inner)).astype(BF16)
                dv = tn(probs.astype(BF16), gc)
                dk = tn(gscores, q)
                if r == 0:
                    dvs[cols], dks[cols] = dv, dk
                else:
                    old = slice(0, r * BLOCK)
                    dvs[old] += dv[old]
                    dks[old] += dk[old]
                    dvs[rows], dks[rows] = dv[rows], dk[rows]
                dq = nn(gscores, k)
                gate = (doc_col[rows] == doc_col[0:1]).astype(F32)
                mem_scores = nt(q, mk) * SCORE_SCALE
                centre, width, offsets, inv, density = gaussian(mem_scores, gauss)
                grec = (gc.astype(F32) * gate).astype(BF16)
                gdens = nt(grec, mv) * density
                ratio = offsets * inv
                gcentre = -jnp.sum(gdens * ratio, axis=-1, keepdims=True)
                gvar = 0.5 * jnp.sum(gdens * (ratio * ratio - inv), axis=-1, keepdims=True)
                gcl = gcentre * (centre * (1.0 - centre))
                gwl = gvar * (SIGMA_SCALE * jax.nn.sigmoid(width))
                grad0 = grad0 + column_sum(gcl * mem_scores)
                grad1 = grad1 + column_sum(gwl * mem_scores)
                gms = (gcl * gauss[0:1] + gwl * gauss[1:2]).astype(BF16)
                gmv = tn(density.astype(BF16), grec)
                gmk = tn(gms, q)
                if r == 0:
                    gmvs[...], gmks[...] = gmv, gmk
                else:
                    gmvs[...] += gmv
                    gmks[...] += gmk
                blocks.append(((dq + nn(gms, mk)) * SCORE_SCALE).astype(BF16))
            small[i, 8 + 2 * g:9 + 2 * g] = grad0
            small[i, 9 + 2 * g:10 + 2 * g] = grad1
            gqs.append(jnp.concatenate(blocks, axis=0))
            gks.append((dks[...] * SCORE_SCALE).astype(BF16))
            gvs.append(dvs[...].astype(BF16))
            gmk_all.append((gmks[...] * SCORE_SCALE).astype(BF16))
            gmv_all.append(gmvs[...].astype(BF16))
            if g == 0:
                @pl.when(i == 2)
                def _():
                    tail_m.third()
            if g == 1:
                @pl.when(i == 1)
                def _():
                    tail_m.second()

                @pl.when(i == 2)
                def _():
                    tail_m.fourth()
            if g == 2:
                @pl.when(i == 2)
                def _():
                    tail_m.fifth()
                    tail_a.second()

        gq4, gk4, gv4, gmk4, gmv4 = (jnp.concatenate(p, axis=1) for p in (gqs, gks, gvs, gmk_all, gmv_all))

        @pl.when(i == 2)
        def _():
            swap_att(0).sent()

        def store(kind, value):
            gbuf[slot, :, :, kind] = value.reshape(2, 2, 4, ROWS, D)

        store(0, tn(gq4, n12[...]))
        store(1, tn(gk4, n12[...]) + tn(gmk4, coeffs[...]))
        store(2, tn(gv4, n12[...]) + tn(gmv4, coeffs[...]))
        store(3, tn(context[i], gbranch[...]))

        @pl.when(i > 0)
        def _():
            pl.semaphore_wait(credita, 1)

        swap_att(i).start()
        small[i, 6:7] = column_sum(gq4.astype(F32))
        small[i, 7:8] = column_sum(gv4.astype(F32))
        acc[...] += nn(gq4, weight(0)) + nn(gk4, weight(1)) + nn(gv4, weight(2))

        @pl.when(i == 0)
        def _():
            load_att(2, 0).start()

        return carry

    lax.fori_loop(0, PARTS, group, 0)
    def norm_one(i, carry):
        rows = pl.ds(i * CHUNK, CHUNK)
        grad = acc[rows]
        values, inverse = normalize(x[rows].astype(F32))
        gnorm[rows] = hidden[rows] + norm_back(grad, values, inverse, ln_gain[0:1])
        put(0, column_sum(grad * values))
        put(2, column_sum(grad))
        return carry

    lax.fori_loop(0, SEG // CHUNK, norm_one, 0)
    gin_moves = spread(gnorm, gin_all, 3)
    for move in gin_moves[:3]:
        move.start()
    att.first(2, own_att(2))

    def small_stage(stage, place, at, count):
        made = []
        for k in range(1, count):
            made.append(links.add(
                lambda: slots.at[stage, place], lambda: slots.at[stage, place],
                lambda k=k: at(lax.rem(place + k, count)),
                lambda k=k: slots.at[stage, lax.rem(place + count - k, count)]))
        for link in made:
            link.start()
        return made

    def small_sum(made, stage, count):
        for link in made:
            link.wait()
        value = slots[stage, 0]
        for k in range(1, count):
            value = value + slots[stage, k]
        return value

    slots[0, me.c] = small[...]
    made = small_stage(0, me.c, lambda p: me.at(c=p), 2)
    tail_m.sixth()
    tail_a.third()
    slots[1, me.x] = small_sum(made, 0, 2)
    made = small_stage(1, me.x, lambda p: me.at(x=p), 4)
    mixed_moves[1].wait()
    mixed_moves[3].start()
    tail_b.second()
    tail_a.fourth()
    slots[2, me.z] = small_sum(made, 1, 4)
    made = small_stage(2, me.z, lambda p: me.at(z=p), 4)
    tail_b.third()
    tail_a.fifth()
    slots[3, me.y] = small_sum(made, 2, 4)
    made = small_stage(3, me.y, lambda p: me.at(y=p), 4)
    tail_b.fourth()
    tail_a.sixth()
    tail_b.fifth()
    tail_b.sixth()
    small_total[...] = small_sum(made, 3, 4)
    gin_moves[1].wait()
    gin_moves[3].start()
    for moves in (mixed_moves, gin_moves):
        moves[0].wait()
        moves[2].wait()
        moves[3].wait()
    tail_m.finish()
    tail_a.finish()
    tail_b.finish()
    swap_att(1).sent()
    swap_att(2).sent()
    pl.semaphore_wait(creditm, 1)
    pl.semaphore_wait(credita, 1)
    for sums in (mlp, att):
        for part in range(PARTS):
            for half in (0, 1):
                for k in (1, 2, 3):
                    sums.send(part, half, k).sent()
    links.finish()


def tail_scratch(parts, kinds, dtype):
    return [
        pltpu.VMEM((6, parts, 2, kinds, ROWS, LANES), F32),
        pltpu.VMEM((2, 2, parts, kinds, ROWS, LANES), F32),
        pltpu.VMEM((3, parts, kinds, ROWS, LANES), F32),
        pltpu.VMEM((parts, kinds, ROWS, LANES), dtype),
    ]


def sums_scratch(kinds):
    return [
        pltpu.VMEM((2, kinds, 4, 4, ROWS, D), F32),
        pltpu.VMEM((PARTS, 6, 2, kinds, 4, ROWS, LANES), BF16),
        pltpu.VMEM((PARTS, 6, 2, kinds, 4, ROWS, LANES), BF16),
        pltpu.VMEM((PARTS, 2, 2, kinds, 4, ROWS, LANES), F32),
    ]


def shards(inputs, memory, doc_ids, key_valid, sticky_bins, ln_gain, ln_shift, w_qkv, b_qv, w_gauss, w_out, b_out,
           w_fc, b_fc, w_proj, b_proj, cotangent):
    head = lax.axis_index("head")
    vmem, hbm = pl.BlockSpec(memory_space=pltpu.VMEM), pl.BlockSpec(memory_space=pl.ANY)
    S, V = jax.ShapeDtypeStruct, pltpu.VMEM
    qkv_rows = w_qkv.transpose(0, 2, 1).reshape(3, PARTS, HD, D)
    patt = jnp.concatenate([qkv_rows, w_out.reshape(1, PARTS, HD, D)], axis=0).transpose(1, 0, 2, 3)
    patt = patt.reshape(PARTS, 4, 4, ROWS, D)
    pmlp = jnp.stack([w_fc.T.reshape(PARTS, 256, D), w_proj.reshape(PARTS, 256, D)], axis=1)
    pmlp = pmlp.reshape(PARTS, 2, 4, 4, ROWS, D)
    bqv = jnp.pad(b_qv.reshape(2, PARTS, HD), ((0, 0), (0, 0), (0, 256 - HD)))
    small = jnp.concatenate([bqv, w_gauss, b_fc.reshape(1, PARTS, 256), jnp.zeros((3, PARTS, 256), F32)], axis=0)
    small = small.transpose(1, 0, 2)
    x, cot = inputs[head], cotangent[head]
    docs, valid = doc_ids[head], key_valid[head]
    doc_col, doc_row, valid_row = docs.reshape(SEG, 1), docs.reshape(1, SEG), valid.reshape(1, SEG)

    count = 2 * (2 + 12 + 8) + 6
    watt, wmlp, sall, coeffs, hidden, qs, ks, vs, mks, mvs, lse, context = pl.pallas_call(
        attend_kernel,
        out_shape=(
            S((2, 2, PARTS, 4, 4, ROWS, D), BF16), S((2, 2, PARTS, 2, 4, 4, ROWS, D), BF16), S((4, PARTS, 8, 256), F32),
            S((N, D), BF16), S((SEG, D), F32), S((PARTS, SEG, 256), BF16), S((PARTS, SEG, 256), BF16),
            S((PARTS, SEG, 256), BF16), S((PARTS, N, 256), BF16), S((PARTS, N, 256), BF16), S((PARTS, SEG, 128), F32),
            S((PARTS, SEG, 256), BF16)),
        in_specs=[vmem] * 12,
        out_specs=[hbm] * 3 + [vmem] * 9,
        scratch_shapes=[
            V((2, 2, PARTS, 4, 4, ROWS, D), BF16), V((4, 128, D), BF16), V((4, PARTS, 8, 256), F32), V((SEG, SEG), F32),
            V((SEG, D), BF16), V((4, SEG, HD), BF16), V((4, SEG, HD), BF16), V((4, SEG, HD), BF16),
            pltpu.SemaphoreType.DMA((count,)), pltpu.SemaphoreType.DMA((count,)), pltpu.SemaphoreType.DMA((6,))],
        compiler_params=pltpu.CompilerParams(collective_id=1, has_side_effects=True, vmem_limit_bytes=VMEM_LIMIT),
        name="gather_attend",
    )(patt, pmlp, memory, small, sticky_bins[head][None], x, doc_col, doc_row, valid_row, ln_gain, ln_shift, b_out[None])

    count = 2 * PARTS * 7 + 3 * (6 + 3 + 1 + 12) + 6 + 10
    tatt, tmlp, small_total, mixed_all, gin_all = pl.pallas_call(
        backward_kernel,
        out_shape=(
            S((PARTS, 1, 4, 4, ROWS, D), F32), S((PARTS, 2, 4, 4, ROWS, D), BF16), S((PARTS, 24, 256), F32),
            S((4, SEG, D), BF16), S((4, SEG, D), F32)),
        in_specs=[vmem] * 2 + [hbm] * 3 + [vmem] * 15,
        out_specs=[hbm, hbm, vmem, hbm, hbm],
        scratch_shapes=[
            V((2, 2, 2, 4, 4, ROWS, D), BF16), V((2, 2, 2, 4, 4, ROWS, D), F32),
            V((SEG, D), F32), V((SEG, D), F32), V((SEG, D), F32), V((SEG, D), BF16), V((SEG, D), BF16), V((SEG, D), BF16),
            V((SEG, SEG), F32), V((4, SEG, HD), BF16), V((4, SEG, HD), BF16), V((4, SEG, HD), BF16), V((4, SEG, HD), BF16),
            V((SEG, HD), F32), V((SEG, HD), F32), V((N, HD), F32), V((N, HD), F32)]
        + sums_scratch(2) + sums_scratch(1)
        + tail_scratch(3, 2, BF16) + tail_scratch(2, 1, F32) + tail_scratch(1, 1, F32)
        + [V((PARTS, 24, 256), F32), V((4, 4, PARTS, 24, 256), F32),
           pltpu.SemaphoreType.DMA((count,)), pltpu.SemaphoreType.DMA((count,)),
           pltpu.SemaphoreType.REGULAR, pltpu.SemaphoreType.REGULAR, pltpu.SemaphoreType.DMA((8,))],
        compiler_params=pltpu.CompilerParams(collective_id=2, has_side_effects=True, vmem_limit_bytes=VMEM_LIMIT),
        name="mlp_backward",
    )(x, cot, hidden, watt, wmlp, coeffs, sall, doc_col, doc_row, valid_row, ln_gain, ln_shift, b_proj[None],
      qs, ks, vs, mks, mvs, lse, context)

    tatt = tatt.reshape(PARTS, 4, HD, D)
    tmlp = tmlp.reshape(PARTS, 2, 256, D)
    g_bqv = lax.dynamic_index_in_dim(small_total[:, 6:8].reshape(PARTS, 2, 4, HD), head, 2, keepdims=False)
    g_gauss = lax.dynamic_index_in_dim(small_total[:, 8:16].reshape(PARTS, 4, 2, 256), head, 1, keepdims=False)
    g_bfc = lax.dynamic_index_in_dim(small_total[:, 16:20], head, 1, keepdims=False)
    rows = small_total[:, 0:6].transpose(1, 0, 2).reshape(6, D)
    return (
        mixed_all,
        gin_all,
        rows[0:2],
        rows[2:4],
        tatt[:, :3].transpose(1, 3, 0, 2).reshape(3, D, 192),
        g_bqv.transpose(1, 0, 2).reshape(2, 192),
        g_gauss.transpose(1, 0, 2),
        tatt[:, 3].reshape(192, D),
        rows[4],
        tmlp[:, 0].reshape(D, D).T.astype(F32),
        g_bfc.reshape(D),
        tmlp[:, 1].reshape(D, D).astype(F32),
        rows[5],
    )


def solution(mesh):
    return jax.shard_map(
        shards,
        mesh=mesh,
        in_specs=(
            P("dp", None, None),
            P("dp", "head", None),
            P("dp", None),
            P("dp", None),
            P("dp", None),
            P(),
            P(),
            P(None, None, "head"),
            P(None, "head"),
            P(None, "head", None),
            P("head", None),
            P(),
            P(None, "head"),
            P("head"),
            P("head", None),
            P(),
            P("dp", None, None),
        ),
        out_specs=(
            P("dp", None, None),
            P("dp", None, None),
            P(),
            P(),
            P(None, None, "head"),
            P(None, "head"),
            P(None, "head", None),
            P("head", None),
            P(),
            P(None, "head"),
            P("head"),
            P("head", None),
            P(),
        ),
        check_vma=False,
    )
```

```python
from functools import partial

import jax
import jax.numpy as jnp
from jax import lax
from jax.experimental import pallas as pl
from jax.experimental.pallas import tpu as pltpu
from jax.sharding import PartitionSpec as P

MESH = pl.DeviceIdType.MESH
BF16, F32 = jnp.bfloat16, jnp.float32
D, N, HEADS, HD, FF, SEG, HALF = 768, 256, 12, 64, 3072, 512, 256
PARTS, ROWS, LANES = 3, 16, 384
EPSILON = 1e-05
RIDGE_WEIGHT = 0.5
SIGMA_SCALE = 0.01
SCORE_SCALE = 0.125
NEG_FILL = -1e30
GELU_COEFF = 0.7978845608028654
PRECISE = lax.Precision.HIGHEST
VMEM_LIMIT = 60 * 1024 * 1024
BLOCK = 256
CHUNK = 128
BLOCKS = SEG // BLOCK


class Place:
    def __init__(self):
        dp, head = lax.axis_index("dp"), lax.axis_index("head")
        self.head = head
        self.yl = lax.div(dp, 16)
        self.z = lax.rem(lax.div(dp, 4), 4)
        self.x = lax.rem(dp, 4)
        self.yh = lax.div(head, 2)
        self.c = lax.rem(head, 2)
        self.y = self.yh * 2 + self.yl

    def at(self, x=None, z=None, y=None, c=None):
        x = self.x if x is None else x
        z = self.z if z is None else z
        c = self.c if c is None else c
        if y is None:
            yl, yh = self.yl, self.yh
        else:
            yl, yh = lax.rem(y, 2), lax.div(y, 2)
        return (yl * 16 + z * 4 + x, yh * 2 + c)

    def core(self):
        return self.at(c=1 - self.c)

    def ring(self, along_x, k):
        return self.at(x=step(self.x, k)) if along_x else self.at(z=step(self.z, k))


def step(place, by):
    return lax.rem(place + by, 4)


def lanes(half):
    return pl.ds(half * LANES, LANES)


def greet(devices):
    sem = pltpu.get_barrier_semaphore()
    for device in devices:
        pl.semaphore_signal(sem, inc=1, device_id=device, device_id_type=MESH)


def met(devices):
    pl.semaphore_wait(pltpu.get_barrier_semaphore(), len(devices))


class Links:
    def __init__(self, send, recv):
        self.send, self.recv, self.used, self.all = send, recv, 0, []

    def add(self, src, dst, device, arrives):
        link = Link(self, self.used, src, dst, device, arrives)
        self.used += 1
        self.all.append(link)
        return link

    def finish(self):
        for link in self.all:
            if not link.done:
                link.sent()


class Link:
    def __init__(self, links, index, src, dst, device, arrives):
        self.links, self.index, self.done = links, index, False
        self.src, self.dst, self.device, self.arrives = src, dst, device, arrives

    def copy(self, dst):
        return pltpu.make_async_remote_copy(
            src_ref=self.src(), dst_ref=dst, send_sem=self.links.send.at[self.index],
            recv_sem=self.links.recv.at[self.index], device_id=self.device(), device_id_type=MESH)

    def start(self):
        self.copy(self.dst()).start()

    def wait(self):
        self.copy(self.arrives()).wait_recv()

    def sent(self):
        self.copy(self.dst()).wait_send()


class PlaneGather:
    def __init__(self, links, me, view, row, column):
        self.one, self.two = [[], []], [[], []]
        for k in (1, 3, 2):
            back = 4 - k
            self.one[0].append(links.add(
                lambda: view(me.z, me.x, 0), lambda: view(me.z, me.x, 0), lambda k=k: me.ring(True, k),
                lambda back=back: view(me.z, step(me.x, back), 0)))
            self.one[1].append(links.add(
                lambda: view(me.z, me.x, 1), lambda: view(me.z, me.x, 1), lambda k=k: me.ring(False, k),
                lambda back=back: view(step(me.z, back), me.x, 1)))
            self.two[0].append(links.add(
                lambda: row(me.z, 0), lambda: row(me.z, 0), lambda k=k: me.ring(False, k),
                lambda back=back: row(step(me.z, back), 0)))
            self.two[1].append(links.add(
                lambda: column(me.x, 1), lambda: column(me.x, 1), lambda k=k: me.ring(True, k),
                lambda back=back: column(step(me.x, back), 1)))

    def first(self):
        for a, b in zip(*self.one):
            a.start()
            b.start()

    def second(self):
        for half in (0, 1):
            for link in self.one[half]:
                link.wait()
            for link in self.two[half]:
                link.start()

    def finish(self):
        for a, b in zip(*self.two):
            a.wait()
            b.wait()


def nt(a, b):
    return lax.dot_general(a, b, (((1,), (1,)), ((), ())), preferred_element_type=F32)


def nn(a, b):
    return lax.dot_general(a, b, (((1,), (0,)), ((), ())), preferred_element_type=F32)


def tn(a, b):
    return lax.dot_general(a, b, (((0,), (0,)), ((), ())), preferred_element_type=F32)


def normalize(values):
    centred = values - jnp.mean(values, axis=-1, keepdims=True)
    inverse = lax.rsqrt(jnp.mean(centred * centred, axis=-1, keepdims=True) + EPSILON)
    return centred * inverse, inverse


def norm_back(grad, normed, inverse, gain):
    scaled = grad * gain
    return inverse * (scaled - jnp.mean(scaled, axis=-1, keepdims=True)
                      - normed * jnp.mean(scaled * normed, axis=-1, keepdims=True))


def column_sum(values):
    return jnp.sum(values, axis=0, keepdims=True)


def as_column(row):
    return jnp.broadcast_to(row.astype(F32), (8, SEG)).T[:, 0:1]


def mask_bias(doc_row, valid_row):
    doc_row = doc_row.astype(F32)
    doc_col = as_column(doc_row)
    rows = lax.broadcasted_iota(jnp.int32, (SEG, SEG), 0)
    cols = lax.broadcasted_iota(jnp.int32, (SEG, SEG), 1)
    live = (valid_row == 1) | (rows == cols)
    return jnp.where((cols <= rows) & (doc_col == doc_row) & live, 0.0, NEG_FILL)


def gaussian(mem_scores, gauss):
    centre = jax.nn.sigmoid(jnp.sum(mem_scores * gauss[0:1], axis=-1, keepdims=True))
    width = jnp.sum(mem_scores * gauss[1:2], axis=-1, keepdims=True)
    softplus = jnp.maximum(width, 0.0) + jnp.log1p(jnp.exp(-jnp.abs(width)))
    variance = SIGMA_SCALE * softplus + (1.0 / N) ** 2
    places = (lax.broadcasted_iota(jnp.int32, (1, N), 1).astype(F32) + 0.5) / N
    offsets = centre - places
    inverse = 1.0 / variance
    density = (1.0 / N) * lax.rsqrt(variance) * jnp.exp(-0.5 * offsets * offsets * inverse)
    return centre, width, offsets, inverse, density


LOWEST, HIGHEST = RIDGE_WEIGHT, 650.0


def attend_kernel(inputs, memory, doc_ids, key_valid, sticky_bins, ln_gain, ln_shift, w_qkv, b_qv, w_gauss, w_out, b_out,
                  w_fc, b_fc, w_proj,
                  watt_out, wmlp, sall_out, coeffs, hidden, qs, ks, vs, mks, mvs, lse, context,
                  watt, pmlp, mseg, sall, x, gate, bias, n1, hq, hk, hv, send, recv, local):
    me = Place()
    mine = pl.ds(me.head, 1)
    peers = ([me.core(), me.at(y=3 - me.y), me.at(y=step(me.y, 2)), me.at(y=step(me.y, 2), c=1 - me.c)]
             + [me.ring(True, k) for k in (1, 2, 3)] + [me.ring(False, k) for k in (1, 2, 3)])
    greet(peers)
    load_x = pltpu.make_async_copy(inputs.at[me.head], x, local.at[0])
    load_x.start()
    for kind in range(3):
        for i in range(PARTS):
            watt[me.yh, me.c, i, kind] = w_qkv[kind, i * HD:(i + 1) * HD].reshape(4, ROWS, D)
    for i in range(PARTS):
        watt[me.yh, me.c, i, 3] = w_out[i * HD:(i + 1) * HD].reshape(4, ROWS, D)
    mine_small = sall.at[me.head]
    mine_small[...] = jnp.zeros((PARTS, 8, 256), F32)
    for i in range(PARTS):
        mine_small[i, 0:2, 0:HD] = b_qv[:, i * HD:(i + 1) * HD]
        mine_small[i, 2:4] = w_gauss[i]
        mine_small[i, 4:5] = b_fc[i * 256:(i + 1) * 256].reshape(1, 256)
    for i in range(PARTS):
        pmlp[i, 0] = w_fc[:, i * 256:(i + 1) * 256].T.reshape(4, 4, ROWS, D)
        pmlp[i, 1] = w_proj[i * 256:(i + 1) * 256].reshape(4, 4, ROWS, D)
    met(peers)

    links = Links(send, recv)

    class Gather:
        def __init__(self, wall, own, low, high):
            def block(yh, c, z, xx, cut):
                return wall.at[yh, c, low:high, ..., z, xx, :, cut]

            every = slice(None)

            def view(z, xx, half, c=None):
                return block(1 - me.yh, me.c if c is None else c, z, xx, lanes(half))

            def row(z, half, c=None):
                return view(z, every, half, c)

            def column(xx, half, c=None):
                return view(every, xx, half, c)

            self.across = links.add(
                lambda: own().at[low:high, ..., me.z, me.x, :, :], lambda: block(me.yh, me.c, me.z, me.x, every),
                lambda: me.at(y=3 - me.y), lambda: block(1 - me.yh, me.c, me.z, me.x, every))
            self.plane = PlaneGather(links, me, view, row, column)
            self.passed = []
            for k in (0, 1, 3, 2):
                self.passed.append(links.add(
                    lambda k=k: row(step(me.z, k), 0), lambda k=k: row(step(me.z, k), 0), me.core,
                    lambda k=k: row(step(me.z, k), 0, 1 - me.c)))
                self.passed.append(links.add(
                    lambda k=k: column(step(me.x, k), 1), lambda k=k: column(step(me.x, k), 1), me.core,
                    lambda k=k: column(step(me.x, k), 1, 1 - me.c)))

        def first(self):
            self.across.wait()
            self.plane.first()

        def second(self):
            self.plane.second()
            self.passed[0].start()
            self.passed[1].start()

        def third(self):
            self.plane.finish()
            for link in self.passed[2:]:
                link.start()

        def ready(self):
            for link in self.passed:
                link.wait()

    own_att = lambda: watt.at[me.yh, me.c]
    own_mlp = lambda: pmlp
    early, late = Gather(watt, own_att, 0, 1), Gather(watt, own_att, 1, PARTS)
    units = Gather(wmlp, own_mlp, 0, PARTS)
    swap_att = links.add(own_att, own_att, me.core, lambda: watt.at[me.yh, 1 - me.c])
    swap_mlp = links.add(own_mlp, lambda: wmlp.at[me.yh, me.c], me.core, lambda: wmlp.at[me.yh, 1 - me.c])
    sent, sent_small = [], []
    for k in (1, 2, 3):
        def other(k=k):
            return lax.rem(me.head + k, 4)

        def device(k=k):
            return (me.yl * 16 + me.z * 4 + me.x, lax.rem(me.head + k, 4))

        def before(k=k):
            return lax.rem(me.head + (4 - k), 4)

        sent.append(links.add(lambda other=other: memory.at[other()], lambda: mseg.at[me.head], device,
                              lambda before=before: mseg.at[before()]))
        sent_small.append(links.add(lambda: sall.at[me.head], lambda: sall.at[me.head], device,
                                    lambda before=before: sall.at[before()]))
    early.across.start()
    late.across.start()
    units.across.start()
    for link in sent:
        link.start()
    swap_att.start()
    for link in sent_small:
        link.start()
    swap_mlp.start()
    keep_mlp = pltpu.make_async_copy(pmlp, wmlp.at[me.yh, me.c], local.at[1])
    keep_mlp.start()
    mseg[mine] = memory[mine]
    early.first()
    load_x.wait()
    values, _ = normalize(x[...].astype(F32))
    n1[...] = (values * ln_gain[0:1] + ln_shift[0:1]).astype(BF16)
    hidden[...] = x[...].astype(F32) + b_out[...]
    late.first()

    dot = partial(jnp.dot, preferred_element_type=F32, precision=PRECISE)
    rows = lax.broadcasted_iota(jnp.int32, (N, N), 0)
    cols = lax.broadcasted_iota(jnp.int32, (N, N), 1)
    gap = (rows - cols).astype(F32)
    curve = jnp.exp(-0.5 * gap * gap)
    eye = (rows == cols).astype(F32)
    picked = (sticky_bins[mine] == rows).astype(F32)
    counts = 1.0 + jnp.sum(picked, axis=1, keepdims=True)
    gram = dot(curve, counts * curve) + RIDGE_WEIGHT * eye

    def newton(count, state):
        def body(_, state):
            inverse, gap = state
            scale = 2.0 / (2.0 - gap * gap)
            inverse = scale * (2.0 * inverse - dot(inverse, dot(gram, inverse)))
            return inverse, gap * gap / (2.0 - gap * gap)

        return lax.fori_loop(0, count, body, state)

    state = ((2.0 / (LOWEST + HIGHEST)) * eye, jnp.float32((HIGHEST - LOWEST) / (HIGHEST + LOWEST)))
    early.second()
    state = newton(2, state)
    late.second()
    units.first()
    state = newton(2, state)
    early.third()
    state = newton(3, state)
    late.third()
    units.second()
    inverse, _ = newton(3, state)
    docs = doc_ids[mine]
    bias[...] = mask_bias(docs, key_valid[mine])
    gate[...] = (as_column(docs) == docs[:, 0:1].astype(F32)).astype(F32)
    for link in sent:
        link.wait()
    first_half = mseg[0:2].reshape(HALF, D).astype(F32)
    held = first_half + jnp.dot(picked.astype(BF16), mseg[2:4].reshape(HALF, D), preferred_element_type=F32)
    coeffs[...] = dot(inverse, dot(curve, held)).astype(BF16)
    swap_att.wait()
    early.ready()
    for link in sent_small:
        link.wait()
    out = [pltpu.make_async_copy(watt, watt_out, local.at[2]), pltpu.make_async_copy(sall, sall_out, local.at[3])]
    hooks = (((1, 0), units.third),)

    def group(i, carry):
        def weight(kind):
            return watt[:, :, i, kind].reshape(4 * HD, D)

        def heads_row(r):
            return jnp.concatenate([sall[g, i, r:r + 1, 0:HD] for g in range(4)], axis=1)

        @pl.when(i == 1)
        def _():
            late.ready()
            for copy in out:
                copy.start()

        q4 = (nt(n1[...], weight(0)) + heads_row(0)).astype(BF16)
        k4 = nt(n1[...], weight(1)).astype(BF16)
        v4 = (nt(n1[...], weight(2)) + heads_row(1)).astype(BF16)
        mk4 = nt(coeffs[...], weight(1)).astype(BF16)
        mv4 = nt(coeffs[...], weight(2)).astype(BF16)
        qs[i], ks[i], vs[i], mks[i], mvs[i] = q4, k4, v4, mk4, mv4
        for g in range(4):
            part = slice(g * HD, (g + 1) * HD)
            hq[g], hk[g], hv[g] = q4[:, part], k4[:, part], v4[:, part]
        parts = []
        for g in range(4):
            part = slice(g * HD, (g + 1) * HD)
            mk, mv = mk4[:, part], mv4[:, part]
            blocks = []
            for r in range(BLOCKS):
                rows, cols = slice(r * BLOCK, (r + 1) * BLOCK), slice(0, (r + 1) * BLOCK)
                q = hq[g, rows]
                scores = nt(q, hk[g, cols]) * SCORE_SCALE + bias[rows, cols]
                top = jnp.max(scores, axis=-1, keepdims=True)
                weights = jnp.exp(scores - top)
                total = jnp.sum(weights, axis=-1, keepdims=True)
                lse[i, rows, g:g + 1] = top + jnp.log(total)
                probs = (weights * (1.0 / total)).astype(BF16)
                attended = nn(probs, hv[g, cols])
                mem_scores = nt(q, mk) * SCORE_SCALE
                density = gaussian(mem_scores, sall[g, i, 2:4])[-1].astype(BF16)
                blocks.append((attended + gate[rows] * nn(density, mv)).astype(BF16))
            parts.append(jnp.concatenate(blocks, axis=0))
            for when, move in hooks:
                if when[1] == g:
                    @pl.when(i == when[0])
                    def _(move=move):
                        move()

        mixed = jnp.concatenate(parts, axis=1)
        context[i] = mixed
        hidden[...] += nn(mixed, weight(3))

        return carry

    lax.fori_loop(0, PARTS, group, 0)
    swap_mlp.wait()
    units.ready()
    keep_mlp.wait()
    for copy in out:
        copy.wait()
    links.finish()


class Sums:
    def __init__(self, links, me, kinds, other, sbuf, rbuf, kept, credit):
        self.links, self.me, self.kinds = links, me, kinds
        self.other, self.sbuf, self.rbuf, self.kept, self.credit = other, sbuf, rbuf, kept, credit
        self.base = links.used
        links.used += PARTS * 7

    def swap(self, part, src):
        return Link(self.links, self.base + part, src, lambda: self.other, self.me.core, lambda: self.other)

    def send(self, part, half, k):
        i = half * 3 + k - 1
        return Link(self.links, self.base + PARTS + part * 6 + i, lambda: self.sbuf.at[part, i],
                    lambda: self.rbuf.at[part, i], lambda: self.me.ring(half == 0, k), lambda: self.rbuf.at[part, i])

    def first(self, part, own):
        me = self.me
        self.swap(part, lambda: self.other).wait()
        for k in (2, 1, 3, 0):
            for half in (0, 1):
                def body(i, carry, half=half, k=k):
                    t, kind = lax.div(i, self.kinds), lax.rem(i, self.kinds)
                    for q in range(4):
                        z, x = (q, step(me.x, k)) if half == 0 else (step(me.z, k), q)
                        cut = slice(half * LANES, (half + 1) * LANES)
                        value = own(t, kind, z, x, cut) + self.other[t, kind, z, x, :, cut]
                        if k == 0:
                            self.kept[part, half, t, kind, q] = value
                        else:
                            self.sbuf[part, half * 3 + k - 1, t, kind, q] = value.astype(BF16)
                    return carry

                lax.fori_loop(0, 2 * self.kinds, body, 0)
                if k:
                    self.send(part, half, k).start()
        pl.semaphore_signal(self.credit, inc=1, device_id=me.core(), device_id_type=MESH)


class Tail:
    def __init__(self, links, me, sums, low, high, total, rbuf2, ylocal, ybuf, final, local):
        self.me, self.sums, self.low, self.high, self.total = me, sums, low, high, total
        self.rbuf2, self.ylocal, self.ybuf, self.final, self.local = rbuf2, ylocal, ybuf, final, local
        kept = sums.kept
        self.two = {}
        for half in (0, 1):
            across = (lambda: me.z) if half == 0 else (lambda: me.x)
            for k in (2, 1, 3):
                i = half * 3 + k - 1
                self.two[half, k] = links.add(
                    lambda half=half, k=k, across=across: kept.at[low:high, half, :, :, step(across(), k)],
                    lambda i=i: rbuf2.at[i], lambda half=half, k=k: me.ring(half == 1, k), lambda i=i: rbuf2.at[i])
        self.three = []
        for k in (2, 1, 3):
            def target(k=k):
                return step(me.y, k)

            self.three.append(links.add(
                lambda target=target: ylocal.at[lax.div(target(), 2), lax.rem(target(), 2)],
                lambda k=k: ybuf.at[k - 1], lambda target=target: me.at(y=target()), lambda k=k: ybuf.at[k - 1]))

        def view(z, x, half):
            return total.at[low:high, :, z, x, :, lanes(half)]

        def row(z, half):
            return total.at[low:high, :, z, :, :, lanes(half)]

        def column(x, half):
            return total.at[low:high, :, :, x, :, lanes(half)]

        self.view = view
        self.mate = links.add(lambda: final, lambda: view(me.z, me.x, me.yl),
                              lambda: me.at(y=me.yh * 2 + 1 - me.yl), lambda: view(me.z, me.x, 1 - me.yl))
        self.gather = PlaneGather(links, me, view, row, column)

    def second(self):
        sums, kept = self.sums, self.sums.kept
        for half in (0, 1):
            for part in range(self.low, self.high):
                for k in (1, 2, 3):
                    sums.send(part, half, k).wait()

                def body(i, carry, half=half, part=part):
                    t, kind = lax.div(i, sums.kinds), lax.rem(i, sums.kinds)
                    value = kept[part, half, t, kind]
                    for k in (1, 2, 3):
                        value = value + sums.rbuf[part, half * 3 + k - 1, t, kind].astype(F32)
                    kept[part, half, t, kind] = value
                    return carry

                lax.fori_loop(0, 2 * sums.kinds, body, 0)
            for k in (2, 1, 3):
                self.two[half, k].start()

    def third(self):
        me, kept = self.me, self.sums.kept
        for half in (0, 1):
            for k in (1, 2, 3):
                self.two[half, k].wait()
            across = me.z if half == 0 else me.x
            for p in range(self.low, self.high):
                for t in (0, 1):
                    value = kept[p, half, t, :, across]
                    for k in (1, 2, 3):
                        value = value + self.rbuf2[half * 3 + k - 1, p - self.low, t]
                    self.ylocal[t, half, p - self.low] = value
        for link in self.three:
            link.start()

    def keep(self):
        return pltpu.make_async_copy(self.final, self.view(self.me.z, self.me.x, self.me.yl), self.local)

    def fourth(self):
        me = self.me
        for link in self.three:
            link.wait()
        self.final[...] = (self.ylocal[me.yh, me.yl] + self.ybuf[0] + self.ybuf[1] + self.ybuf[2]).astype(
            self.final.dtype)
        self.keep().start()
        self.mate.start()

    def fifth(self):
        self.keep().wait()
        self.mate.wait()
        self.gather.first()

    def sixth(self):
        self.gather.second()

    def finish(self):
        self.gather.finish()


def backward_kernel(inputs, cotangent, hidden_in, watt, wmlp, coeffs, sall, doc_ids, key_valid, ln_gain, ln_shift, b_proj,
                    qs, ks, vs, mks, mvs, lse, context,
                    tatt, tmlp, small_total, mixed_all, gin_all,
                    x, cot, gate, wbuf, gbuf, hidden, acc, gnorm, n12, gbranch, mixed, bias, hq, hk, hv, gcs, dks, dvs, gmks, gmvs,
                    otherm, sbufm, rbufm, keptm, othera, sbufa, rbufa, kepta,
                    *rest):
    tails_m, tails_a, (small, slots, send, recv, creditm, credita, local) = rest[:12], rest[12:24], rest[24:]
    me = Place()
    peers = ([me.core()] + [me.ring(True, k) for k in (1, 2, 3)] + [me.ring(False, k) for k in (1, 2, 3)]
             + [me.at(y=step(me.y, k)) for k in (1, 2, 3)])
    greet(peers)
    links = Links(send, recv)
    mlp = Sums(links, me, 2, otherm, sbufm, rbufm, keptm, creditm)
    att = Sums(links, me, 1, othera, sbufa, rbufa, kepta, credita)
    m = [Tail(links, me, mlp, p, p + 1, tmlp, *tails_m[4 * p:4 * p + 4], local.at[4 + p]) for p in range(PARTS)]
    a = [Tail(links, me, att, p, p + 1, tatt, *tails_a[4 * p:4 * p + 4], local.at[7 + p]) for p in range(PARTS)]

    def load(index, slot):
        part, mine = lax.div(index, 2), lax.rem(index, 2)
        owner = mine * me.c + (1 - mine) * (1 - me.c)
        return pltpu.make_async_copy(wmlp.at[:, owner, part], wbuf.at[slot], local.at[slot])

    def load_att(part, slot):
        return pltpu.make_async_copy(watt.at[:, :, part], wbuf.at[slot], local.at[slot])

    load_hidden = pltpu.make_async_copy(hidden_in, hidden, local.at[12])
    load_hidden.start()
    load_cot = pltpu.make_async_copy(cotangent.at[me.head], cot, local.at[10])
    load_cot.start()
    load(0, 0).start()
    load(1, 1).start()
    load_x = pltpu.make_async_copy(inputs.at[me.head], x, local.at[11])
    load_x.start()
    load_hidden.wait()

    def start_mlp(i, carry):
        rows = pl.ds(i * CHUNK, CHUNK)
        values, _ = normalize(hidden[rows])
        n12[rows] = (values * ln_gain[1:2] + ln_shift[1:2]).astype(BF16)
        acc[rows] = hidden[rows] + b_proj[...]
        return carry

    lax.fori_loop(0, SEG // CHUNK, start_mlp, 0)
    load_cot.wait()
    load_x.wait()
    gnorm[...] = jnp.zeros_like(gnorm)
    small[...] = jnp.zeros_like(small)
    met(peers)

    def own_mlp(t, kind, z, xx, cut):
        return gbuf[1, t, kind, z, xx, :, cut]

    def swap_mlp(part):
        return mlp.swap(part, lambda: gbuf.at[0])

    def units(index, carry):
        part, mine = lax.div(index, 2), lax.rem(index, 2)
        owner = mine * me.c + (1 - mine) * (1 - me.c)
        load(index, mine).wait()

        @pl.when((mine == 0) & (part > 0))
        def _():
            mlp.first(part - 1, own_mlp)
            swap_mlp(part - 1).sent()

        @pl.when(index == 5)
        def _():
            m[0].second()

        wfc = wbuf[mine, :, 0].reshape(512, D)
        wproj = wbuf[mine, :, 1].reshape(512, D)
        bias_fc = jnp.concatenate([sall[owner, part, 4:5], sall[2 + owner, part, 4:5]], axis=1)
        pre = nt(n12[...], wfc) + bias_fc
        inner = jnp.tanh(GELU_COEFF * (pre + 0.044715 * pre * pre * pre))
        activation = (0.5 * pre * (1.0 + inner)).astype(BF16)
        slope = 0.5 * (1.0 + inner) + (0.5 * GELU_COEFF) * pre * (1.0 - inner * inner) * (
            1.0 + 3.0 * 0.044715 * pre * pre)
        acc[...] += nn(activation, wproj)
        gpre = (nt(cot[...], wproj) * slope).astype(BF16)
        units_sum = column_sum(gpre.astype(F32))
        small[part, pl.ds(16 + owner, 1)] = units_sum[:, 0:256]
        small[part, pl.ds(18 + owner, 1)] = units_sum[:, 256:512]
        gnorm[...] += nn(gpre, wfc)
        gbuf[mine, :, 0] = tn(gpre, n12[...]).reshape(2, 4, 4, ROWS, D)
        gbuf[mine, :, 1] = tn(activation, cot[...]).reshape(2, 4, 4, ROWS, D)

        @pl.when(mine == 0)
        def _():
            @pl.when(part > 0)
            def _():
                pl.semaphore_wait(creditm, 1)

            swap_mlp(part).start()

        @pl.when(index < 4)
        def _():
            load(index + 2, mine).start()

        return carry

    lax.fori_loop(0, 6, units, 0)
    load_att(0, 0).start()
    load_att(1, 1).start()
    mlp.first(2, own_mlp)
    swap_mlp(2).sent()
    mixed[...] = acc[...].astype(BF16)
    far_head = (1 - me.yh) * 2 + me.c
    mate, far_mate = me.yh * 2 + 1 - me.c, (1 - me.yh) * 2 + 1 - me.c

    class Spread:
        def __init__(self, block, everywhere, slot):
            self.keep = pltpu.make_async_copy(block, everywhere.at[me.head], local.at[slot])
            self.near = links.add(lambda: block, lambda: everywhere.at[me.head], me.core, lambda: everywhere.at[mate])
            self.far, self.passed = [], []
            for i in range(SEG // CHUNK):
                rows = pl.ds(i * CHUNK, CHUNK)
                self.far.append(links.add(
                    lambda rows=rows: block.at[rows], lambda rows=rows: everywhere.at[me.head, rows],
                    lambda: me.at(y=step(me.y, 2)), lambda rows=rows: everywhere.at[far_head, rows]))
                self.passed.append(links.add(
                    lambda rows=rows: everywhere.at[far_head, rows], lambda rows=rows: everywhere.at[far_head, rows],
                    me.core, lambda rows=rows: everywhere.at[far_mate, rows]))

        def start(self):
            self.keep.start()
            self.near.start()

        def send(self, i):
            self.far[i].start()

        def forward(self, i):
            self.far[i].wait()
            self.passed[i].start()

        def finish(self):
            self.keep.wait()
            self.near.wait()
            for link in self.passed:
                link.wait()

    mixed_moves = Spread(mixed, mixed_all, 2)
    mixed_moves.start()

    def put(row, vector):
        for i in range(3):
            small[i, row:row + 1] += vector[:, i * 256:(i + 1) * 256]

    def norm_two(i, carry):
        rows = pl.ds(i * CHUNK, CHUNK)
        values, inverse = normalize(hidden[rows])
        grad = gnorm[rows]
        cotangent = cot[rows].astype(F32)
        total = cotangent + norm_back(grad, values, inverse, ln_gain[1:2])
        hidden[rows] = total
        gbranch[rows] = total.astype(BF16)
        put(1, column_sum(grad * values))
        put(3, column_sum(grad))
        put(4, column_sum(total))
        put(5, column_sum(cotangent))
        values, _ = normalize(x[rows].astype(F32))
        n12[rows] = (values * ln_gain[0:1] + ln_shift[0:1]).astype(BF16)
        return carry

    lax.fori_loop(0, SEG // CHUNK, norm_two, 0)
    docs = doc_ids[pl.ds(me.head, 1)]
    bias[...] = mask_bias(docs, key_valid[pl.ds(me.head, 1)])
    gate[...] = (as_column(docs) == docs[:, 0:1].astype(F32)).astype(F32)
    acc[...] = jnp.zeros_like(acc)

    def own_att(part):
        slot = lax.rem(part, 2)
        return lambda t, kind, z, xx, cut: gbuf[slot, t, me.c, z, xx, :, cut]

    def swap_att(part):
        slot = lax.rem(part, 2)
        return att.swap(part, lambda: gbuf.at[slot, :, pl.ds(1 - me.c, 1)])

    hooks = (
        ((0, 0), m[1].second), ((0, 1), m[0].third), ((0, 1), partial(mixed_moves.send, 0)), ((0, 2), m[0].fourth),
        ((0, 3), m[2].second), ((0, 3), m[0].fifth),
        ((1, 0), m[1].third), ((1, 0), partial(mixed_moves.send, 1)), ((1, 0), m[0].sixth), ((1, 1), m[1].fourth),
        ((1, 1), m[2].third), ((1, 1), partial(mixed_moves.send, 2)), ((1, 2), m[1].fifth), ((1, 2), a[0].second),
        ((1, 3), m[2].fourth), ((1, 3), m[1].sixth),
        ((2, 0), m[2].fifth), ((2, 0), a[0].third), ((2, 0), partial(mixed_moves.send, 3)), ((2, 1), m[2].sixth),
        ((2, 1), a[0].fourth), ((2, 1), partial(mixed_moves.forward, 0)), ((2, 1), partial(mixed_moves.forward, 1)),
        ((2, 2), a[1].second), ((2, 2), a[0].fifth), ((2, 2), partial(mixed_moves.forward, 2)), ((2, 3), a[1].third),
        ((2, 3), a[0].sixth), ((2, 3), partial(mixed_moves.forward, 3)))

    def group(i, carry):
        slot = lax.rem(i, 2)
        load_att(i, slot).wait()

        def weight(kind):
            return wbuf[slot, :, :, kind].reshape(4 * HD, D)

        q4, k4, v4, mk4, mv4 = qs[i], ks[i], vs[i], mks[i], mvs[i]
        gc4 = nt(gbranch[...], weight(3)).astype(BF16)
        for g in range(4):
            part = slice(g * HD, (g + 1) * HD)
            hq[g], hk[g], hv[g], gcs[g] = q4[:, part], k4[:, part], v4[:, part], gc4[:, part]

        @pl.when(i > 0)
        def _():
            att.first(i - 1, own_att(i - 1))

        gqs, gks, gvs, gmk_all, gmv_all = [], [], [], [], []
        for g in range(4):
            part = slice(g * HD, (g + 1) * HD)
            mk, mv = mk4[:, part], mv4[:, part]
            gauss = sall[g, i, 2:4]
            blocks = []
            grad0 = jnp.zeros((1, N), F32)
            grad1 = jnp.zeros((1, N), F32)
            for r in range(BLOCKS):
                rows, cols = slice(r * BLOCK, (r + 1) * BLOCK), slice(0, (r + 1) * BLOCK)
                q, gc = hq[g, rows], gcs[g, rows]
                k, v = hk[g, cols], hv[g, cols]
                scores = nt(q, k) * SCORE_SCALE + bias[rows, cols]
                probs = jnp.exp(scores - lse[i, rows, g:g + 1])
                gprobs = nt(gc, v)
                inner = jnp.sum(probs * gprobs, axis=-1, keepdims=True)
                gscores = (probs * (gprobs - inner)).astype(BF16)
                dv = tn(probs.astype(BF16), gc)
                dk = tn(gscores, q)
                if r == 0:
                    dvs[cols], dks[cols] = dv, dk
                else:
                    old = slice(0, r * BLOCK)
                    dvs[old] += dv[old]
                    dks[old] += dk[old]
                    dvs[rows], dks[rows] = dv[rows], dk[rows]
                dq = nn(gscores, k)
                mem_scores = nt(q, mk) * SCORE_SCALE
                centre, width, offsets, inv, density = gaussian(mem_scores, gauss)
                grec = (gc.astype(F32) * gate[rows]).astype(BF16)
                gdens = nt(grec, mv) * density
                ratio = offsets * inv
                gcentre = -jnp.sum(gdens * ratio, axis=-1, keepdims=True)
                gvar = 0.5 * jnp.sum(gdens * (ratio * ratio - inv), axis=-1, keepdims=True)
                gcl = gcentre * (centre * (1.0 - centre))
                gwl = gvar * (SIGMA_SCALE * jax.nn.sigmoid(width))
                grad0 = grad0 + column_sum(gcl * mem_scores)
                grad1 = grad1 + column_sum(gwl * mem_scores)
                gms = (gcl * gauss[0:1] + gwl * gauss[1:2]).astype(BF16)
                gmv = tn(density.astype(BF16), grec)
                gmk = tn(gms, q)
                if r == 0:
                    gmvs[...], gmks[...] = gmv, gmk
                else:
                    gmvs[...] += gmv
                    gmks[...] += gmk
                blocks.append(((dq + nn(gms, mk)) * SCORE_SCALE).astype(BF16))
            small[i, 8 + 2 * g:9 + 2 * g] = grad0
            small[i, 9 + 2 * g:10 + 2 * g] = grad1
            gqs.append(jnp.concatenate(blocks, axis=0))
            gks.append((dks[...] * SCORE_SCALE).astype(BF16))
            gvs.append(dvs[...].astype(BF16))
            gmk_all.append((gmks[...] * SCORE_SCALE).astype(BF16))
            gmv_all.append(gmvs[...].astype(BF16))
            for when, move in hooks:
                if when[1] == g:
                    @pl.when(i == when[0])
                    def _(move=move):
                        move()

        gq4, gk4, gv4, gmk4, gmv4 = (jnp.concatenate(p, axis=1) for p in (gqs, gks, gvs, gmk_all, gmv_all))

        @pl.when(i == 2)
        def _():
            swap_att(0).sent()

        def store(kind, value):
            gbuf[slot, :, :, kind] = value.reshape(2, 2, 4, ROWS, D)

        store(0, tn(gq4, n12[...]))
        store(1, tn(gk4, n12[...]) + tn(gmk4, coeffs[...]))
        store(2, tn(gv4, n12[...]) + tn(gmv4, coeffs[...]))
        store(3, tn(context[i], gbranch[...]))

        @pl.when(i > 0)
        def _():
            pl.semaphore_wait(credita, 1)

        swap_att(i).start()
        small[i, 6:7] = column_sum(gq4.astype(F32))
        small[i, 7:8] = column_sum(gv4.astype(F32))
        acc[...] += nn(gq4, weight(0)) + nn(gk4, weight(1)) + nn(gv4, weight(2))

        @pl.when(i == 0)
        def _():
            load_att(2, 0).start()

        return carry

    lax.fori_loop(0, PARTS, group, 0)
    def norm_one(i, carry):
        rows = pl.ds(i * CHUNK, CHUNK)
        grad = acc[rows]
        values, inverse = normalize(x[rows].astype(F32))
        gbranch[rows] = (hidden[rows] + norm_back(grad, values, inverse, ln_gain[0:1])).astype(BF16)
        put(0, column_sum(grad * values))
        put(2, column_sum(grad))
        return carry

    lax.fori_loop(0, SEG // CHUNK, norm_one, 0)
    att.first(2, own_att(2))
    gin_moves = Spread(gbranch, gin_all, 3)
    gin_moves.start()
    gin_moves.send(0)
    gin_moves.send(1)

    def small_stage(stage, place, at, count):
        made = []
        for k in range(1, count):
            made.append(links.add(
                lambda: slots.at[stage, place], lambda: slots.at[stage, place],
                lambda k=k: at(lax.rem(place + k, count)),
                lambda k=k: slots.at[stage, lax.rem(place + count - k, count)]))
        for link in made:
            link.start()
        return made

    def small_sum(made, stage, count):
        for link in made:
            link.wait()
        value = slots[stage, 0]
        for k in range(1, count):
            value = value + slots[stage, k]
        return value

    slots[0, me.c] = small[...]
    made = small_stage(0, me.c, lambda p: me.at(c=p), 2)
    a[1].fourth()
    slots[1, me.x] = small_sum(made, 0, 2)
    made = small_stage(1, me.x, lambda p: me.at(x=p), 4)
    a[1].fifth()
    a[2].second()
    slots[2, me.z] = small_sum(made, 1, 4)
    made = small_stage(2, me.z, lambda p: me.at(z=p), 4)
    a[1].sixth()
    a[2].third()
    gin_moves.send(2)
    gin_moves.send(3)
    slots[3, me.y] = small_sum(made, 2, 4)
    made = small_stage(3, me.y, lambda p: me.at(y=p), 4)
    a[2].fourth()
    a[2].fifth()
    a[2].sixth()
    small_total[...] = small_sum(made, 3, 4)
    for i in range(SEG // CHUNK):
        gin_moves.forward(i)
    mixed_moves.finish()
    gin_moves.finish()
    for tail in m + a:
        tail.finish()
    swap_att(1).sent()
    swap_att(2).sent()
    pl.semaphore_wait(creditm, 1)
    pl.semaphore_wait(credita, 1)
    for sums in (mlp, att):
        for part in range(PARTS):
            for half in (0, 1):
                for k in (1, 2, 3):
                    sums.send(part, half, k).sent()
    links.finish()


def tail_scratch(parts, kinds, dtype):
    return [
        pltpu.VMEM((6, parts, 2, kinds, ROWS, LANES), F32),
        pltpu.VMEM((2, 2, parts, kinds, ROWS, LANES), F32),
        pltpu.VMEM((3, parts, kinds, ROWS, LANES), F32),
        pltpu.VMEM((parts, kinds, ROWS, LANES), dtype),
    ]


def sums_scratch(kinds):
    return [
        pltpu.VMEM((2, kinds, 4, 4, ROWS, D), F32),
        pltpu.VMEM((PARTS, 6, 2, kinds, 4, ROWS, LANES), BF16),
        pltpu.VMEM((PARTS, 6, 2, kinds, 4, ROWS, LANES), BF16),
        pltpu.VMEM((PARTS, 2, 2, kinds, 4, ROWS, LANES), F32),
    ]


def shards(inputs, memory, doc_ids, key_valid, sticky_bins, ln_gain, ln_shift, w_qkv, b_qv, w_gauss, w_out, b_out,
           w_fc, b_fc, w_proj, b_proj, cotangent):
    vmem, hbm = pl.BlockSpec(memory_space=pltpu.VMEM), pl.BlockSpec(memory_space=pl.ANY)
    S, V = jax.ShapeDtypeStruct, pltpu.VMEM
    count = 3 * (1 + 12 + 8) + 2 + 6
    watt, wmlp, sall, coeffs, hidden, qs, ks, vs, mks, mvs, lse, context = pl.pallas_call(
        attend_kernel,
        out_shape=(
            S((2, 2, PARTS, 4, 4, ROWS, D), BF16), S((2, 2, PARTS, 2, 4, 4, ROWS, D), BF16), S((4, PARTS, 8, 256), F32),
            S((N, D), BF16), S((SEG, D), F32), S((PARTS, SEG, 256), BF16), S((PARTS, SEG, 256), BF16),
            S((PARTS, SEG, 256), BF16), S((PARTS, N, 256), BF16), S((PARTS, N, 256), BF16), S((PARTS, SEG, 128), F32),
            S((PARTS, SEG, 256), BF16)),
        in_specs=[hbm] + [vmem] * 14,
        out_specs=[hbm] * 3 + [vmem] * 9,
        scratch_shapes=[
            V((2, 2, PARTS, 4, 4, ROWS, D), BF16), V((PARTS, 2, 4, 4, ROWS, D), BF16), V((4, 128, D), BF16),
            V((4, PARTS, 8, 256), F32), V((SEG, D), BF16), V((SEG, 1), F32), V((SEG, SEG), F32),
            V((SEG, D), BF16), V((4, SEG, HD), BF16), V((4, SEG, HD), BF16), V((4, SEG, HD), BF16),
            pltpu.SemaphoreType.DMA((count,)), pltpu.SemaphoreType.DMA((count,)), pltpu.SemaphoreType.DMA((4,))],
        compiler_params=pltpu.CompilerParams(collective_id=1, has_side_effects=True, vmem_limit_bytes=VMEM_LIMIT),
        name="gather_attend",
    )(inputs, memory, doc_ids, key_valid, sticky_bins, ln_gain, ln_shift, w_qkv.transpose(0, 2, 1), b_qv, w_gauss.transpose(1, 0, 2), w_out, b_out,
      w_fc, b_fc, w_proj)

    count = 2 * PARTS * 7 + 2 * PARTS * (6 + 3 + 1 + 12) + 2 * 9 + 10
    tatt, tmlp, small_total, mixed_all, gin_all = pl.pallas_call(
        backward_kernel,
        out_shape=(
            S((PARTS, 1, 4, 4, ROWS, D), F32), S((PARTS, 2, 4, 4, ROWS, D), BF16), S((PARTS, 24, 256), F32),
            S((4, SEG, D), BF16), S((4, SEG, D), BF16)),
        in_specs=[hbm] * 5 + [vmem] * 14,
        out_specs=[hbm, hbm, vmem, hbm, hbm],
        scratch_shapes=[
            V((SEG, D), BF16), V((SEG, D), BF16), V((SEG, 1), F32),
            V((2, 2, 2, 4, 4, ROWS, D), BF16), V((2, 2, 2, 4, 4, ROWS, D), F32),
            V((SEG, D), F32), V((SEG, D), F32), V((SEG, D), F32), V((SEG, D), BF16), V((SEG, D), BF16), V((SEG, D), BF16),
            V((SEG, SEG), F32), V((4, SEG, HD), BF16), V((4, SEG, HD), BF16), V((4, SEG, HD), BF16), V((4, SEG, HD), BF16),
            V((SEG, HD), F32), V((SEG, HD), F32), V((N, HD), F32), V((N, HD), F32)]
        + sums_scratch(2) + sums_scratch(1)
        + tail_scratch(1, 2, BF16) * PARTS + tail_scratch(1, 1, F32) * PARTS
        + [V((PARTS, 24, 256), F32), V((4, 4, PARTS, 24, 256), F32),
           pltpu.SemaphoreType.DMA((count,)), pltpu.SemaphoreType.DMA((count,)),
           pltpu.SemaphoreType.REGULAR, pltpu.SemaphoreType.REGULAR, pltpu.SemaphoreType.DMA((13,))],
        compiler_params=pltpu.CompilerParams(collective_id=2, has_side_effects=True, vmem_limit_bytes=VMEM_LIMIT),
        name="mlp_backward",
    )(inputs, cotangent, hidden, watt, wmlp, coeffs, sall, doc_ids, key_valid, ln_gain, ln_shift, b_proj,
      qs, ks, vs, mks, mvs, lse, context)
    return finish(tatt.reshape(PARTS, 4, HD, D), tmlp.reshape(PARTS, 2, 256, D), small_total, mixed_all, gin_all)


def finish_kernel(tatt, tmlp, small, mixed_in, gin_in, mixed, gin, gain, shift, wqkv, bqv, gauss, wout, bout, wfc, bfc, wproj,
                  bproj):
    at = pl.program_id(0)
    mixed[...] = mixed_in[...]
    gin[...] = gin_in[...].astype(F32)

    @pl.when(at < PARTS)
    def _():
        wfc[...] = tmlp[0, 0].astype(F32).T
        wproj[...] = tmlp[0, 1].astype(F32)

    @pl.when(at == PARTS)
    def _():
        head = lax.axis_index("head")
        for kind in range(3):
            wqkv[kind] = jnp.concatenate([tatt[i, kind] for i in range(PARTS)], axis=0)
        for i in range(PARTS):
            wout[i * HD:(i + 1) * HD] = tatt[i, 3]
        for i in range(PARTS):
            part = slice(i * 256, (i + 1) * 256)
            gain[0:1, part], gain[1:2, part] = small[i, 0:1], small[i, 1:2]
            shift[0:1, part], shift[1:2, part] = small[i, 2:3], small[i, 3:4]
            bout[part], bproj[part] = small[i, 4], small[i, 5]
            value, biases, widths = small[i, 16], small[i, 6:8, 0:HD], small[i, 8:10]
            for g in range(1, 4):
                value = jnp.where(head == g, small[i, 16 + g], value)
                biases = jnp.where(head == g, small[i, 6:8, g * HD:(g + 1) * HD], biases)
                widths = jnp.where(head == g, small[i, 8 + 2 * g:10 + 2 * g], widths)
            bfc[part] = value
            bqv[:, i * HD:(i + 1) * HD] = biases
            gauss[i] = widths


def finish(tatt, tmlp, small, mixed_all, gin_all):
    S = jax.ShapeDtypeStruct
    whole = lambda *shape: pl.BlockSpec(shape, lambda i: (0,) * len(shape))
    part = lambda i: jnp.minimum(i, PARTS - 1)
    segment = pl.BlockSpec((1, SEG, D), lambda i: (i, 0, 0))
    out = pl.pallas_call(
        finish_kernel,
        grid=(4,),
        out_shape=(
            S((4, SEG, D), BF16), S((4, SEG, D), F32), S((2, D), F32), S((2, D), F32), S((3, 192, D), F32), S((2, 192), F32),
            S((3, 2, N), F32), S((192, D), F32), S((D,), F32), S((D, D), F32), S((D,), F32), S((D, D), F32),
            S((D,), F32)),
        in_specs=[whole(PARTS, 4, HD, D), pl.BlockSpec((1, 2, 256, D), lambda i: (part(i), 0, 0, 0)),
                  whole(PARTS, 24, 256), segment, segment],
        out_specs=(
            segment, segment, whole(2, D), whole(2, D), whole(3, 192, D), whole(2, 192), whole(3, 2, N), whole(192, D),
            whole(D), pl.BlockSpec((D, 256), lambda i: (0, part(i))), whole(D),
            pl.BlockSpec((256, D), lambda i: (part(i), 0)), whole(D)),
        compiler_params=pltpu.CompilerParams(vmem_limit_bytes=VMEM_LIMIT),
        name="finish",
    )(tatt, tmlp, small, mixed_all, gin_all)
    out = list(out)
    out[4], out[6] = out[4].transpose(0, 2, 1), out[6].transpose(1, 0, 2)
    return tuple(out)


def solution(mesh):
    return jax.shard_map(
        shards,
        mesh=mesh,
        in_specs=(
            P("dp", None, None),
            P("dp", "head", None),
            P("dp", None),
            P("dp", None),
            P("dp", None),
            P(),
            P(),
            P(None, None, "head"),
            P(None, "head"),
            P(None, "head", None),
            P("head", None),
            P(),
            P(None, "head"),
            P("head"),
            P("head", None),
            P(),
            P("dp", None, None),
        ),
        out_specs=(
            P("dp", None, None),
            P("dp", None, None),
            P(),
            P(),
            P(None, None, "head"),
            P(None, "head"),
            P(None, "head", None),
            P("head", None),
            P(),
            P(None, "head"),
            P("head"),
            P("head", None),
            P(),
        ),
        check_vma=False,
    )
```

```python
from functools import partial

import jax
import jax.numpy as jnp
from jax import lax
from jax.experimental import pallas as pl
from jax.experimental.pallas import tpu as pltpu
from jax.sharding import PartitionSpec as P

MESH = pl.DeviceIdType.MESH
BF16, F32 = jnp.bfloat16, jnp.float32
D, N, HEADS, HD, FF, SEG, HALF = 768, 256, 12, 64, 3072, 512, 256
PARTS, ROWS, LANES = 3, 16, 384
EPSILON = 1e-05
RIDGE_WEIGHT = 0.5
SIGMA_SCALE = 0.01
SCORE_SCALE = 0.125
NEG_FILL = -1e30
GELU_COEFF = 0.7978845608028654
PRECISE = lax.Precision.HIGHEST
VMEM_LIMIT = 60 * 1024 * 1024
BLOCK = 256
CHUNK = 128
BLOCKS = SEG // BLOCK


class Place:
    def __init__(self):
        dp, head = lax.axis_index("dp"), lax.axis_index("head")
        self.head = head
        self.yl = lax.div(dp, 16)
        self.z = lax.rem(lax.div(dp, 4), 4)
        self.x = lax.rem(dp, 4)
        self.yh = lax.div(head, 2)
        self.c = lax.rem(head, 2)
        self.y = self.yh * 2 + self.yl

    def at(self, x=None, z=None, y=None, c=None):
        x = self.x if x is None else x
        z = self.z if z is None else z
        c = self.c if c is None else c
        if y is None:
            yl, yh = self.yl, self.yh
        else:
            yl, yh = lax.rem(y, 2), lax.div(y, 2)
        return (yl * 16 + z * 4 + x, yh * 2 + c)

    def core(self):
        return self.at(c=1 - self.c)

    def ring(self, along_x, k):
        return self.at(x=step(self.x, k)) if along_x else self.at(z=step(self.z, k))


def step(place, by):
    return lax.rem(place + by, 4)


def lanes(half):
    return pl.ds(half * LANES, LANES)


def greet(devices):
    sem = pltpu.get_barrier_semaphore()
    for device in devices:
        pl.semaphore_signal(sem, inc=1, device_id=device, device_id_type=MESH)


def met(devices):
    pl.semaphore_wait(pltpu.get_barrier_semaphore(), len(devices))


class Links:
    def __init__(self, send, recv):
        self.send, self.recv, self.used, self.all = send, recv, 0, []

    def add(self, src, dst, device, arrives):
        link = Link(self, self.used, src, dst, device, arrives)
        self.used += 1
        self.all.append(link)
        return link

    def finish(self):
        for link in self.all:
            if not link.done:
                link.sent()


class Link:
    def __init__(self, links, index, src, dst, device, arrives):
        self.links, self.index, self.done = links, index, False
        self.src, self.dst, self.device, self.arrives = src, dst, device, arrives

    def copy(self, dst):
        return pltpu.make_async_remote_copy(
            src_ref=self.src(), dst_ref=dst, send_sem=self.links.send.at[self.index],
            recv_sem=self.links.recv.at[self.index], device_id=self.device(), device_id_type=MESH)

    def start(self):
        self.copy(self.dst()).start()

    def wait(self):
        self.copy(self.arrives()).wait_recv()

    def sent(self):
        self.copy(self.dst()).wait_send()


class PlaneGather:
    def __init__(self, links, me, view, row, column):
        self.one, self.two = [[], []], [[], []]
        for k in (1, 3, 2):
            back = 4 - k
            self.one[0].append(links.add(
                lambda: view(me.z, me.x, 0), lambda: view(me.z, me.x, 0), lambda k=k: me.ring(True, k),
                lambda back=back: view(me.z, step(me.x, back), 0)))
            self.one[1].append(links.add(
                lambda: view(me.z, me.x, 1), lambda: view(me.z, me.x, 1), lambda k=k: me.ring(False, k),
                lambda back=back: view(step(me.z, back), me.x, 1)))
            self.two[0].append(links.add(
                lambda: row(me.z, 0), lambda: row(me.z, 0), lambda k=k: me.ring(False, k),
                lambda back=back: row(step(me.z, back), 0)))
            self.two[1].append(links.add(
                lambda: column(me.x, 1), lambda: column(me.x, 1), lambda k=k: me.ring(True, k),
                lambda back=back: column(step(me.x, back), 1)))

    def first(self):
        for a, b in zip(*self.one):
            a.start()
            b.start()

    def second(self):
        for half in (0, 1):
            for link in self.one[half]:
                link.wait()
            for link in self.two[half]:
                link.start()

    def finish(self):
        for a, b in zip(*self.two):
            a.wait()
            b.wait()


def nt(a, b):
    return lax.dot_general(a, b, (((1,), (1,)), ((), ())), preferred_element_type=F32)


def nn(a, b):
    return lax.dot_general(a, b, (((1,), (0,)), ((), ())), preferred_element_type=F32)


def tn(a, b):
    return lax.dot_general(a, b, (((0,), (0,)), ((), ())), preferred_element_type=F32)


def normalize(values):
    centred = values - jnp.mean(values, axis=-1, keepdims=True)
    inverse = lax.rsqrt(jnp.mean(centred * centred, axis=-1, keepdims=True) + EPSILON)
    return centred * inverse, inverse


def norm_back(grad, normed, inverse, gain):
    scaled = grad * gain
    return inverse * (scaled - jnp.mean(scaled, axis=-1, keepdims=True)
                      - normed * jnp.mean(scaled * normed, axis=-1, keepdims=True))


def column_sum(values):
    return jnp.sum(values, axis=0, keepdims=True)


def as_column(row):
    return jnp.broadcast_to(row.astype(F32), (8, SEG)).T[:, 0:1]


def mask_bias(doc_row, valid_row):
    doc_row = doc_row.astype(F32)
    doc_col = as_column(doc_row)
    rows = lax.broadcasted_iota(jnp.int32, (SEG, SEG), 0)
    cols = lax.broadcasted_iota(jnp.int32, (SEG, SEG), 1)
    live = (valid_row == 1) | (rows == cols)
    return jnp.where((cols <= rows) & (doc_col == doc_row) & live, 0.0, NEG_FILL)


def gaussian(mem_scores, gauss):
    centre = jax.nn.sigmoid(jnp.sum(mem_scores * gauss[0:1], axis=-1, keepdims=True))
    width = jnp.sum(mem_scores * gauss[1:2], axis=-1, keepdims=True)
    softplus = jnp.maximum(width, 0.0) + jnp.log1p(jnp.exp(-jnp.abs(width)))
    variance = SIGMA_SCALE * softplus + (1.0 / N) ** 2
    places = (lax.broadcasted_iota(jnp.int32, (1, N), 1).astype(F32) + 0.5) / N
    offsets = centre - places
    inverse = 1.0 / variance
    density = (1.0 / N) * lax.rsqrt(variance) * jnp.exp(-0.5 * offsets * offsets * inverse)
    return centre, width, offsets, inverse, density


LOWEST, HIGHEST = RIDGE_WEIGHT, 650.0


def attend_kernel(inputs, memory, doc_ids, key_valid, sticky_bins, ln_gain, ln_shift, w_qkv, b_qv, w_gauss, w_out, b_out,
                  w_fc, b_fc, w_proj,
                  watt_out, wmlp, sall_out, coeffs, hidden, qs, ks, vs, mks, mvs, lse, context,
                  watt, pmlp, mseg, sall, x, gate, bias, n1, hq, hk, hv, send, recv, local):
    me = Place()
    mine = pl.ds(me.head, 1)
    peers = ([me.core(), me.at(y=3 - me.y), me.at(y=step(me.y, 2)), me.at(y=step(me.y, 2), c=1 - me.c)]
             + [me.ring(True, k) for k in (1, 2, 3)] + [me.ring(False, k) for k in (1, 2, 3)])
    greet(peers)
    load_x = pltpu.make_async_copy(inputs.at[me.head], x, local.at[0])
    load_x.start()
    for kind in range(3):
        for i in range(PARTS):
            watt[me.yh, me.c, i, kind] = w_qkv[kind, i * HD:(i + 1) * HD].reshape(4, ROWS, D)
    for i in range(PARTS):
        watt[me.yh, me.c, i, 3] = w_out[i * HD:(i + 1) * HD].reshape(4, ROWS, D)
    mine_small = sall.at[me.head]
    mine_small[...] = jnp.zeros((PARTS, 8, 256), F32)
    for i in range(PARTS):
        mine_small[i, 0:2, 0:HD] = b_qv[:, i * HD:(i + 1) * HD]
        mine_small[i, 2:4] = w_gauss[i]
        mine_small[i, 4:5] = b_fc[i * 256:(i + 1) * 256].reshape(1, 256)
    for i in range(PARTS):
        pmlp[i, 0] = w_fc[:, i * 256:(i + 1) * 256].T.reshape(4, 4, ROWS, D)
        pmlp[i, 1] = w_proj[i * 256:(i + 1) * 256].reshape(4, 4, ROWS, D)
    met(peers)

    links = Links(send, recv)

    class Gather:
        def __init__(self, wall, own, low, high):
            def block(yh, c, z, xx, cut):
                return wall.at[yh, c, low:high, ..., z, xx, :, cut]

            every = slice(None)

            def view(z, xx, half, c=None):
                return block(1 - me.yh, me.c if c is None else c, z, xx, lanes(half))

            def row(z, half, c=None):
                return view(z, every, half, c)

            def column(xx, half, c=None):
                return view(every, xx, half, c)

            self.across = links.add(
                lambda: own().at[low:high, ..., me.z, me.x, :, :], lambda: block(me.yh, me.c, me.z, me.x, every),
                lambda: me.at(y=3 - me.y), lambda: block(1 - me.yh, me.c, me.z, me.x, every))
            self.plane = PlaneGather(links, me, view, row, column)
            self.passed = []
            for k in (0, 1, 3, 2):
                self.passed.append(links.add(
                    lambda k=k: row(step(me.z, k), 0), lambda k=k: row(step(me.z, k), 0), me.core,
                    lambda k=k: row(step(me.z, k), 0, 1 - me.c)))
                self.passed.append(links.add(
                    lambda k=k: column(step(me.x, k), 1), lambda k=k: column(step(me.x, k), 1), me.core,
                    lambda k=k: column(step(me.x, k), 1, 1 - me.c)))

        def first(self):
            self.across.wait()
            self.plane.first()

        def second(self):
            self.plane.second()
            self.passed[0].start()
            self.passed[1].start()

        def third(self):
            self.plane.finish()
            for link in self.passed[2:]:
                link.start()

        def ready(self):
            for link in self.passed:
                link.wait()

    own_att = lambda: watt.at[me.yh, me.c]
    own_mlp = lambda: pmlp
    early, late = Gather(watt, own_att, 0, 1), Gather(watt, own_att, 1, PARTS)
    units = Gather(wmlp, own_mlp, 0, PARTS)
    swap_att = links.add(own_att, own_att, me.core, lambda: watt.at[me.yh, 1 - me.c])
    swap_mlp = links.add(own_mlp, lambda: wmlp.at[me.yh, me.c], me.core, lambda: wmlp.at[me.yh, 1 - me.c])
    sent, sent_small = [], []
    for k in (1, 2, 3):
        def other(k=k):
            return lax.rem(me.head + k, 4)

        def device(k=k):
            return (me.yl * 16 + me.z * 4 + me.x, lax.rem(me.head + k, 4))

        def before(k=k):
            return lax.rem(me.head + (4 - k), 4)

        sent.append(links.add(lambda other=other: memory.at[other()], lambda: mseg.at[me.head], device,
                              lambda before=before: mseg.at[before()]))
        sent_small.append(links.add(lambda: sall.at[me.head], lambda: sall.at[me.head], device,
                                    lambda before=before: sall.at[before()]))
    early.across.start()
    late.across.start()
    units.across.start()
    for link in sent:
        link.start()
    swap_att.start()
    for link in sent_small:
        link.start()
    swap_mlp.start()
    keep_mlp = pltpu.make_async_copy(pmlp, wmlp.at[me.yh, me.c], local.at[1])
    keep_mlp.start()
    mseg[mine] = memory[mine]
    early.first()
    load_x.wait()
    values, _ = normalize(x[...].astype(F32))
    n1[...] = (values * ln_gain[0:1] + ln_shift[0:1]).astype(BF16)
    hidden[...] = x[...].astype(F32) + b_out[...]
    late.first()

    dot = partial(jnp.dot, preferred_element_type=F32, precision=PRECISE)
    rows = lax.broadcasted_iota(jnp.int32, (N, N), 0)
    cols = lax.broadcasted_iota(jnp.int32, (N, N), 1)
    gap = (rows - cols).astype(F32)
    curve = jnp.exp(-0.5 * gap * gap)
    eye = (rows == cols).astype(F32)
    picked = (sticky_bins[mine] == rows).astype(F32)
    counts = 1.0 + jnp.sum(picked, axis=1, keepdims=True)
    gram = dot(curve, counts * curve) + RIDGE_WEIGHT * eye

    def newton(count, state):
        def body(_, state):
            inverse, gap = state
            scale = 2.0 / (2.0 - gap * gap)
            inverse = scale * (2.0 * inverse - dot(inverse, dot(gram, inverse)))
            return inverse, gap * gap / (2.0 - gap * gap)

        return lax.fori_loop(0, count, body, state)

    state = ((2.0 / (LOWEST + HIGHEST)) * eye, jnp.float32((HIGHEST - LOWEST) / (HIGHEST + LOWEST)))
    early.second()
    state = newton(2, state)
    late.second()
    units.first()
    state = newton(2, state)
    early.third()
    state = newton(3, state)
    late.third()
    units.second()
    inverse, _ = newton(3, state)
    docs = doc_ids[mine]
    bias[...] = mask_bias(docs, key_valid[mine])
    gate[...] = (as_column(docs) == docs[:, 0:1].astype(F32)).astype(F32)
    for link in sent:
        link.wait()
    first_half = mseg[0:2].reshape(HALF, D).astype(F32)
    held = first_half + jnp.dot(picked.astype(BF16), mseg[2:4].reshape(HALF, D), preferred_element_type=F32)
    coeffs[...] = dot(inverse, dot(curve, held)).astype(BF16)
    swap_att.wait()
    early.ready()
    for link in sent_small:
        link.wait()
    out = [pltpu.make_async_copy(watt, watt_out, local.at[2]), pltpu.make_async_copy(sall, sall_out, local.at[3])]
    hooks = (((1, 0), units.third),)

    def group(i, carry):
        def weight(kind):
            return watt[:, :, i, kind].reshape(4 * HD, D)

        def heads_row(r):
            return jnp.concatenate([sall[g, i, r:r + 1, 0:HD] for g in range(4)], axis=1)

        @pl.when(i == 1)
        def _():
            late.ready()
            for copy in out:
                copy.start()

        q4 = (nt(n1[...], weight(0)) + heads_row(0)).astype(BF16)
        k4 = nt(n1[...], weight(1)).astype(BF16)
        v4 = (nt(n1[...], weight(2)) + heads_row(1)).astype(BF16)
        mk4 = nt(coeffs[...], weight(1)).astype(BF16)
        mv4 = nt(coeffs[...], weight(2)).astype(BF16)
        qs[i], ks[i], vs[i], mks[i], mvs[i] = q4, k4, v4, mk4, mv4
        for g in range(4):
            part = slice(g * HD, (g + 1) * HD)
            hq[g], hk[g], hv[g] = q4[:, part], k4[:, part], v4[:, part]
        parts = []
        for g in range(4):
            part = slice(g * HD, (g + 1) * HD)
            mk, mv = mk4[:, part], mv4[:, part]
            blocks = []
            for r in range(BLOCKS):
                rows, cols = slice(r * BLOCK, (r + 1) * BLOCK), slice(0, (r + 1) * BLOCK)
                q = hq[g, rows]
                scores = nt(q, hk[g, cols]) * SCORE_SCALE + bias[rows, cols]
                top = jnp.max(scores, axis=-1, keepdims=True)
                weights = jnp.exp(scores - top)
                total = jnp.sum(weights, axis=-1, keepdims=True)
                lse[i, rows, g:g + 1] = top + jnp.log(total)
                probs = (weights * (1.0 / total)).astype(BF16)
                attended = nn(probs, hv[g, cols])
                mem_scores = nt(q, mk) * SCORE_SCALE
                density = gaussian(mem_scores, sall[g, i, 2:4])[-1].astype(BF16)
                blocks.append((attended + gate[rows] * nn(density, mv)).astype(BF16))
            parts.append(jnp.concatenate(blocks, axis=0))
            for when, move in hooks:
                if when[1] == g:
                    @pl.when(i == when[0])
                    def _(move=move):
                        move()

        mixed = jnp.concatenate(parts, axis=1)
        context[i] = mixed
        hidden[...] += nn(mixed, weight(3))

        return carry

    lax.fori_loop(0, PARTS, group, 0)
    swap_mlp.wait()
    units.ready()
    keep_mlp.wait()
    for copy in out:
        copy.wait()
    links.finish()


class Sums:
    def __init__(self, links, me, kinds, other, sbuf, rbuf, kept, credit):
        self.links, self.me, self.kinds = links, me, kinds
        self.other, self.sbuf, self.rbuf, self.kept, self.credit = other, sbuf, rbuf, kept, credit
        self.base = links.used
        links.used += PARTS * 7

    def swap(self, part, src):
        return Link(self.links, self.base + part, src, lambda: self.other, self.me.core, lambda: self.other)

    def send(self, part, half, k):
        i = half * 3 + k - 1
        return Link(self.links, self.base + PARTS + part * 6 + i, lambda: self.sbuf.at[part, i],
                    lambda: self.rbuf.at[part, i], lambda: self.me.ring(half == 0, k), lambda: self.rbuf.at[part, i])

    def first(self, part, own):
        me = self.me
        self.swap(part, lambda: self.other).wait()
        for k in (2, 1, 3, 0):
            for half in (0, 1):
                def body(i, carry, half=half, k=k):
                    t, kind = lax.div(i, self.kinds), lax.rem(i, self.kinds)
                    for q in range(4):
                        z, x = (q, step(me.x, k)) if half == 0 else (step(me.z, k), q)
                        cut = slice(half * LANES, (half + 1) * LANES)
                        value = own(t, kind, z, x, cut) + self.other[t, kind, z, x, :, cut]
                        if k == 0:
                            self.kept[part, half, t, kind, q] = value
                        else:
                            self.sbuf[part, half * 3 + k - 1, t, kind, q] = value.astype(BF16)
                    return carry

                lax.fori_loop(0, 2 * self.kinds, body, 0)
                if k:
                    self.send(part, half, k).start()
        pl.semaphore_signal(self.credit, inc=1, device_id=me.core(), device_id_type=MESH)


class Tail:
    def __init__(self, links, me, sums, low, high, total, rbuf2, ylocal, ybuf, final, local):
        self.me, self.sums, self.low, self.high, self.total = me, sums, low, high, total
        self.rbuf2, self.ylocal, self.ybuf, self.final, self.local = rbuf2, ylocal, ybuf, final, local
        kept = sums.kept
        self.two = {}
        for half in (0, 1):
            across = (lambda: me.z) if half == 0 else (lambda: me.x)
            for k in (2, 1, 3):
                i = half * 3 + k - 1
                self.two[half, k] = links.add(
                    lambda half=half, k=k, across=across: kept.at[low:high, half, :, :, step(across(), k)],
                    lambda i=i: rbuf2.at[i], lambda half=half, k=k: me.ring(half == 1, k), lambda i=i: rbuf2.at[i])
        self.three = []
        for k in (2, 1, 3):
            def target(k=k):
                return step(me.y, k)

            self.three.append(links.add(
                lambda target=target: ylocal.at[lax.div(target(), 2), lax.rem(target(), 2)],
                lambda k=k: ybuf.at[k - 1], lambda target=target: me.at(y=target()), lambda k=k: ybuf.at[k - 1]))

        def view(z, x, half):
            return total.at[low:high, :, z, x, :, lanes(half)]

        def row(z, half):
            return total.at[low:high, :, z, :, :, lanes(half)]

        def column(x, half):
            return total.at[low:high, :, :, x, :, lanes(half)]

        self.view = view
        self.mate = links.add(lambda: final, lambda: view(me.z, me.x, me.yl),
                              lambda: me.at(y=me.yh * 2 + 1 - me.yl), lambda: view(me.z, me.x, 1 - me.yl))
        self.gather = PlaneGather(links, me, view, row, column)

    def second(self):
        sums, kept = self.sums, self.sums.kept
        for half in (0, 1):
            for part in range(self.low, self.high):
                for k in (1, 2, 3):
                    sums.send(part, half, k).wait()

                def body(i, carry, half=half, part=part):
                    t, kind = lax.div(i, sums.kinds), lax.rem(i, sums.kinds)
                    value = kept[part, half, t, kind]
                    for k in (1, 2, 3):
                        value = value + sums.rbuf[part, half * 3 + k - 1, t, kind].astype(F32)
                    kept[part, half, t, kind] = value
                    return carry

                lax.fori_loop(0, 2 * sums.kinds, body, 0)
            for k in (2, 1, 3):
                self.two[half, k].start()

    def third(self):
        me, kept = self.me, self.sums.kept
        for half in (0, 1):
            for k in (1, 2, 3):
                self.two[half, k].wait()
            across = me.z if half == 0 else me.x
            for p in range(self.low, self.high):
                for t in (0, 1):
                    value = kept[p, half, t, :, across]
                    for k in (1, 2, 3):
                        value = value + self.rbuf2[half * 3 + k - 1, p - self.low, t]
                    self.ylocal[t, half, p - self.low] = value
        for link in self.three:
            link.start()

    def keep(self):
        return pltpu.make_async_copy(self.final, self.view(self.me.z, self.me.x, self.me.yl), self.local)

    def fourth(self):
        me = self.me
        for link in self.three:
            link.wait()
        self.final[...] = (self.ylocal[me.yh, me.yl] + self.ybuf[0] + self.ybuf[1] + self.ybuf[2]).astype(
            self.final.dtype)
        self.keep().start()
        self.mate.start()

    def fifth(self):
        self.keep().wait()
        self.mate.wait()
        self.gather.first()

    def sixth(self):
        self.gather.second()

    def finish(self):
        self.gather.finish()


class TailY:
    def __init__(self, links, me, sums, part, total, ybuf, rbuf2, final, local):
        self.me, self.sums, self.part, self.total = me, sums, part, total
        self.ybuf, self.rbuf2, self.final, self.local = ybuf, rbuf2, final, local
        kept = sums.kept
        self.two, self.three = [], []
        for k in (2, 1, 3):
            def target(k=k):
                return step(me.y, k)

            self.two.append(links.add(
                lambda target=target: kept.at[part, lax.rem(target(), 2), lax.div(target(), 2)],
                lambda k=k: ybuf.at[k - 1], lambda target=target: me.at(y=target()), lambda k=k: ybuf.at[k - 1]))

        def peer(k):
            return me.at(x=step(me.x, k * me.yl), z=step(me.z, k * (1 - me.yl)))

        for k in (2, 1, 3):
            self.three.append(links.add(
                lambda k=k: kept.at[part, me.yl, me.yh, :, step(self.across(), k)],
                lambda k=k: rbuf2.at[k - 1], lambda k=k: peer(k), lambda k=k: rbuf2.at[k - 1]))

        def view(z, x, half):
            return total.at[part, :, z, x, :, lanes(half)]

        def row(z, half):
            return total.at[part, :, z, :, :, lanes(half)]

        def column(x, half):
            return total.at[part, :, :, x, :, lanes(half)]

        self.view = view
        self.mate = links.add(lambda: final, lambda: view(me.z, me.x, me.yl),
                              lambda: me.at(y=me.yh * 2 + 1 - me.yl), lambda: view(me.z, me.x, 1 - me.yl))
        self.gather = PlaneGather(links, me, view, row, column)

    def across(self):
        return self.me.z * (1 - self.me.yl) + self.me.x * self.me.yl

    def second(self):
        sums, kept, part = self.sums, self.sums.kept, self.part
        for half in (0, 1):
            for k in (1, 2, 3):
                sums.send(part, half, k).wait()

            def body(i, carry, half=half):
                t, kind = lax.div(i, sums.kinds), lax.rem(i, sums.kinds)
                value = kept[part, half, t, kind]
                for k in (1, 2, 3):
                    value = value + sums.rbuf[part, half * 3 + k - 1, t, kind].astype(F32)
                kept[part, half, t, kind] = value
                return carry

            lax.fori_loop(0, 2 * sums.kinds, body, 0)
        for link in self.two:
            link.start()

    def third(self):
        me, kept, part = self.me, self.sums.kept, self.part
        for link in self.two:
            link.wait()
        for kind in range(self.sums.kinds):
            value = kept[part, me.yl, me.yh, kind]
            for k in range(3):
                value = value + self.ybuf[k, kind]
            kept[part, me.yl, me.yh, kind] = value
        for link in self.three:
            link.start()

    def keep(self):
        return pltpu.make_async_copy(self.final, self.view(self.me.z, self.me.x, self.me.yl), self.local)

    def fourth(self):
        me, kept, part = self.me, self.sums.kept, self.part
        for link in self.three:
            link.wait()
        self.final[...] = (kept[part, me.yl, me.yh, :, self.across()] + self.rbuf2[0] + self.rbuf2[1]
                           + self.rbuf2[2]).astype(self.final.dtype)
        self.keep().start()
        self.mate.start()

    def fifth(self):
        self.keep().wait()
        self.mate.wait()
        self.gather.first()

    def sixth(self):
        self.gather.second()

    def finish(self):
        self.gather.finish()


def backward_kernel(inputs, cotangent, hidden_in, watt, wmlp, coeffs, sall, doc_ids, key_valid, ln_gain, ln_shift, b_proj,
                    qs, ks, vs, mks, mvs, lse, context,
                    tatt, tmlp, small_total, mixed_all, gin_all,
                    x, cot, gate, wbuf, gbuf, hidden, acc, gnorm, n12, gbranch, mixed, bias, hq, hk, hv, gcs,
                    otherm, sbufm, rbufm, keptm, othera, sbufa, rbufa, kepta,
                    *rest):
    tails_m, tails_a, (small, slots, send, recv, creditm, credita, local) = rest[:9], rest[9:21], rest[21:]
    me = Place()
    peers = ([me.core()] + [me.ring(True, k) for k in (1, 2, 3)] + [me.ring(False, k) for k in (1, 2, 3)]
             + [me.at(y=step(me.y, k)) for k in (1, 2, 3)])
    greet(peers)
    links = Links(send, recv)
    mlp = Sums(links, me, 2, otherm, sbufm, rbufm, keptm, creditm)
    att = Sums(links, me, 1, othera, sbufa, rbufa, kepta, credita)
    m = [TailY(links, me, mlp, p, tmlp, *tails_m[3 * p:3 * p + 3], local.at[4 + p]) for p in range(PARTS)]
    a = [Tail(links, me, att, p, p + 1, tatt, *tails_a[4 * p:4 * p + 4], local.at[7 + p]) for p in range(PARTS)]

    def load(index, slot):
        part, mine = lax.div(index, 2), lax.rem(index, 2)
        owner = mine * me.c + (1 - mine) * (1 - me.c)
        return pltpu.make_async_copy(wmlp.at[:, owner, part], wbuf.at[slot], local.at[slot])

    def load_att(part, slot):
        return pltpu.make_async_copy(watt.at[:, :, part], wbuf.at[slot], local.at[slot])

    load_hidden = pltpu.make_async_copy(hidden_in, hidden, local.at[12])
    load_hidden.start()
    load_cot = pltpu.make_async_copy(cotangent.at[me.head], cot, local.at[10])
    load_cot.start()
    load(0, 0).start()
    load(1, 1).start()
    load_x = pltpu.make_async_copy(inputs.at[me.head], x, local.at[11])
    load_x.start()
    load_hidden.wait()

    def start_mlp(i, carry):
        rows = pl.ds(i * CHUNK, CHUNK)
        values, _ = normalize(hidden[rows])
        n12[rows] = (values * ln_gain[1:2] + ln_shift[1:2]).astype(BF16)
        acc[rows] = hidden[rows] + b_proj[...]
        return carry

    lax.fori_loop(0, SEG // CHUNK, start_mlp, 0)
    load_cot.wait()
    load_x.wait()
    gnorm[...] = jnp.zeros_like(gnorm)
    small[...] = jnp.zeros_like(small)
    met(peers)

    def own_mlp(t, kind, z, xx, cut):
        return gbuf[1, t, kind, z, xx, :, cut]

    def swap_mlp(part):
        return mlp.swap(part, lambda: gbuf.at[0])

    def units(index, carry):
        part, mine = lax.div(index, 2), lax.rem(index, 2)
        owner = mine * me.c + (1 - mine) * (1 - me.c)
        load(index, mine).wait()

        @pl.when((mine == 0) & (part > 0))
        def _():
            mlp.first(part - 1, own_mlp)
            swap_mlp(part - 1).sent()

        @pl.when(index == 5)
        def _():
            m[0].second()

        wfc = wbuf[mine, :, 0].reshape(512, D)
        wproj = wbuf[mine, :, 1].reshape(512, D)
        bias_fc = jnp.concatenate([sall[owner, part, 4:5], sall[2 + owner, part, 4:5]], axis=1)
        pre = nt(n12[...], wfc) + bias_fc
        inner = jnp.tanh(GELU_COEFF * (pre + 0.044715 * pre * pre * pre))
        activation = (0.5 * pre * (1.0 + inner)).astype(BF16)
        slope = 0.5 * (1.0 + inner) + (0.5 * GELU_COEFF) * pre * (1.0 - inner * inner) * (
            1.0 + 3.0 * 0.044715 * pre * pre)
        acc[...] += nn(activation, wproj)
        gpre = (nt(cot[...], wproj) * slope).astype(BF16)
        units_sum = column_sum(gpre.astype(F32))
        small[part, pl.ds(16 + owner, 1)] = units_sum[:, 0:256]
        small[part, pl.ds(18 + owner, 1)] = units_sum[:, 256:512]
        gnorm[...] += nn(gpre, wfc)
        gbuf[mine, :, 0] = tn(gpre, n12[...]).reshape(2, 4, 4, ROWS, D)
        gbuf[mine, :, 1] = tn(activation, cot[...]).reshape(2, 4, 4, ROWS, D)

        @pl.when(mine == 0)
        def _():
            @pl.when(part > 0)
            def _():
                pl.semaphore_wait(creditm, 1)

            swap_mlp(part).start()

        @pl.when(index < 4)
        def _():
            load(index + 2, mine).start()

        return carry

    lax.fori_loop(0, 6, units, 0)
    load_att(0, 0).start()
    load_att(1, 1).start()
    mlp.first(2, own_mlp)
    swap_mlp(2).sent()
    mixed[...] = acc[...].astype(BF16)
    far_head = (1 - me.yh) * 2 + me.c
    mate, far_mate = me.yh * 2 + 1 - me.c, (1 - me.yh) * 2 + 1 - me.c

    class Spread:
        def __init__(self, block, everywhere, slot):
            self.keep = pltpu.make_async_copy(block, everywhere.at[me.head], local.at[slot])
            self.near = links.add(lambda: block, lambda: everywhere.at[me.head], me.core, lambda: everywhere.at[mate])
            self.far, self.passed = [], []
            for i in range(SEG // CHUNK):
                rows = pl.ds(i * CHUNK, CHUNK)
                self.far.append(links.add(
                    lambda rows=rows: block.at[rows], lambda rows=rows: everywhere.at[me.head, rows],
                    lambda: me.at(y=step(me.y, 2)), lambda rows=rows: everywhere.at[far_head, rows]))
                self.passed.append(links.add(
                    lambda rows=rows: everywhere.at[far_head, rows], lambda rows=rows: everywhere.at[far_head, rows],
                    me.core, lambda rows=rows: everywhere.at[far_mate, rows]))

        def start(self):
            self.keep.start()
            self.near.start()

        def send(self, i):
            self.far[i].start()

        def forward(self, i):
            self.far[i].wait()
            self.passed[i].start()

        def finish(self):
            self.keep.wait()
            self.near.wait()
            for link in self.passed:
                link.wait()

    mixed_moves = Spread(mixed, mixed_all, 2)
    mixed_moves.start()

    def put(row, vector):
        for i in range(3):
            small[i, row:row + 1] += vector[:, i * 256:(i + 1) * 256]

    def norm_two(i, carry):
        rows = pl.ds(i * CHUNK, CHUNK)
        values, inverse = normalize(hidden[rows])
        grad = gnorm[rows]
        cotangent = cot[rows].astype(F32)
        total = cotangent + norm_back(grad, values, inverse, ln_gain[1:2])
        hidden[rows] = total
        gbranch[rows] = total.astype(BF16)
        put(1, column_sum(grad * values))
        put(3, column_sum(grad))
        put(4, column_sum(total))
        put(5, column_sum(cotangent))
        values, _ = normalize(x[rows].astype(F32))
        n12[rows] = (values * ln_gain[0:1] + ln_shift[0:1]).astype(BF16)
        return carry

    lax.fori_loop(0, SEG // CHUNK, norm_two, 0)
    docs = doc_ids[pl.ds(me.head, 1)]
    bias[...] = mask_bias(docs, key_valid[pl.ds(me.head, 1)])
    gate[...] = (as_column(docs) == docs[:, 0:1].astype(F32)).astype(F32)
    acc[...] = jnp.zeros_like(acc)

    def own_att(part):
        slot = lax.rem(part, 2)
        return lambda t, kind, z, xx, cut: gbuf[slot, t, me.c, z, xx, :, cut]

    def swap_att(part):
        slot = lax.rem(part, 2)
        return att.swap(part, lambda: gbuf.at[slot, :, pl.ds(1 - me.c, 1)])

    hooks = (
        ((0, 2), m[1].second), ((0, 3), m[0].third), ((1, 0), m[0].fourth), ((1, 1), m[0].fifth),
        ((1, 1), partial(mixed_moves.send, 0)),
        ((1, 2), m[2].second), ((1, 2), m[1].third), ((1, 3), m[1].fourth), ((1, 3), m[0].sixth), ((2, 0), m[1].fifth),
        ((2, 0), partial(mixed_moves.send, 1)), ((2, 1), a[0].second), ((2, 1), m[2].third),
        ((2, 1), partial(mixed_moves.send, 2)),
        ((2, 2), m[2].fourth), ((2, 2), m[1].sixth), ((2, 3), m[2].fifth), ((2, 3), partial(mixed_moves.send, 3)),
        ((2, 3), partial(mixed_moves.forward, 0)))

    def group(i, carry):
        slot = lax.rem(i, 2)
        load_att(i, slot).wait()

        def weight(kind):
            return wbuf[slot, :, :, kind].reshape(4 * HD, D)

        q4, k4, v4, mk4, mv4 = qs[i], ks[i], vs[i], mks[i], mvs[i]
        gc4 = nt(gbranch[...], weight(3)).astype(BF16)
        gc4t = nt(weight(3), gbranch[...]).astype(BF16)
        q4t = q4.T
        gate_row = (docs == docs[:, 0:1]).astype(BF16)
        for g in range(4):
            part = slice(g * HD, (g + 1) * HD)
            hq[g], hk[g], hv[g], gcs[g] = q4[:, part], k4[:, part], v4[:, part], gc4[:, part]

        @pl.when(i > 0)
        def _():
            att.first(i - 1, own_att(i - 1))

        gqs, gks, gvs, gmk_all, gmv_all = [], [], [], [], []
        for g in range(4):
            part = slice(g * HD, (g + 1) * HD)
            mk, mv = mk4[:, part], mv4[:, part]
            gct, qt = gc4t[part], q4t[part]
            grect = gct * gate_row
            gauss = sall[g, i, 2:4]
            blocks = []
            grad0 = jnp.zeros((1, N), F32)
            grad1 = jnp.zeros((1, N), F32)
            for r in range(BLOCKS):
                rows, cols = slice(r * BLOCK, (r + 1) * BLOCK), slice(0, (r + 1) * BLOCK)
                q, gc = hq[g, rows], gcs[g, rows]
                k, v = hk[g, cols], hv[g, cols]
                scores = nt(q, k) * SCORE_SCALE + bias[rows, cols]
                probs = jnp.exp(scores - lse[i, rows, g:g + 1])
                gprobs = nt(gc, v)
                inner = jnp.sum(probs * gprobs, axis=-1, keepdims=True)
                gscores = (probs * (gprobs - inner)).astype(BF16)
                dv = nn(gct[:, rows], probs.astype(BF16))
                dk = nn(qt[:, rows], gscores)
                if r:
                    dv = jnp.concatenate([dv[:, :r * BLOCK] + dvs, dv[:, r * BLOCK:]], axis=1)
                    dk = jnp.concatenate([dk[:, :r * BLOCK] + dks, dk[:, r * BLOCK:]], axis=1)
                dvs, dks = dv, dk
                dq = nn(gscores, k)
                mem_scores = nt(q, mk) * SCORE_SCALE
                centre, width, offsets, inv, density = gaussian(mem_scores, gauss)
                grec = (gc.astype(F32) * gate[rows]).astype(BF16)
                gdens = nt(grec, mv) * density
                ratio = offsets * inv
                gcentre = -jnp.sum(gdens * ratio, axis=-1, keepdims=True)
                gvar = 0.5 * jnp.sum(gdens * (ratio * ratio - inv), axis=-1, keepdims=True)
                gcl = gcentre * (centre * (1.0 - centre))
                gwl = gvar * (SIGMA_SCALE * jax.nn.sigmoid(width))
                grad0 = grad0 + column_sum(gcl * mem_scores)
                grad1 = grad1 + column_sum(gwl * mem_scores)
                gms = (gcl * gauss[0:1] + gwl * gauss[1:2]).astype(BF16)
                gmv = nn(grect[:, rows], density.astype(BF16))
                gmk = nn(qt[:, rows], gms)
                gmvs, gmks = (gmv, gmk) if r == 0 else (gmvs + gmv, gmks + gmk)
                blocks.append(((dq + nn(gms, mk)) * SCORE_SCALE).astype(BF16))
            small[i, 8 + 2 * g:9 + 2 * g] = grad0
            small[i, 9 + 2 * g:10 + 2 * g] = grad1
            gqs.append(jnp.concatenate(blocks, axis=0))
            gks.append((dks * SCORE_SCALE).astype(BF16))
            gvs.append(dvs.astype(BF16))
            gmk_all.append((gmks * SCORE_SCALE).astype(BF16))
            gmv_all.append(gmvs.astype(BF16))
            for when, move in hooks:
                if when[1] == g:
                    @pl.when(i == when[0])
                    def _(move=move):
                        move()

        gq4 = jnp.concatenate(gqs, axis=1)
        gk4t, gv4t, gmk4t, gmv4t = (jnp.concatenate(p, axis=0) for p in (gks, gvs, gmk_all, gmv_all))

        @pl.when(i == 2)
        def _():
            swap_att(0).sent()

        def store(kind, value):
            gbuf[slot, :, :, kind] = value.reshape(2, 2, 4, ROWS, D)

        store(0, tn(gq4, n12[...]))
        store(1, nn(gk4t, n12[...]) + nn(gmk4t, coeffs[...]))
        store(2, nn(gv4t, n12[...]) + nn(gmv4t, coeffs[...]))
        store(3, tn(context[i], gbranch[...]))

        @pl.when(i > 0)
        def _():
            pl.semaphore_wait(credita, 1)

        swap_att(i).start()
        small[i, 6:7] = column_sum(gq4.astype(F32))
        gk4, gv4 = gk4t.T, gv4t.T
        small[i, 7:8] = column_sum(gv4.astype(F32))
        acc[...] += nn(gq4, weight(0)) + nn(gk4, weight(1)) + nn(gv4, weight(2))

        @pl.when(i == 0)
        def _():
            load_att(2, 0).start()

        return carry

    lax.fori_loop(0, PARTS, group, 0)
    att.first(2, own_att(2))
    a[0].third()
    a[1].second()
    m[2].sixth()

    def norm_one(i, carry):
        rows = pl.ds(i * CHUNK, CHUNK)
        grad = acc[rows]
        values, inverse = normalize(x[rows].astype(F32))
        gbranch[rows] = (hidden[rows] + norm_back(grad, values, inverse, ln_gain[0:1])).astype(BF16)
        put(0, column_sum(grad * values))
        put(2, column_sum(grad))
        return carry

    lax.fori_loop(0, SEG // CHUNK, norm_one, 0)
    a[0].fourth()
    a[1].third()
    gin_moves = Spread(gbranch, gin_all, 3)
    gin_moves.start()
    gin_moves.send(0)
    gin_moves.send(1)
    mixed_moves.forward(1)
    mixed_moves.forward(2)
    a[0].fifth()

    def small_stage(stage, place, at, count):
        made = []
        for k in range(1, count):
            made.append(links.add(
                lambda: slots.at[stage, place], lambda: slots.at[stage, place],
                lambda k=k: at(lax.rem(place + k, count)),
                lambda k=k: slots.at[stage, lax.rem(place + count - k, count)]))
        for link in made:
            link.start()
        return made

    def small_sum(made, stage, count):
        for link in made:
            link.wait()
        value = slots[stage, 0]
        for k in range(1, count):
            value = value + slots[stage, k]
        return value

    slots[0, me.c] = small[...]
    made = small_stage(0, me.c, lambda p: me.at(c=p), 2)
    a[2].second()
    a[1].fourth()
    a[0].sixth()
    slots[1, me.x] = small_sum(made, 0, 2)
    made = small_stage(1, me.x, lambda p: me.at(x=p), 4)
    a[1].fifth()
    a[2].third()
    gin_moves.send(2)
    gin_moves.send(3)
    mixed_moves.forward(3)
    slots[2, me.z] = small_sum(made, 1, 4)
    made = small_stage(2, me.z, lambda p: me.at(z=p), 4)
    a[1].sixth()
    a[2].fourth()
    slots[3, me.y] = small_sum(made, 2, 4)
    made = small_stage(3, me.y, lambda p: me.at(y=p), 4)
    a[2].fifth()
    a[2].sixth()
    small_total[...] = small_sum(made, 3, 4)
    for i in range(SEG // CHUNK):
        gin_moves.forward(i)
    mixed_moves.finish()
    gin_moves.finish()
    for tail in m + a:
        tail.finish()
    swap_att(1).sent()
    swap_att(2).sent()
    pl.semaphore_wait(creditm, 1)
    pl.semaphore_wait(credita, 1)
    for sums in (mlp, att):
        for part in range(PARTS):
            for half in (0, 1):
                for k in (1, 2, 3):
                    sums.send(part, half, k).sent()
    links.finish()


def tail_y_scratch(kinds, dtype):
    return [
        pltpu.VMEM((3, kinds, 4, ROWS, LANES), F32),
        pltpu.VMEM((3, kinds, ROWS, LANES), F32),
        pltpu.VMEM((kinds, ROWS, LANES), dtype),
    ]


def tail_scratch(parts, kinds, dtype):
    return [
        pltpu.VMEM((6, parts, 2, kinds, ROWS, LANES), F32),
        pltpu.VMEM((2, 2, parts, kinds, ROWS, LANES), F32),
        pltpu.VMEM((3, parts, kinds, ROWS, LANES), F32),
        pltpu.VMEM((parts, kinds, ROWS, LANES), dtype),
    ]


def sums_scratch(kinds):
    return [
        pltpu.VMEM((2, kinds, 4, 4, ROWS, D), F32),
        pltpu.VMEM((PARTS, 6, 2, kinds, 4, ROWS, LANES), BF16),
        pltpu.VMEM((PARTS, 6, 2, kinds, 4, ROWS, LANES), BF16),
        pltpu.VMEM((PARTS, 2, 2, kinds, 4, ROWS, LANES), F32),
    ]


def shards(inputs, memory, doc_ids, key_valid, sticky_bins, ln_gain, ln_shift, w_qkv, b_qv, w_gauss, w_out, b_out,
           w_fc, b_fc, w_proj, b_proj, cotangent):
    vmem, hbm = pl.BlockSpec(memory_space=pltpu.VMEM), pl.BlockSpec(memory_space=pl.ANY)
    S, V = jax.ShapeDtypeStruct, pltpu.VMEM
    count = 3 * (1 + 12 + 8) + 2 + 6
    watt, wmlp, sall, coeffs, hidden, qs, ks, vs, mks, mvs, lse, context = pl.pallas_call(
        attend_kernel,
        out_shape=(
            S((2, 2, PARTS, 4, 4, ROWS, D), BF16), S((2, 2, PARTS, 2, 4, 4, ROWS, D), BF16), S((4, PARTS, 8, 256), F32),
            S((N, D), BF16), S((SEG, D), F32), S((PARTS, SEG, 256), BF16), S((PARTS, SEG, 256), BF16),
            S((PARTS, SEG, 256), BF16), S((PARTS, N, 256), BF16), S((PARTS, N, 256), BF16), S((PARTS, SEG, 128), F32),
            S((PARTS, SEG, 256), BF16)),
        in_specs=[hbm] + [vmem] * 14,
        out_specs=[hbm] * 3 + [vmem] * 9,
        scratch_shapes=[
            V((2, 2, PARTS, 4, 4, ROWS, D), BF16), V((PARTS, 2, 4, 4, ROWS, D), BF16), V((4, 128, D), BF16),
            V((4, PARTS, 8, 256), F32), V((SEG, D), BF16), V((SEG, 1), F32), V((SEG, SEG), F32),
            V((SEG, D), BF16), V((4, SEG, HD), BF16), V((4, SEG, HD), BF16), V((4, SEG, HD), BF16),
            pltpu.SemaphoreType.DMA((count,)), pltpu.SemaphoreType.DMA((count,)), pltpu.SemaphoreType.DMA((4,))],
        compiler_params=pltpu.CompilerParams(collective_id=1, has_side_effects=True, vmem_limit_bytes=VMEM_LIMIT),
        name="gather_attend",
    )(inputs, memory, doc_ids, key_valid, sticky_bins, ln_gain, ln_shift, w_qkv.transpose(0, 2, 1), b_qv, w_gauss.transpose(1, 0, 2), w_out, b_out,
      w_fc, b_fc, w_proj)

    count = 2 * PARTS * 7 + 2 * PARTS * (6 + 3 + 1 + 12) + 2 * 9 + 10
    tatt, tmlp, small_total, mixed_all, gin_all = pl.pallas_call(
        backward_kernel,
        out_shape=(
            S((PARTS, 1, 4, 4, ROWS, D), F32), S((PARTS, 2, 4, 4, ROWS, D), BF16), S((PARTS, 24, 256), F32),
            S((4, SEG, D), BF16), S((4, SEG, D), BF16)),
        in_specs=[hbm] * 5 + [vmem] * 14,
        out_specs=[hbm, hbm, vmem, hbm, hbm],
        scratch_shapes=[
            V((SEG, D), BF16), V((SEG, D), BF16), V((SEG, 1), F32),
            V((2, 2, 2, 4, 4, ROWS, D), BF16), V((2, 2, 2, 4, 4, ROWS, D), F32),
            V((SEG, D), F32), V((SEG, D), F32), V((SEG, D), F32), V((SEG, D), BF16), V((SEG, D), BF16), V((SEG, D), BF16),
            V((SEG, SEG), F32), V((4, SEG, HD), BF16), V((4, SEG, HD), BF16), V((4, SEG, HD), BF16), V((4, SEG, HD), BF16),
            ]
        + sums_scratch(2) + sums_scratch(1)
        + tail_y_scratch(2, BF16) * PARTS + tail_scratch(1, 1, F32) * PARTS
        + [V((PARTS, 24, 256), F32), V((4, 4, PARTS, 24, 256), F32),
           pltpu.SemaphoreType.DMA((count,)), pltpu.SemaphoreType.DMA((count,)),
           pltpu.SemaphoreType.REGULAR, pltpu.SemaphoreType.REGULAR, pltpu.SemaphoreType.DMA((13,))],
        compiler_params=pltpu.CompilerParams(collective_id=2, has_side_effects=True, vmem_limit_bytes=VMEM_LIMIT),
        name="mlp_backward",
    )(inputs, cotangent, hidden, watt, wmlp, coeffs, sall, doc_ids, key_valid, ln_gain, ln_shift, b_proj,
      qs, ks, vs, mks, mvs, lse, context)
    return finish(tatt.reshape(PARTS, 4, HD, D), tmlp.reshape(PARTS, 2, 256, D), small_total, mixed_all, gin_all)


def finish_kernel(tatt, tmlp, small, mixed_in, gin_in, mixed, gin, gain, shift, wqkv, bqv, gauss, wout, bout, wfc, bfc, wproj,
                  bproj):
    at = pl.program_id(0)
    mixed[...] = mixed_in[...]
    gin[...] = gin_in[...].astype(F32)

    @pl.when(at < PARTS)
    def _():
        wfc[...] = tmlp[0, 0].astype(F32).T
        wproj[...] = tmlp[0, 1].astype(F32)

    @pl.when(at == PARTS)
    def _():
        head = lax.axis_index("head")
        for kind in range(3):
            wqkv[kind] = jnp.concatenate([tatt[i, kind] for i in range(PARTS)], axis=0)
        for i in range(PARTS):
            wout[i * HD:(i + 1) * HD] = tatt[i, 3]
        for i in range(PARTS):
            part = slice(i * 256, (i + 1) * 256)
            gain[0:1, part], gain[1:2, part] = small[i, 0:1], small[i, 1:2]
            shift[0:1, part], shift[1:2, part] = small[i, 2:3], small[i, 3:4]
            bout[part], bproj[part] = small[i, 4], small[i, 5]
            value, biases, widths = small[i, 16], small[i, 6:8, 0:HD], small[i, 8:10]
            for g in range(1, 4):
                value = jnp.where(head == g, small[i, 16 + g], value)
                biases = jnp.where(head == g, small[i, 6:8, g * HD:(g + 1) * HD], biases)
                widths = jnp.where(head == g, small[i, 8 + 2 * g:10 + 2 * g], widths)
            bfc[part] = value
            bqv[:, i * HD:(i + 1) * HD] = biases
            gauss[i] = widths


def finish(tatt, tmlp, small, mixed_all, gin_all):
    S = jax.ShapeDtypeStruct
    whole = lambda *shape: pl.BlockSpec(shape, lambda i: (0,) * len(shape))
    part = lambda i: jnp.minimum(i, PARTS - 1)
    segment = pl.BlockSpec((1, SEG, D), lambda i: (i, 0, 0))
    out = pl.pallas_call(
        finish_kernel,
        grid=(4,),
        out_shape=(
            S((4, SEG, D), BF16), S((4, SEG, D), F32), S((2, D), F32), S((2, D), F32), S((3, 192, D), F32), S((2, 192), F32),
            S((3, 2, N), F32), S((192, D), F32), S((D,), F32), S((D, D), F32), S((D,), F32), S((D, D), F32),
            S((D,), F32)),
        in_specs=[whole(PARTS, 4, HD, D), pl.BlockSpec((1, 2, 256, D), lambda i: (part(i), 0, 0, 0)),
                  whole(PARTS, 24, 256), segment, segment],
        out_specs=(
            segment, segment, whole(2, D), whole(2, D), whole(3, 192, D), whole(2, 192), whole(3, 2, N), whole(192, D),
            whole(D), pl.BlockSpec((D, 256), lambda i: (0, part(i))), whole(D),
            pl.BlockSpec((256, D), lambda i: (part(i), 0)), whole(D)),
        compiler_params=pltpu.CompilerParams(vmem_limit_bytes=VMEM_LIMIT),
        name="finish",
    )(tatt, tmlp, small, mixed_all, gin_all)
    out = list(out)
    out[4], out[6] = out[4].transpose(0, 2, 1), out[6].transpose(1, 0, 2)
    return tuple(out)


def solution(mesh):
    return jax.shard_map(
        shards,
        mesh=mesh,
        in_specs=(
            P("dp", None, None),
            P("dp", "head", None),
            P("dp", None),
            P("dp", None),
            P("dp", None),
            P(),
            P(),
            P(None, None, "head"),
            P(None, "head"),
            P(None, "head", None),
            P("head", None),
            P(),
            P(None, "head"),
            P("head"),
            P("head", None),
            P(),
            P("dp", None, None),
        ),
        out_specs=(
            P("dp", None, None),
            P("dp", None, None),
            P(),
            P(),
            P(None, None, "head"),
            P(None, "head"),
            P(None, "head", None),
            P("head", None),
            P(),
            P(None, "head"),
            P("head"),
            P("head", None),
            P(),
        ),
        check_vma=False,
    )
```

```python
from functools import partial

import jax
import jax.numpy as jnp
from jax import lax
from jax.experimental import pallas as pl
from jax.experimental.pallas import tpu as pltpu
from jax.sharding import PartitionSpec as P

MESH = pl.DeviceIdType.MESH
BF16, F32 = jnp.bfloat16, jnp.float32
D, N, HEADS, HD, FF, SEG, HALF = 768, 256, 12, 64, 3072, 512, 256
PARTS, ROWS, LANES = 3, 16, 384
EPSILON = 1e-05
RIDGE_WEIGHT = 0.5
SIGMA_SCALE = 0.01
SCORE_SCALE = 0.125
NEG_FILL = -1e30
GELU_COEFF = 0.7978845608028654
PRECISE = lax.Precision.HIGHEST
VMEM_LIMIT = 60 * 1024 * 1024
BLOCK = 256
CHUNK = 128
BLOCKS = SEG // BLOCK


class Place:
    def __init__(self):
        dp, head = lax.axis_index("dp"), lax.axis_index("head")
        self.head = head
        self.yl = lax.div(dp, 16)
        self.z = lax.rem(lax.div(dp, 4), 4)
        self.x = lax.rem(dp, 4)
        self.yh = lax.div(head, 2)
        self.c = lax.rem(head, 2)
        self.y = self.yh * 2 + self.yl

    def at(self, x=None, z=None, y=None, c=None):
        x = self.x if x is None else x
        z = self.z if z is None else z
        c = self.c if c is None else c
        if y is None:
            yl, yh = self.yl, self.yh
        else:
            yl, yh = lax.rem(y, 2), lax.div(y, 2)
        return (yl * 16 + z * 4 + x, yh * 2 + c)

    def core(self):
        return self.at(c=1 - self.c)

    def ring(self, along_x, k):
        return self.at(x=step(self.x, k)) if along_x else self.at(z=step(self.z, k))


def step(place, by):
    return lax.rem(place + by, 4)


def lanes(half):
    return pl.ds(half * LANES, LANES)


def greet(devices):
    sem = pltpu.get_barrier_semaphore()
    for device in devices:
        pl.semaphore_signal(sem, inc=1, device_id=device, device_id_type=MESH)


def met(devices):
    pl.semaphore_wait(pltpu.get_barrier_semaphore(), len(devices))


class Links:
    def __init__(self, send, recv):
        self.send, self.recv, self.used, self.all = send, recv, 0, []

    def add(self, src, dst, device, arrives):
        link = Link(self, self.used, src, dst, device, arrives)
        self.used += 1
        self.all.append(link)
        return link

    def finish(self):
        for link in self.all:
            if not link.done:
                link.sent()


class Link:
    def __init__(self, links, index, src, dst, device, arrives):
        self.links, self.index, self.done = links, index, False
        self.src, self.dst, self.device, self.arrives = src, dst, device, arrives

    def copy(self, dst):
        return pltpu.make_async_remote_copy(
            src_ref=self.src(), dst_ref=dst, send_sem=self.links.send.at[self.index],
            recv_sem=self.links.recv.at[self.index], device_id=self.device(), device_id_type=MESH)

    def start(self):
        self.copy(self.dst()).start()

    def wait(self):
        self.copy(self.arrives()).wait_recv()

    def sent(self):
        self.copy(self.dst()).wait_send()


class PlaneGather:
    def __init__(self, links, me, view, row, column):
        self.one, self.two = [[], []], [[], []]
        for k in (1, 3, 2):
            back = 4 - k
            self.one[0].append(links.add(
                lambda: view(me.z, me.x, 0), lambda: view(me.z, me.x, 0), lambda k=k: me.ring(True, k),
                lambda back=back: view(me.z, step(me.x, back), 0)))
            self.one[1].append(links.add(
                lambda: view(me.z, me.x, 1), lambda: view(me.z, me.x, 1), lambda k=k: me.ring(False, k),
                lambda back=back: view(step(me.z, back), me.x, 1)))
            self.two[0].append(links.add(
                lambda: row(me.z, 0), lambda: row(me.z, 0), lambda k=k: me.ring(False, k),
                lambda back=back: row(step(me.z, back), 0)))
            self.two[1].append(links.add(
                lambda: column(me.x, 1), lambda: column(me.x, 1), lambda k=k: me.ring(True, k),
                lambda back=back: column(step(me.x, back), 1)))

    def first(self):
        for a, b in zip(*self.one):
            a.start()
            b.start()

    def second(self):
        for half in (0, 1):
            for link in self.one[half]:
                link.wait()
            for link in self.two[half]:
                link.start()

    def finish(self):
        for a, b in zip(*self.two):
            a.wait()
            b.wait()


def nt(a, b):
    return lax.dot_general(a, b, (((1,), (1,)), ((), ())), preferred_element_type=F32)


def nn(a, b):
    return lax.dot_general(a, b, (((1,), (0,)), ((), ())), preferred_element_type=F32)


def tn(a, b):
    return lax.dot_general(a, b, (((0,), (0,)), ((), ())), preferred_element_type=F32)


def normalize(values):
    centred = values - jnp.mean(values, axis=-1, keepdims=True)
    inverse = lax.rsqrt(jnp.mean(centred * centred, axis=-1, keepdims=True) + EPSILON)
    return centred * inverse, inverse


def norm_back(grad, normed, inverse, gain):
    scaled = grad * gain
    return inverse * (scaled - jnp.mean(scaled, axis=-1, keepdims=True)
                      - normed * jnp.mean(scaled * normed, axis=-1, keepdims=True))


def column_sum(values):
    return jnp.sum(values, axis=0, keepdims=True)


def as_column(row):
    return jnp.broadcast_to(row.astype(F32), (8, SEG)).T[:, 0:1]


def mask_bias(doc_row, valid_row):
    doc_row = doc_row.astype(F32)
    doc_col = as_column(doc_row)
    rows = lax.broadcasted_iota(jnp.int32, (SEG, SEG), 0)
    cols = lax.broadcasted_iota(jnp.int32, (SEG, SEG), 1)
    live = (valid_row == 1) | (rows == cols)
    return jnp.where((cols <= rows) & (doc_col == doc_row) & live, 0.0, NEG_FILL)


def gaussian(mem_scores, gauss):
    centre = jax.nn.sigmoid(jnp.sum(mem_scores * gauss[0:1], axis=-1, keepdims=True))
    width = jnp.sum(mem_scores * gauss[1:2], axis=-1, keepdims=True)
    softplus = jnp.maximum(width, 0.0) + jnp.log1p(jnp.exp(-jnp.abs(width)))
    variance = SIGMA_SCALE * softplus + (1.0 / N) ** 2
    places = (lax.broadcasted_iota(jnp.int32, (1, N), 1).astype(F32) + 0.5) / N
    offsets = centre - places
    inverse = 1.0 / variance
    density = (1.0 / N) * lax.rsqrt(variance) * jnp.exp(-0.5 * offsets * offsets * inverse)
    return centre, width, offsets, inverse, density


LOWEST, HIGHEST = RIDGE_WEIGHT, 650.0


def attend_kernel(inputs, memory, doc_ids, key_valid, sticky_bins, ln_gain, ln_shift, w_qkv, b_qv, w_gauss, w_out, b_out,
                  w_fc, b_fc, w_proj,
                  watt_out, wmlp, sall_out, coeffs, hidden, qs, ks, vs, mks, mvs, lse, context,
                  watt, pmlp, mseg, sall, x, gate, bias, n1, hq, hk, hv, send, recv, local):
    me = Place()
    mine = pl.ds(me.head, 1)
    peers = ([me.core(), me.at(y=3 - me.y), me.at(y=step(me.y, 2)), me.at(y=step(me.y, 2), c=1 - me.c)]
             + [me.ring(True, k) for k in (1, 2, 3)] + [me.ring(False, k) for k in (1, 2, 3)])
    greet(peers)
    load_x = pltpu.make_async_copy(inputs.at[me.head], x, local.at[0])
    load_x.start()
    for kind in range(3):
        for i in range(PARTS):
            watt[me.yh, me.c, i, kind] = w_qkv[kind, i * HD:(i + 1) * HD].reshape(4, ROWS, D)
    for i in range(PARTS):
        watt[me.yh, me.c, i, 3] = w_out[i * HD:(i + 1) * HD].reshape(4, ROWS, D)
    mine_small = sall.at[me.head]
    mine_small[...] = jnp.zeros((PARTS, 8, 256), F32)
    for i in range(PARTS):
        mine_small[i, 0:2, 0:HD] = b_qv[:, i * HD:(i + 1) * HD]
        mine_small[i, 2:4] = w_gauss[i]
        mine_small[i, 4:5] = b_fc[i * 256:(i + 1) * 256].reshape(1, 256)
    for i in range(PARTS):
        pmlp[i, 0] = w_fc[:, i * 256:(i + 1) * 256].T.reshape(4, 4, ROWS, D)
        pmlp[i, 1] = w_proj[i * 256:(i + 1) * 256].reshape(4, 4, ROWS, D)
    met(peers)

    links = Links(send, recv)

    class Gather:
        def __init__(self, wall, own, low, high):
            def block(yh, c, z, xx, cut):
                return wall.at[yh, c, low:high, ..., z, xx, :, cut]

            every = slice(None)

            def view(z, xx, half, c=None):
                return block(1 - me.yh, me.c if c is None else c, z, xx, lanes(half))

            def row(z, half, c=None):
                return view(z, every, half, c)

            def column(xx, half, c=None):
                return view(every, xx, half, c)

            self.across = links.add(
                lambda: own().at[low:high, ..., me.z, me.x, :, :], lambda: block(me.yh, me.c, me.z, me.x, every),
                lambda: me.at(y=3 - me.y), lambda: block(1 - me.yh, me.c, me.z, me.x, every))
            self.plane = PlaneGather(links, me, view, row, column)
            self.passed = []
            for k in (0, 1, 3, 2):
                self.passed.append(links.add(
                    lambda k=k: row(step(me.z, k), 0), lambda k=k: row(step(me.z, k), 0), me.core,
                    lambda k=k: row(step(me.z, k), 0, 1 - me.c)))
                self.passed.append(links.add(
                    lambda k=k: column(step(me.x, k), 1), lambda k=k: column(step(me.x, k), 1), me.core,
                    lambda k=k: column(step(me.x, k), 1, 1 - me.c)))

        def first(self):
            self.across.wait()
            self.plane.first()

        def second(self):
            self.plane.second()
            self.passed[0].start()
            self.passed[1].start()

        def third(self):
            self.plane.finish()
            for link in self.passed[2:]:
                link.start()

        def ready(self):
            for link in self.passed:
                link.wait()

    own_att = lambda: watt.at[me.yh, me.c]
    own_mlp = lambda: pmlp
    early, late = Gather(watt, own_att, 0, 1), Gather(watt, own_att, 1, PARTS)
    units = Gather(wmlp, own_mlp, 0, PARTS)
    swap_att = links.add(own_att, own_att, me.core, lambda: watt.at[me.yh, 1 - me.c])
    swap_mlp = links.add(own_mlp, lambda: wmlp.at[me.yh, me.c], me.core, lambda: wmlp.at[me.yh, 1 - me.c])
    sent, sent_small = [], []
    for k in (1, 2, 3):
        def other(k=k):
            return lax.rem(me.head + k, 4)

        def device(k=k):
            return (me.yl * 16 + me.z * 4 + me.x, lax.rem(me.head + k, 4))

        def before(k=k):
            return lax.rem(me.head + (4 - k), 4)

        sent.append(links.add(lambda other=other: memory.at[other()], lambda: mseg.at[me.head], device,
                              lambda before=before: mseg.at[before()]))
        sent_small.append(links.add(lambda: sall.at[me.head], lambda: sall.at[me.head], device,
                                    lambda before=before: sall.at[before()]))
    early.across.start()
    late.across.start()
    units.across.start()
    for link in sent:
        link.start()
    swap_att.start()
    for link in sent_small:
        link.start()
    swap_mlp.start()
    keep_mlp = pltpu.make_async_copy(pmlp, wmlp.at[me.yh, me.c], local.at[1])
    keep_mlp.start()
    mseg[mine] = memory[mine]
    early.first()
    load_x.wait()
    values, _ = normalize(x[...].astype(F32))
    n1[...] = (values * ln_gain[0:1] + ln_shift[0:1]).astype(BF16)
    hidden[...] = x[...].astype(F32) + b_out[...]
    late.first()

    dot = partial(jnp.dot, preferred_element_type=F32, precision=PRECISE)
    rows = lax.broadcasted_iota(jnp.int32, (N, N), 0)
    cols = lax.broadcasted_iota(jnp.int32, (N, N), 1)
    gap = (rows - cols).astype(F32)
    curve = jnp.exp(-0.5 * gap * gap)
    eye = (rows == cols).astype(F32)
    picked = (sticky_bins[mine] == rows).astype(F32)
    counts = 1.0 + jnp.sum(picked, axis=1, keepdims=True)
    gram = dot(curve, counts * curve) + RIDGE_WEIGHT * eye

    def newton(count, state):
        def body(_, state):
            inverse, gap = state
            scale = 2.0 / (2.0 - gap * gap)
            inverse = scale * (2.0 * inverse - dot(inverse, dot(gram, inverse)))
            return inverse, gap * gap / (2.0 - gap * gap)

        return lax.fori_loop(0, count, body, state)

    state = ((2.0 / (LOWEST + HIGHEST)) * eye, jnp.float32((HIGHEST - LOWEST) / (HIGHEST + LOWEST)))
    early.second()
    state = newton(2, state)
    late.second()
    units.first()
    state = newton(2, state)
    early.third()
    state = newton(3, state)
    late.third()
    units.second()
    inverse, _ = newton(3, state)
    docs = doc_ids[mine]
    bias[...] = mask_bias(docs, key_valid[mine])
    gate[...] = (as_column(docs) == docs[:, 0:1].astype(F32)).astype(F32)
    for link in sent:
        link.wait()
    first_half = mseg[0:2].reshape(HALF, D).astype(F32)
    held = first_half + jnp.dot(picked.astype(BF16), mseg[2:4].reshape(HALF, D), preferred_element_type=F32)
    coeffs[...] = dot(inverse, dot(curve, held)).astype(BF16)
    swap_att.wait()
    early.ready()
    for link in sent_small:
        link.wait()
    out = [pltpu.make_async_copy(watt, watt_out, local.at[2]), pltpu.make_async_copy(sall, sall_out, local.at[3])]
    hooks = (((1, 0), units.third),)

    def group(i, carry):
        def weight(kind):
            return watt[:, :, i, kind].reshape(4 * HD, D)

        def heads_row(r):
            return jnp.concatenate([sall[g, i, r:r + 1, 0:HD] for g in range(4)], axis=1)

        @pl.when(i == 1)
        def _():
            late.ready()
            for copy in out:
                copy.start()

        q4 = (nt(n1[...], weight(0)) + heads_row(0)).astype(BF16)
        k4 = nt(n1[...], weight(1)).astype(BF16)
        v4 = (nt(n1[...], weight(2)) + heads_row(1)).astype(BF16)
        mk4 = nt(coeffs[...], weight(1)).astype(BF16)
        mv4 = nt(coeffs[...], weight(2)).astype(BF16)
        qs[i], ks[i], vs[i], mks[i], mvs[i] = q4, k4, v4, mk4, mv4
        for g in range(4):
            part = slice(g * HD, (g + 1) * HD)
            hq[g], hk[g], hv[g] = q4[:, part], k4[:, part], v4[:, part]
        parts = []
        for g in range(4):
            part = slice(g * HD, (g + 1) * HD)
            mk, mv = mk4[:, part], mv4[:, part]
            blocks = []
            for r in range(BLOCKS):
                rows, cols = slice(r * BLOCK, (r + 1) * BLOCK), slice(0, (r + 1) * BLOCK)
                q = hq[g, rows]
                scores = nt(q, hk[g, cols]) * SCORE_SCALE + bias[rows, cols]
                top = jnp.max(scores, axis=-1, keepdims=True)
                weights = jnp.exp(scores - top)
                total = jnp.sum(weights, axis=-1, keepdims=True)
                lse[i, rows, g:g + 1] = top + jnp.log(total)
                probs = (weights * (1.0 / total)).astype(BF16)
                attended = nn(probs, hv[g, cols])
                mem_scores = nt(q, mk) * SCORE_SCALE
                density = gaussian(mem_scores, sall[g, i, 2:4])[-1].astype(BF16)
                blocks.append((attended + gate[rows] * nn(density, mv)).astype(BF16))
            parts.append(jnp.concatenate(blocks, axis=0))
            for when, move in hooks:
                if when[1] == g:
                    @pl.when(i == when[0])
                    def _(move=move):
                        move()

        mixed = jnp.concatenate(parts, axis=1)
        context[i] = mixed
        hidden[...] += nn(mixed, weight(3))

        return carry

    lax.fori_loop(0, PARTS, group, 0)
    swap_mlp.wait()
    units.ready()
    keep_mlp.wait()
    for copy in out:
        copy.wait()
    links.finish()


class Sums:
    def __init__(self, links, me, kinds, other, sbuf, rbuf, kept, credit):
        self.links, self.me, self.kinds = links, me, kinds
        self.other, self.sbuf, self.rbuf, self.kept, self.credit = other, sbuf, rbuf, kept, credit
        self.base = links.used
        links.used += PARTS * 7

    def swap(self, part, src):
        return Link(self.links, self.base + part, src, lambda: self.other, self.me.core, lambda: self.other)

    def send(self, part, half, k):
        i = half * 3 + k - 1
        return Link(self.links, self.base + PARTS + part * 6 + i, lambda: self.sbuf.at[part, i],
                    lambda: self.rbuf.at[part, i], lambda: self.me.ring(half == 0, k), lambda: self.rbuf.at[part, i])

    def first(self, part, own):
        me = self.me
        self.swap(part, lambda: self.other).wait()
        for k in (2, 1, 3, 0):
            for half in (0, 1):
                def body(i, carry, half=half, k=k):
                    t, kind = lax.div(i, self.kinds), lax.rem(i, self.kinds)
                    for q in range(4):
                        z, x = (q, step(me.x, k)) if half == 0 else (step(me.z, k), q)
                        cut = slice(half * LANES, (half + 1) * LANES)
                        value = own(t, kind, z, x, cut) + self.other[t, kind, z, x, :, cut]
                        if k == 0:
                            self.kept[part, half, t, kind, q] = value
                        else:
                            self.sbuf[part, half * 3 + k - 1, t, kind, q] = value.astype(BF16)
                    return carry

                lax.fori_loop(0, 2 * self.kinds, body, 0)
                if k:
                    self.send(part, half, k).start()
        pl.semaphore_signal(self.credit, inc=1, device_id=me.core(), device_id_type=MESH)


class Tail:
    def __init__(self, links, me, sums, low, high, total, rbuf2, ylocal, ybuf, final, local):
        self.me, self.sums, self.low, self.high, self.total = me, sums, low, high, total
        self.rbuf2, self.ylocal, self.ybuf, self.final, self.local = rbuf2, ylocal, ybuf, final, local
        kept = sums.kept
        self.two = {}
        for half in (0, 1):
            across = (lambda: me.z) if half == 0 else (lambda: me.x)
            for k in (2, 1, 3):
                i = half * 3 + k - 1
                self.two[half, k] = links.add(
                    lambda half=half, k=k, across=across: kept.at[low:high, half, :, :, step(across(), k)],
                    lambda i=i: rbuf2.at[i], lambda half=half, k=k: me.ring(half == 1, k), lambda i=i: rbuf2.at[i])
        self.three = []
        for k in (2, 1, 3):
            def target(k=k):
                return step(me.y, k)

            self.three.append(links.add(
                lambda target=target: ylocal.at[lax.div(target(), 2), lax.rem(target(), 2)],
                lambda k=k: ybuf.at[k - 1], lambda target=target: me.at(y=target()), lambda k=k: ybuf.at[k - 1]))

        def view(z, x, half):
            return total.at[low:high, :, z, x, :, lanes(half)]

        def row(z, half):
            return total.at[low:high, :, z, :, :, lanes(half)]

        def column(x, half):
            return total.at[low:high, :, :, x, :, lanes(half)]

        self.view = view
        self.mate = links.add(lambda: final, lambda: view(me.z, me.x, me.yl),
                              lambda: me.at(y=me.yh * 2 + 1 - me.yl), lambda: view(me.z, me.x, 1 - me.yl))
        self.gather = PlaneGather(links, me, view, row, column)

    def second(self):
        sums, kept = self.sums, self.sums.kept
        for half in (0, 1):
            for part in range(self.low, self.high):
                for k in (1, 2, 3):
                    sums.send(part, half, k).wait()

                def body(i, carry, half=half, part=part):
                    t, kind = lax.div(i, sums.kinds), lax.rem(i, sums.kinds)
                    value = kept[part, half, t, kind]
                    for k in (1, 2, 3):
                        value = value + sums.rbuf[part, half * 3 + k - 1, t, kind].astype(F32)
                    kept[part, half, t, kind] = value
                    return carry

                lax.fori_loop(0, 2 * sums.kinds, body, 0)
            for k in (2, 1, 3):
                self.two[half, k].start()

    def third(self):
        me, kept = self.me, self.sums.kept
        for half in (0, 1):
            for k in (1, 2, 3):
                self.two[half, k].wait()
            across = me.z if half == 0 else me.x
            for p in range(self.low, self.high):
                for t in (0, 1):
                    value = kept[p, half, t, :, across]
                    for k in (1, 2, 3):
                        value = value + self.rbuf2[half * 3 + k - 1, p - self.low, t]
                    self.ylocal[t, half, p - self.low] = value
        for link in self.three:
            link.start()

    def keep(self):
        return pltpu.make_async_copy(self.final, self.view(self.me.z, self.me.x, self.me.yl), self.local)

    def fourth(self):
        me = self.me
        for link in self.three:
            link.wait()
        self.final[...] = (self.ylocal[me.yh, me.yl] + self.ybuf[0] + self.ybuf[1] + self.ybuf[2]).astype(
            self.final.dtype)
        self.keep().start()
        self.mate.start()

    def fifth(self):
        self.keep().wait()
        self.mate.wait()
        self.gather.first()

    def sixth(self):
        self.gather.second()

    def finish(self):
        self.gather.finish()


class TailY:
    def __init__(self, links, me, sums, part, total, ybuf, rbuf2, final, local):
        self.me, self.sums, self.part, self.total = me, sums, part, total
        self.ybuf, self.rbuf2, self.final, self.local = ybuf, rbuf2, final, local
        kept = sums.kept
        self.two, self.three = [], []
        for k in (2, 1, 3):
            def target(k=k):
                return step(me.y, k)

            self.two.append(links.add(
                lambda target=target: kept.at[part, lax.rem(target(), 2), lax.div(target(), 2)],
                lambda k=k: ybuf.at[k - 1], lambda target=target: me.at(y=target()), lambda k=k: ybuf.at[k - 1]))

        def peer(k):
            return me.at(x=step(me.x, k * me.yl), z=step(me.z, k * (1 - me.yl)))

        for k in (2, 1, 3):
            self.three.append(links.add(
                lambda k=k: kept.at[part, me.yl, me.yh, :, step(self.across(), k)],
                lambda k=k: rbuf2.at[k - 1], lambda k=k: peer(k), lambda k=k: rbuf2.at[k - 1]))

        def view(z, x, half):
            return total.at[part, :, z, x, :, lanes(half)]

        def row(z, half):
            return total.at[part, :, z, :, :, lanes(half)]

        def column(x, half):
            return total.at[part, :, :, x, :, lanes(half)]

        self.view = view
        self.mate = links.add(lambda: final, lambda: view(me.z, me.x, me.yl),
                              lambda: me.at(y=me.yh * 2 + 1 - me.yl), lambda: view(me.z, me.x, 1 - me.yl))
        self.gather = PlaneGather(links, me, view, row, column)

    def across(self):
        return self.me.z * (1 - self.me.yl) + self.me.x * self.me.yl

    def second(self):
        sums, kept, part = self.sums, self.sums.kept, self.part
        for half in (0, 1):
            for k in (1, 2, 3):
                sums.send(part, half, k).wait()

            def body(i, carry, half=half):
                t, kind = lax.div(i, sums.kinds), lax.rem(i, sums.kinds)
                value = kept[part, half, t, kind]
                for k in (1, 2, 3):
                    value = value + sums.rbuf[part, half * 3 + k - 1, t, kind].astype(F32)
                kept[part, half, t, kind] = value
                return carry

            lax.fori_loop(0, 2 * sums.kinds, body, 0)
        for link in self.two:
            link.start()

    def third(self):
        me, kept, part = self.me, self.sums.kept, self.part
        for link in self.two:
            link.wait()
        for kind in range(self.sums.kinds):
            value = kept[part, me.yl, me.yh, kind]
            for k in range(3):
                value = value + self.ybuf[k, kind]
            kept[part, me.yl, me.yh, kind] = value
        for link in self.three:
            link.start()

    def keep(self):
        return pltpu.make_async_copy(self.final, self.view(self.me.z, self.me.x, self.me.yl), self.local)

    def fourth(self):
        me, kept, part = self.me, self.sums.kept, self.part
        for link in self.three:
            link.wait()
        self.final[...] = (kept[part, me.yl, me.yh, :, self.across()] + self.rbuf2[0] + self.rbuf2[1]
                           + self.rbuf2[2]).astype(self.final.dtype)
        self.keep().start()
        self.mate.start()

    def fifth(self):
        self.keep().wait()
        self.mate.wait()
        self.gather.first()

    def sixth(self):
        self.gather.second()

    def finish(self):
        self.gather.finish()


def backward_kernel(inputs, cotangent, hidden_in, watt, wmlp, coeffs, sall, doc_ids, key_valid, ln_gain, ln_shift, b_proj,
                    qs, ks, vs, mks, mvs, lse, context,
                    tatt, tmlp, small_total, mixed_all, gin_all,
                    x, cot, gate, wbuf, gbuf, hidden, acc, gnorm, n12, gbranch, mixed, bias, hq, hk, hv, gcs,
                    otherm, sbufm, rbufm, keptm, othera, sbufa, rbufa, kepta,
                    *rest):
    tails_m, tails_a, (small, slots, send, recv, creditm, credita, local) = rest[:9], rest[9:21], rest[21:]
    me = Place()
    peers = ([me.core()] + [me.ring(True, k) for k in (1, 2, 3)] + [me.ring(False, k) for k in (1, 2, 3)]
             + [me.at(y=step(me.y, k)) for k in (1, 2, 3)])
    greet(peers)
    links = Links(send, recv)
    mlp = Sums(links, me, 2, otherm, sbufm, rbufm, keptm, creditm)
    att = Sums(links, me, 1, othera, sbufa, rbufa, kepta, credita)
    m = [TailY(links, me, mlp, p, tmlp, *tails_m[3 * p:3 * p + 3], local.at[4 + p]) for p in range(PARTS)]
    a = [Tail(links, me, att, p, p + 1, tatt, *tails_a[4 * p:4 * p + 4], local.at[7 + p]) for p in range(PARTS)]

    def load(index, slot):
        part, mine = lax.div(index, 2), lax.rem(index, 2)
        owner = mine * me.c + (1 - mine) * (1 - me.c)
        return pltpu.make_async_copy(wmlp.at[:, owner, part], wbuf.at[slot], local.at[slot])

    def load_att(part, slot):
        return pltpu.make_async_copy(watt.at[:, :, part], wbuf.at[slot], local.at[slot])

    load_hidden = pltpu.make_async_copy(hidden_in, hidden, local.at[12])
    load_hidden.start()
    load_cot = pltpu.make_async_copy(cotangent.at[me.head], cot, local.at[10])
    load_cot.start()
    load(0, 0).start()
    load(1, 1).start()
    load_x = pltpu.make_async_copy(inputs.at[me.head], x, local.at[11])
    load_x.start()
    load_hidden.wait()

    def start_mlp(i, carry):
        rows = pl.ds(i * CHUNK, CHUNK)
        values, _ = normalize(hidden[rows])
        n12[rows] = (values * ln_gain[1:2] + ln_shift[1:2]).astype(BF16)
        acc[rows] = hidden[rows] + b_proj[...]
        return carry

    lax.fori_loop(0, SEG // CHUNK, start_mlp, 0)
    load_cot.wait()
    load_x.wait()
    gnorm[...] = jnp.zeros_like(gnorm)
    small[...] = jnp.zeros_like(small)
    met(peers)

    def own_mlp(t, kind, z, xx, cut):
        return gbuf[1, t, kind, z, xx, :, cut]

    def swap_mlp(part):
        return mlp.swap(part, lambda: gbuf.at[0])

    def units(index, carry):
        part, mine = lax.div(index, 2), lax.rem(index, 2)
        owner = mine * me.c + (1 - mine) * (1 - me.c)
        load(index, mine).wait()

        @pl.when((mine == 0) & (part > 0))
        def _():
            mlp.first(part - 1, own_mlp)
            swap_mlp(part - 1).sent()

        @pl.when(index == 5)
        def _():
            m[0].second()

        wfc = wbuf[mine, :, 0].reshape(512, D)
        wproj = wbuf[mine, :, 1].reshape(512, D)
        bias_fc = jnp.concatenate([sall[owner, part, 4:5], sall[2 + owner, part, 4:5]], axis=1)
        pre = nt(n12[...], wfc) + bias_fc
        inner = jnp.tanh(GELU_COEFF * (pre + 0.044715 * pre * pre * pre))
        activation = (0.5 * pre * (1.0 + inner)).astype(BF16)
        slope = 0.5 * (1.0 + inner) + (0.5 * GELU_COEFF) * pre * (1.0 - inner * inner) * (
            1.0 + 3.0 * 0.044715 * pre * pre)
        acc[...] += nn(activation, wproj)
        gpre = (nt(cot[...], wproj) * slope).astype(BF16)
        units_sum = column_sum(gpre.astype(F32))
        small[part, pl.ds(16 + owner, 1)] = units_sum[:, 0:256]
        small[part, pl.ds(18 + owner, 1)] = units_sum[:, 256:512]
        gnorm[...] += nn(gpre, wfc)
        gbuf[mine, :, 0] = tn(gpre, n12[...]).reshape(2, 4, 4, ROWS, D)
        gbuf[mine, :, 1] = tn(activation, cot[...]).reshape(2, 4, 4, ROWS, D)

        @pl.when(mine == 0)
        def _():
            @pl.when(part > 0)
            def _():
                pl.semaphore_wait(creditm, 1)

            swap_mlp(part).start()

        @pl.when(index < 4)
        def _():
            load(index + 2, mine).start()

        return carry

    lax.fori_loop(0, 6, units, 0)
    load_att(0, 0).start()
    load_att(1, 1).start()
    mlp.first(2, own_mlp)
    swap_mlp(2).sent()
    mixed[...] = acc[...].astype(BF16)
    far_head = (1 - me.yh) * 2 + me.c
    mate, far_mate = me.yh * 2 + 1 - me.c, (1 - me.yh) * 2 + 1 - me.c

    class Spread:
        def __init__(self, block, everywhere, slot):
            self.keep = pltpu.make_async_copy(block, everywhere.at[me.head], local.at[slot])
            self.near = links.add(lambda: block, lambda: everywhere.at[me.head], me.core, lambda: everywhere.at[mate])
            self.far, self.passed = [], []
            for i in range(SEG // CHUNK):
                rows = pl.ds(i * CHUNK, CHUNK)
                self.far.append(links.add(
                    lambda rows=rows: block.at[rows], lambda rows=rows: everywhere.at[me.head, rows],
                    lambda: me.at(y=step(me.y, 2)), lambda rows=rows: everywhere.at[far_head, rows]))
                self.passed.append(links.add(
                    lambda rows=rows: everywhere.at[far_head, rows], lambda rows=rows: everywhere.at[far_head, rows],
                    me.core, lambda rows=rows: everywhere.at[far_mate, rows]))

        def start(self):
            self.keep.start()
            self.near.start()

        def send(self, i):
            self.far[i].start()

        def forward(self, i):
            self.far[i].wait()
            self.passed[i].start()

        def finish(self):
            self.keep.wait()
            self.near.wait()
            for link in self.passed:
                link.wait()

    mixed_moves = Spread(mixed, mixed_all, 2)
    mixed_moves.start()

    def put(row, vector):
        for i in range(3):
            small[i, row:row + 1] += vector[:, i * 256:(i + 1) * 256]

    def norm_two(i, carry):
        rows = pl.ds(i * CHUNK, CHUNK)
        values, inverse = normalize(hidden[rows])
        grad = gnorm[rows]
        cotangent = cot[rows].astype(F32)
        total = cotangent + norm_back(grad, values, inverse, ln_gain[1:2])
        hidden[rows] = total
        gbranch[rows] = total.astype(BF16)
        put(1, column_sum(grad * values))
        put(3, column_sum(grad))
        put(4, column_sum(total))
        put(5, column_sum(cotangent))
        values, _ = normalize(x[rows].astype(F32))
        n12[rows] = (values * ln_gain[0:1] + ln_shift[0:1]).astype(BF16)
        return carry

    lax.fori_loop(0, SEG // CHUNK, norm_two, 0)
    docs = doc_ids[pl.ds(me.head, 1)]
    bias[...] = mask_bias(docs, key_valid[pl.ds(me.head, 1)])
    gate[...] = (as_column(docs) == docs[:, 0:1].astype(F32)).astype(F32)
    acc[...] = jnp.zeros_like(acc)

    def own_att(part):
        slot = lax.rem(part, 2)
        return lambda t, kind, z, xx, cut: gbuf[slot, t, me.c, z, xx, :, cut]

    def swap_att(part):
        slot = lax.rem(part, 2)
        return att.swap(part, lambda: gbuf.at[slot, :, pl.ds(1 - me.c, 1)])

    hooks = (
        ((0, 2), m[1].second), ((0, 3), m[0].third), ((1, 0), m[0].fourth), ((1, 1), m[0].fifth),
        ((1, 1), partial(mixed_moves.send, 0)),
        ((1, 2), m[2].second), ((1, 2), m[1].third), ((1, 3), m[1].fourth), ((1, 3), m[0].sixth), ((2, 0), m[1].fifth),
        ((2, 0), partial(mixed_moves.send, 1)), ((2, 1), a[0].second), ((2, 1), m[2].third),
        ((2, 1), partial(mixed_moves.send, 2)),
        ((2, 2), m[2].fourth), ((2, 2), m[1].sixth), ((2, 3), m[2].fifth), ((2, 3), partial(mixed_moves.send, 3)),
        ((2, 3), partial(mixed_moves.forward, 0)))

    def group(i, carry):
        slot = lax.rem(i, 2)
        load_att(i, slot).wait()

        def weight(kind):
            return wbuf[slot, :, :, kind].reshape(4 * HD, D)

        q4, k4, v4, mk4, mv4 = qs[i], ks[i], vs[i], mks[i], mvs[i]
        gc4 = nt(gbranch[...], weight(3)).astype(BF16)
        gc4t = nt(weight(3), gbranch[...]).astype(BF16)
        q4t = q4.T
        gate_row = (docs == docs[:, 0:1]).astype(BF16)
        for g in range(4):
            part = slice(g * HD, (g + 1) * HD)
            hq[g], hk[g], hv[g], gcs[g] = q4[:, part], k4[:, part], v4[:, part], gc4[:, part]

        @pl.when(i > 0)
        def _():
            att.first(i - 1, own_att(i - 1))

        gqs, gks, gvs, gmk_all, gmv_all = [], [], [], [], []
        for g in range(4):
            part = slice(g * HD, (g + 1) * HD)
            mk, mv = mk4[:, part], mv4[:, part]
            gct, qt = gc4t[part], q4t[part]
            grect = gct * gate_row
            gauss = sall[g, i, 2:4]
            blocks = []
            grad0 = jnp.zeros((1, N), F32)
            grad1 = jnp.zeros((1, N), F32)
            for r in range(BLOCKS):
                rows, cols = slice(r * BLOCK, (r + 1) * BLOCK), slice(0, (r + 1) * BLOCK)
                q, gc = hq[g, rows], gcs[g, rows]
                k, v = hk[g, cols], hv[g, cols]
                scores = nt(q, k) * SCORE_SCALE + bias[rows, cols]
                probs = jnp.exp(scores - lse[i, rows, g:g + 1])
                gprobs = nt(gc, v)
                inner = jnp.sum(probs * gprobs, axis=-1, keepdims=True)
                gscores = (probs * (gprobs - inner)).astype(BF16)
                dv = nn(gct[:, rows], probs.astype(BF16))
                dk = nn(qt[:, rows], gscores)
                if r:
                    dv = jnp.concatenate([dv[:, :r * BLOCK] + dvs, dv[:, r * BLOCK:]], axis=1)
                    dk = jnp.concatenate([dk[:, :r * BLOCK] + dks, dk[:, r * BLOCK:]], axis=1)
                dvs, dks = dv, dk
                dq = nn(gscores, k)
                mem_scores = nt(q, mk) * SCORE_SCALE
                centre, width, offsets, inv, density = gaussian(mem_scores, gauss)
                grec = (gc.astype(F32) * gate[rows]).astype(BF16)
                gdens = nt(grec, mv) * density
                ratio = offsets * inv
                gcentre = -jnp.sum(gdens * ratio, axis=-1, keepdims=True)
                gvar = 0.5 * jnp.sum(gdens * (ratio * ratio - inv), axis=-1, keepdims=True)
                gcl = gcentre * (centre * (1.0 - centre))
                gwl = gvar * (SIGMA_SCALE * jax.nn.sigmoid(width))
                grad0 = grad0 + column_sum(gcl * mem_scores)
                grad1 = grad1 + column_sum(gwl * mem_scores)
                gms = (gcl * gauss[0:1] + gwl * gauss[1:2]).astype(BF16)
                gmv = nn(grect[:, rows], density.astype(BF16))
                gmk = nn(qt[:, rows], gms)
                gmvs, gmks = (gmv, gmk) if r == 0 else (gmvs + gmv, gmks + gmk)
                blocks.append(((dq + nn(gms, mk)) * SCORE_SCALE).astype(BF16))
            small[i, 8 + 2 * g:9 + 2 * g] = grad0
            small[i, 9 + 2 * g:10 + 2 * g] = grad1
            gqs.append(jnp.concatenate(blocks, axis=0))
            gks.append((dks * SCORE_SCALE).astype(BF16))
            gvs.append(dvs.astype(BF16))
            gmk_all.append((gmks * SCORE_SCALE).astype(BF16))
            gmv_all.append(gmvs.astype(BF16))
            for when, move in hooks:
                if when[1] == g:
                    @pl.when(i == when[0])
                    def _(move=move):
                        move()

        gq4 = jnp.concatenate(gqs, axis=1)
        gk4t, gv4t, gmk4t, gmv4t = (jnp.concatenate(p, axis=0) for p in (gks, gvs, gmk_all, gmv_all))

        @pl.when(i == 2)
        def _():
            swap_att(0).sent()

        def store(kind, value):
            gbuf[slot, :, :, kind] = value.reshape(2, 2, 4, ROWS, D)

        store(0, tn(gq4, n12[...]))
        store(1, nn(gk4t, n12[...]) + nn(gmk4t, coeffs[...]))
        store(2, nn(gv4t, n12[...]) + nn(gmv4t, coeffs[...]))
        store(3, tn(context[i], gbranch[...]))

        @pl.when(i > 0)
        def _():
            pl.semaphore_wait(credita, 1)

        swap_att(i).start()
        small[i, 6:7] = column_sum(gq4.astype(F32))
        gk4, gv4 = gk4t.T, gv4t.T
        small[i, 7:8] = column_sum(gv4.astype(F32))
        acc[...] += nn(gq4, weight(0)) + nn(gk4, weight(1)) + nn(gv4, weight(2))

        @pl.when(i == 0)
        def _():
            load_att(2, 0).start()

        return carry

    lax.fori_loop(0, PARTS, group, 0)
    a[0].third()
    a[1].second()
    att.first(2, own_att(2))
    m[2].sixth()

    def norm_one(i, carry):
        rows = pl.ds(i * CHUNK, CHUNK)
        grad = acc[rows]
        values, inverse = normalize(x[rows].astype(F32))
        gbranch[rows] = (hidden[rows] + norm_back(grad, values, inverse, ln_gain[0:1])).astype(BF16)
        put(0, column_sum(grad * values))
        put(2, column_sum(grad))
        return carry

    lax.fori_loop(0, SEG // CHUNK, norm_one, 0)
    a[0].fourth()
    a[1].third()
    gin_moves = Spread(gbranch, gin_all, 3)
    gin_moves.start()
    gin_moves.send(0)
    gin_moves.send(1)
    mixed_moves.forward(1)
    mixed_moves.forward(2)
    a[0].fifth()

    def small_stage(stage, place, at, count):
        made = []
        for k in range(1, count):
            made.append(links.add(
                lambda: slots.at[stage, place], lambda: slots.at[stage, place],
                lambda k=k: at(lax.rem(place + k, count)),
                lambda k=k: slots.at[stage, lax.rem(place + count - k, count)]))
        for link in made:
            link.start()
        return made

    def small_sum(made, stage, count):
        for link in made:
            link.wait()
        value = slots[stage, 0]
        for k in range(1, count):
            value = value + slots[stage, k]
        return value

    slots[0, me.c] = small[...]
    made = small_stage(0, me.c, lambda p: me.at(c=p), 2)
    a[2].second()
    a[1].fourth()
    a[0].sixth()
    slots[1, me.x] = small_sum(made, 0, 2)
    made = small_stage(1, me.x, lambda p: me.at(x=p), 4)
    a[1].fifth()
    a[2].third()
    gin_moves.send(2)
    gin_moves.send(3)
    mixed_moves.forward(3)
    slots[2, me.z] = small_sum(made, 1, 4)
    made = small_stage(2, me.z, lambda p: me.at(z=p), 4)
    a[1].sixth()
    a[2].fourth()
    slots[3, me.y] = small_sum(made, 2, 4)
    made = small_stage(3, me.y, lambda p: me.at(y=p), 4)
    a[2].fifth()
    a[2].sixth()
    small_total[...] = small_sum(made, 3, 4)
    for i in range(SEG // CHUNK):
        gin_moves.forward(i)
    mixed_moves.finish()
    gin_moves.finish()
    for tail in m + a:
        tail.finish()
    swap_att(1).sent()
    swap_att(2).sent()
    pl.semaphore_wait(creditm, 1)
    pl.semaphore_wait(credita, 1)
    for sums in (mlp, att):
        for part in range(PARTS):
            for half in (0, 1):
                for k in (1, 2, 3):
                    sums.send(part, half, k).sent()
    links.finish()


def tail_y_scratch(kinds, dtype):
    return [
        pltpu.VMEM((3, kinds, 4, ROWS, LANES), F32),
        pltpu.VMEM((3, kinds, ROWS, LANES), F32),
        pltpu.VMEM((kinds, ROWS, LANES), dtype),
    ]


def tail_scratch(parts, kinds, dtype):
    return [
        pltpu.VMEM((6, parts, 2, kinds, ROWS, LANES), F32),
        pltpu.VMEM((2, 2, parts, kinds, ROWS, LANES), F32),
        pltpu.VMEM((3, parts, kinds, ROWS, LANES), F32),
        pltpu.VMEM((parts, kinds, ROWS, LANES), dtype),
    ]


def sums_scratch(kinds):
    return [
        pltpu.VMEM((2, kinds, 4, 4, ROWS, D), F32),
        pltpu.VMEM((PARTS, 6, 2, kinds, 4, ROWS, LANES), BF16),
        pltpu.VMEM((PARTS, 6, 2, kinds, 4, ROWS, LANES), BF16),
        pltpu.VMEM((PARTS, 2, 2, kinds, 4, ROWS, LANES), F32),
    ]


def shards(inputs, memory, doc_ids, key_valid, sticky_bins, ln_gain, ln_shift, w_qkv, b_qv, w_gauss, w_out, b_out,
           w_fc, b_fc, w_proj, b_proj, cotangent):
    vmem, hbm = pl.BlockSpec(memory_space=pltpu.VMEM), pl.BlockSpec(memory_space=pl.ANY)
    S, V = jax.ShapeDtypeStruct, pltpu.VMEM
    count = 3 * (1 + 12 + 8) + 2 + 6
    watt, wmlp, sall, coeffs, hidden, qs, ks, vs, mks, mvs, lse, context = pl.pallas_call(
        attend_kernel,
        out_shape=(
            S((2, 2, PARTS, 4, 4, ROWS, D), BF16), S((2, 2, PARTS, 2, 4, 4, ROWS, D), BF16), S((4, PARTS, 8, 256), F32),
            S((N, D), BF16), S((SEG, D), F32), S((PARTS, SEG, 256), BF16), S((PARTS, SEG, 256), BF16),
            S((PARTS, SEG, 256), BF16), S((PARTS, N, 256), BF16), S((PARTS, N, 256), BF16), S((PARTS, SEG, 128), F32),
            S((PARTS, SEG, 256), BF16)),
        in_specs=[hbm] + [vmem] * 14,
        out_specs=[hbm] * 3 + [vmem] * 9,
        scratch_shapes=[
            V((2, 2, PARTS, 4, 4, ROWS, D), BF16), V((PARTS, 2, 4, 4, ROWS, D), BF16), V((4, 128, D), BF16),
            V((4, PARTS, 8, 256), F32), V((SEG, D), BF16), V((SEG, 1), F32), V((SEG, SEG), F32),
            V((SEG, D), BF16), V((4, SEG, HD), BF16), V((4, SEG, HD), BF16), V((4, SEG, HD), BF16),
            pltpu.SemaphoreType.DMA((count,)), pltpu.SemaphoreType.DMA((count,)), pltpu.SemaphoreType.DMA((4,))],
        compiler_params=pltpu.CompilerParams(collective_id=1, has_side_effects=True, vmem_limit_bytes=VMEM_LIMIT),
        name="gather_attend",
    )(inputs, memory, doc_ids, key_valid, sticky_bins, ln_gain, ln_shift, w_qkv.transpose(0, 2, 1), b_qv, w_gauss.transpose(1, 0, 2), w_out, b_out,
      w_fc, b_fc, w_proj)

    count = 2 * PARTS * 7 + 2 * PARTS * (6 + 3 + 1 + 12) + 2 * 9 + 10
    tatt, tmlp, small_total, mixed_all, gin_all = pl.pallas_call(
        backward_kernel,
        out_shape=(
            S((PARTS, 1, 4, 4, ROWS, D), F32), S((PARTS, 2, 4, 4, ROWS, D), BF16), S((PARTS, 24, 256), F32),
            S((4, SEG, D), BF16), S((4, SEG, D), BF16)),
        in_specs=[hbm] * 5 + [vmem] * 14,
        out_specs=[hbm, hbm, vmem, hbm, hbm],
        scratch_shapes=[
            V((SEG, D), BF16), V((SEG, D), BF16), V((SEG, 1), F32),
            V((2, 2, 2, 4, 4, ROWS, D), BF16), V((2, 2, 2, 4, 4, ROWS, D), F32),
            V((SEG, D), F32), V((SEG, D), F32), V((SEG, D), F32), V((SEG, D), BF16), V((SEG, D), BF16), V((SEG, D), BF16),
            V((SEG, SEG), F32), V((4, SEG, HD), BF16), V((4, SEG, HD), BF16), V((4, SEG, HD), BF16), V((4, SEG, HD), BF16),
            ]
        + sums_scratch(2) + sums_scratch(1)
        + tail_y_scratch(2, BF16) * PARTS + tail_scratch(1, 1, F32) * PARTS
        + [V((PARTS, 24, 256), F32), V((4, 4, PARTS, 24, 256), F32),
           pltpu.SemaphoreType.DMA((count,)), pltpu.SemaphoreType.DMA((count,)),
           pltpu.SemaphoreType.REGULAR, pltpu.SemaphoreType.REGULAR, pltpu.SemaphoreType.DMA((13,))],
        compiler_params=pltpu.CompilerParams(collective_id=2, has_side_effects=True, vmem_limit_bytes=VMEM_LIMIT),
        name="mlp_backward",
    )(inputs, cotangent, hidden, watt, wmlp, coeffs, sall, doc_ids, key_valid, ln_gain, ln_shift, b_proj,
      qs, ks, vs, mks, mvs, lse, context)
    return finish(tatt.reshape(PARTS, 4, HD, D), tmlp.reshape(PARTS, 2, 256, D), small_total, mixed_all, gin_all)


def finish_kernel(tatt, tmlp, small, mixed_in, gin_in, mixed, gin, gain, shift, wqkv, bqv, gauss, wout, bout, wfc, bfc, wproj,
                  bproj):
    at = pl.program_id(0)
    mixed[...] = mixed_in[...]
    gin[...] = gin_in[...].astype(F32)

    @pl.when(at < PARTS)
    def _():
        wfc[...] = tmlp[0, 0].astype(F32).T
        wproj[...] = tmlp[0, 1].astype(F32)

    @pl.when(at == PARTS)
    def _():
        head = lax.axis_index("head")
        for kind in range(3):
            wqkv[kind] = jnp.concatenate([tatt[i, kind] for i in range(PARTS)], axis=0)
        for i in range(PARTS):
            wout[i * HD:(i + 1) * HD] = tatt[i, 3]
        for i in range(PARTS):
            part = slice(i * 256, (i + 1) * 256)
            gain[0:1, part], gain[1:2, part] = small[i, 0:1], small[i, 1:2]
            shift[0:1, part], shift[1:2, part] = small[i, 2:3], small[i, 3:4]
            bout[part], bproj[part] = small[i, 4], small[i, 5]
            value, biases, widths = small[i, 16], small[i, 6:8, 0:HD], small[i, 8:10]
            for g in range(1, 4):
                value = jnp.where(head == g, small[i, 16 + g], value)
                biases = jnp.where(head == g, small[i, 6:8, g * HD:(g + 1) * HD], biases)
                widths = jnp.where(head == g, small[i, 8 + 2 * g:10 + 2 * g], widths)
            bfc[part] = value
            bqv[:, i * HD:(i + 1) * HD] = biases
            gauss[i] = widths


def finish(tatt, tmlp, small, mixed_all, gin_all):
    S = jax.ShapeDtypeStruct
    whole = lambda *shape: pl.BlockSpec(shape, lambda i: (0,) * len(shape))
    part = lambda i: jnp.minimum(i, PARTS - 1)
    segment = pl.BlockSpec((1, SEG, D), lambda i: (i, 0, 0))
    out = pl.pallas_call(
        finish_kernel,
        grid=(4,),
        out_shape=(
            S((4, SEG, D), BF16), S((4, SEG, D), F32), S((2, D), F32), S((2, D), F32), S((3, 192, D), F32), S((2, 192), F32),
            S((3, 2, N), F32), S((192, D), F32), S((D,), F32), S((D, D), F32), S((D,), F32), S((D, D), F32),
            S((D,), F32)),
        in_specs=[whole(PARTS, 4, HD, D), pl.BlockSpec((1, 2, 256, D), lambda i: (part(i), 0, 0, 0)),
                  whole(PARTS, 24, 256), segment, segment],
        out_specs=(
            segment, segment, whole(2, D), whole(2, D), whole(3, 192, D), whole(2, 192), whole(3, 2, N), whole(192, D),
            whole(D), pl.BlockSpec((D, 256), lambda i: (0, part(i))), whole(D),
            pl.BlockSpec((256, D), lambda i: (part(i), 0)), whole(D)),
        compiler_params=pltpu.CompilerParams(vmem_limit_bytes=VMEM_LIMIT),
        name="finish",
    )(tatt, tmlp, small, mixed_all, gin_all)
    out = list(out)
    out[4], out[6] = out[4].transpose(0, 2, 1), out[6].transpose(1, 0, 2)
    return tuple(out)


def solution(mesh):
    return jax.shard_map(
        shards,
        mesh=mesh,
        in_specs=(
            P("dp", None, None),
            P("dp", "head", None),
            P("dp", None),
            P("dp", None),
            P("dp", None),
            P(),
            P(),
            P(None, None, "head"),
            P(None, "head"),
            P(None, "head", None),
            P("head", None),
            P(),
            P(None, "head"),
            P("head"),
            P("head", None),
            P(),
            P("dp", None, None),
        ),
        out_specs=(
            P("dp", None, None),
            P("dp", None, None),
            P(),
            P(),
            P(None, None, "head"),
            P(None, "head"),
            P(None, "head", None),
            P("head", None),
            P(),
            P(None, "head"),
            P("head"),
            P("head", None),
            P(),
        ),
        check_vma=False,
    )
```
